32 devices in a mesh: batch: 8 (over z, y), head: 4 (over x, core).
Axes of the slice: x: 2, y: 2, z: 4, core: 2. Of those that a mesh axis runs over, the one named last changes fastest.
Arguments:
- tokens: bfloat16 [20480, 768], P(('batch', 'head')), may hold values from -6 to 6
- pass_ids: int32 [20480], P(('batch', 'head')), may hold values from 0 to 4
- segment_ids: int32 [16, 1280], P('batch'), may hold values from 0 to 3, never falling along the last dimension, each value on 1 to 640 neighbouring positions
- pass_embed: bfloat16 [5, 768], replicated, may hold values from -3 to 3
- norm1_gain: bfloat16 [768], replicated, may hold values from 0.5 to 1.5
- norm1_shift: bfloat16 [768], replicated, may hold values from -1 to 1
- qkv_weight: bfloat16 [768, 2304], replicated, may hold values from -0.21875 to 0.21875
- qv_bias: bfloat16 [2, 768], replicated, may hold values from -1 to 1
- out_weight: bfloat16 [768, 768], replicated, may hold values from -0.625 to 0.625
- out_bias: bfloat16 [768], replicated, may hold values from -1 to 1
- norm2_gain: bfloat16 [768], replicated, may hold values from 0.5 to 1.5
- norm2_shift: bfloat16 [768], replicated, may hold values from -1 to 1
- up_weight: bfloat16 [768, 3072], replicated, may hold values from -0.21875 to 0.21875
- up_bias: bfloat16 [3072], replicated, may hold values from -1 to 1
- down_weight: bfloat16 [3072, 768], replicated, may hold values from -0.109375 to 0.109375
- down_bias: bfloat16 [768], replicated, may hold values from -1 to 1
- cotangent: bfloat16 [20480, 768], P(('batch', 'head')), may hold values from -6 to 6
Outputs:
- mixed: bfloat16 [20480, 768], P(('batch', 'head'))
- input_grad: float32 [20480, 768], P(('batch', 'head'))
- pass_embed_grad: float32 [5, 768], P(None, ('batch', 'head'))
- norm1_gain_grad: float32 [768], P(('batch', 'head'))
- norm1_shift_grad: float32 [768], P(('batch', 'head'))
- qkv_weight_grad: float32 [768, 2304], P(None, ('batch', 'head'))
- qv_bias_grad: float32 [2, 768], P(None, ('batch', 'head'))
- out_weight_grad: float32 [768, 768], P(None, ('batch', 'head'))
- out_bias_grad: float32 [768], P(('batch', 'head'))
- norm2_gain_grad: float32 [768], P(('batch', 'head'))
- norm2_shift_grad: float32 [768], P(('batch', 'head'))
- up_weight_grad: float32 [768, 3072], P(None, ('batch', 'head'))
- up_bias_grad: float32 [3072], P(('batch', 'head'))
- down_weight_grad: float32 [3072, 768], P(None, ('batch', 'head'))
- down_bias_grad: float32 [768], P(('batch', 'head'))
The draws below stay inside these ranges and needn't reach their ends.
Inputs may be any that keep to these rules, and one draw needn't show every extreme that they name: `segment_ids`: along a sequence the ids never fall; a segment holds at most 640 tokens and one holds exactly that many.
All inputs are finite; a program needn't handle non-finite values.
Results may differ from the reference program's by a relative error of at most 0.0095.
Values may be sent and summed in bfloat16 or wider, within the bound.
No kernel may reach another device: no remote copies, remote signals or barrier semaphores. Data moves between devices by JAX's collectives and lax.ppermute only.
A program may use at most 192 MiB of HBM per device.

```python
import math
import jax
import jax.numpy as jnp
import numpy as np
from jax import lax

D = 768
HEADS = 12
HEAD_DIM = 64
FF = 3072
PASSES = 5
SEQ_LEN = 1280
SEQS = 16
TOKENS = 20480


def set_ends(values, own_key, least, top_value):
    shape = values.shape
    spot = [jax.random.randint(jax.random.fold_in(own_key, axis), (), 0, shape[axis]) for axis in range(len(shape))]
    values = values.at[tuple(spot)].set(least)
    longest = shape.index(max(shape))
    spot[longest] = (spot[longest] + 1) % shape[longest]
    return values.at[tuple(spot)].set(top_value)


def with_spikes(values, rng, source, target, shards_of, factor):
    def block_of(axis_at):
        return (jnp.arange(values.shape[axis_at]) // (values.shape[axis_at] // shards_of)).reshape((-1,) + (1,) * (values.ndim - 1 - axis_at))

    one_side = jax.random.permutation(rng, shards_of)[block_of(target)]
    far = (block_of(target) + shards_of // 2) % shards_of
    return jnp.where((block_of(source) == one_side) | (block_of(source) == far), factor * values, values)


def block_levels(rng, extent, cuts, least, top_value):
    level, own = 1.0, jax.random.fold_in(rng, 6)
    for dim, blocks in cuts:
        steps = jnp.exp(jax.random.uniform(jax.random.fold_in(own, dim), (blocks,), jnp.float32, least / len(cuts), top_value / len(cuts)))
        level = level * jnp.repeat(steps, extent[dim] // blocks).reshape([-1 if axis == dim else 1 for axis in range(len(extent))])
    return level


def length_profile(count, total, most, lean):
    loads = [(1 << 20) // math.isqrt(grade ** lean) + 1 for grade in range(2, count + 1)]
    rest, counts = total - most - (count - 1), [1] * (count - 1)
    while rest > 0:
        free = [i for i in range(count - 1) if counts[i] < most]
        mass, budget = sum([loads[i] for i in free]), rest
        for i in free:
            extra = min(most - counts[i], max(1, budget * loads[i] // mass), rest)
            counts[i] = counts[i] + extra
            rest = rest - extra
    return np.array([most] + counts)


def ragged_sizes(rng, amount, total, bound, skew):
    if amount == 2:
        one = jax.random.randint(rng, (), max(1, total - bound), min(bound, total - 1) + 1)
        return jnp.stack([one, total - one])
    lengths = jnp.asarray(length_profile(amount, total, bound, skew), jnp.int32)
    couples = (amount - 1) // 2
    source_of, sink = lengths[1:1 + 2 * couples:2], lengths[2:2 + 2 * couples:2]
    margin = jnp.minimum(source_of - 1, bound - sink)
    shifted = jax.random.randint(jax.random.fold_in(rng, 1), (couples,), 0, 1 << 20) % (margin + 1)
    lengths = lengths.at[1:1 + 2 * couples:2].set(source_of - shifted).at[2:2 + 2 * couples:2].set(sink + shifted)
    return lengths[jax.random.permutation(jax.random.fold_in(rng, 2), amount)]


def bell_draw(stream_key, extent, deviation, reach, shards=(), kind=jnp.bfloat16):
    values = jax.random.normal(stream_key, extent, jnp.float32) * deviation
    if len(shards) > 0:
        values = block_levels(stream_key, extent, shards, -0.22, 0.18) * values
    return jnp.clip(values, min=-reach, max=reach).astype(kind)


def bell_draw_with(rng, extent, width, bound, split, heavy, kind=jnp.bfloat16):
    entries = width * jax.random.normal(rng, extent, jnp.float32)
    if split:
        entries = entries * block_levels(rng, extent, split, -0.22, 0.18)
    return jnp.clip(with_spikes(entries, jax.random.fold_in(rng, 3), *heavy), -bound, bound).astype(kind)


def setup_inputs(seed: int = 0) -> dict:
    key_list = jax.random.split(jax.random.key(seed), 18)
    tokens = bell_draw(key_list[0], (TOKENS, D), 1.0, 6.0, ((0, 32),))
    pass_ids = set_ends(jax.random.randint(key_list[1], (TOKENS,), 0, PASSES), jax.random.fold_in(key_list[1], 1), 0, PASSES - 1).astype(jnp.int32)
    segment_ids = jax.vmap(lambda own: jnp.searchsorted(jnp.cumsum(ragged_sizes(own, 4, SEQ_LEN, SEQ_LEN // 2, 1)), jnp.arange(SEQ_LEN), side="right"))(jax.random.split(key_list[2], SEQS)).reshape((SEQS, SEQ_LEN)).astype(jnp.int32)
    pass_embed = bell_draw(key_list[3], (PASSES, D), 0.5, 3.0)
    norm1_gain = jnp.clip(1.0 + 0.1 * jax.random.normal(key_list[4], (D,), jnp.float32), 0.5, 1.5).astype(jnp.bfloat16)
    norm1_shift = bell_draw(key_list[5], (D,), 0.2, 1.0)
    qkv_weight = bell_draw(key_list[6], (D, 3 * D), D ** -0.5, 0.21875)
    qv_bias = bell_draw(key_list[7], (2, D), 0.2, 1.0)
    out_weight = bell_draw(key_list[8], (D, D), (D // 8) ** -0.5, 0.625)
    out_bias = bell_draw(key_list[9], (D,), 0.2, 1.0)
    norm2_gain = jnp.clip(1.0 + 0.1 * jax.random.normal(key_list[10], (D,), jnp.float32), 0.5, 1.5).astype(jnp.bfloat16)
    norm2_shift = bell_draw(key_list[11], (D,), 0.2, 1.0)
    up_weight = bell_draw(key_list[12], (D, FF), D ** -0.5, 0.21875)
    up_bias = bell_draw(key_list[13], (FF,), 0.2, 1.0)
    down_weight = bell_draw(key_list[14], (FF, D), FF ** -0.5, 0.109375)
    down_bias = bell_draw(key_list[15], (D,), 0.2, 1.0)
    cotangent = bell_draw_with(key_list[16], (TOKENS, D), 1.0, 6.0, ((0, 32),), (0, 1, 32, 2.75))
    return {"tokens": tokens, "pass_ids": pass_ids, "segment_ids": segment_ids, "pass_embed": pass_embed, "norm1_gain": norm1_gain, "norm1_shift": norm1_shift, "qkv_weight": qkv_weight, "qv_bias": qv_bias, "out_weight": out_weight, "out_bias": out_bias, "norm2_gain": norm2_gain, "norm2_shift": norm2_shift, "up_weight": up_weight, "up_bias": up_bias, "down_weight": down_weight, "down_bias": down_bias, "cotangent": cotangent}


@jax.custom_vjp
def low(v):
    return lax.optimization_barrier(v.astype(jnp.bfloat16)).astype(jnp.float32)

@jax.custom_vjp
def low_back(v):
    return v

def low_keep(v):
    return (low(v), None)

def low_pass(kept, grad):
    return (grad,)

def back_keep(v):
    return (v, None)

def back_low(kept, grad):
    return (low(grad),)
low.defvjp(low_keep, low_pass)
low_back.defvjp(back_keep, back_low)

def layer_norm(values, gain, shift):
    center = values - lax.optimization_barrier(jnp.mean(values, -1, keepdims=True))
    spread = lax.optimization_barrier(jnp.mean(center * center, -1, keepdims=True))
    return center * lax.rsqrt(spread + 1e-05) * gain + shift

def product(left, right):
    return jnp.dot(left, right, precision=lax.Precision.HIGHEST, preferred_element_type=jnp.float32)

def attend_sequence(inputs):
    q_rows, k_rows, v_rows, seg_row = inputs
    scores = jnp.einsum('qhd,khd->hqk', q_rows, k_rows, precision=lax.Precision.HIGHEST) * 0.125
    places = jnp.arange(SEQ_LEN)
    allowed = (places[:, None] >= places[None, :]) & (seg_row[:, None] == seg_row[None, :])
    scores = low_back(jnp.where(allowed[None], scores, -1e+30))
    probability = low(jax.nn.softmax(scores, axis=-1))
    attended = jnp.einsum('hqk,khd->qhd', probability, v_rows, precision=lax.Precision.HIGHEST)
    return attended.reshape(SEQ_LEN, D)

def reference(tokens, pass_ids, segment_ids, pass_embed, norm1_gain, norm1_shift, qkv_weight, qv_bias, out_weight, out_bias, norm2_gain, norm2_shift, up_weight, up_bias, down_weight, down_bias, cotangent):
    one_hot = (pass_ids[:, None] == jnp.arange(PASSES)[None, :]).astype(jnp.float32)

    def forward(inputs, table, gain1, shift1, qkv_w, qv_b, out_w, out_b, gain2, shift2, up_w, up_b, down_w, down_b):
        hidden = inputs + product(one_hot, table)
        normed = low(layer_norm(hidden, gain1, shift1))
        bias_full = jnp.concatenate([qv_b[0], jnp.zeros((D,), jnp.float32), qv_b[1]])
        joined = low_back(low(product(normed, qkv_w) + bias_full))
        shaped = joined.reshape(SEQS, SEQ_LEN, 3, HEADS, HEAD_DIM)
        attended = lax.map(jax.checkpoint(attend_sequence), (shaped[:, :, 0], shaped[:, :, 1], shaped[:, :, 2], segment_ids))
        attended = low_back(low(attended.reshape(TOKENS, D)))
        after_attn = hidden + low_back(product(attended, out_w) + out_b)
        normed2 = low(layer_norm(after_attn, gain2, shift2))
        pre_act = low_back(product(normed2, up_w) + up_b)
        activated = low(jax.nn.gelu(pre_act, approximate=True))
        return after_attn + product(activated, down_w) + down_b
    floats = tuple((item.astype(jnp.float32) for item in (tokens, pass_embed, norm1_gain, norm1_shift, qkv_weight, qv_bias, out_weight, out_bias, norm2_gain, norm2_shift, up_weight, up_bias, down_weight, down_bias)))
    result, pullback = jax.vjp(forward, *floats)
    grads = pullback(cotangent.astype(jnp.float32))
    return (result.astype(jnp.bfloat16), grads[0], grads[1], grads[2], grads[3], grads[4], grads[5], grads[6], grads[7], grads[8], grads[9], grads[10], grads[11], grads[12], grads[13])
```

```python
import jax
import jax.numpy as jnp
from jax import lax
from jax.experimental import pallas as pl
from jax.experimental.pallas import tpu as pltpu
from jax.sharding import PartitionSpec as P

HEAD_DIM = 64
SEQ_LEN = 1280
PAIR = 2 * HEAD_DIM
BQ = 256
BK = 128
BLOCKS = 8
NEG = -1e30
F32 = jnp.float32
BF16 = jnp.bfloat16
VMEM_LIMIT = 56 * 1024 * 1024


def dot(left, right):
    return lax.dot_general(left, right, (((1,), (0,)), ((), ())), preferred_element_type=F32)


def dot_nt(left, right):
    return lax.dot_general(left, right, (((1,), (1,)), ((), ())), preferred_element_type=F32)


def center_and_scale(values):
    center = values - jnp.mean(values, -1, keepdims=True)
    spread = jnp.mean(center * center, -1, keepdims=True)
    scale = lax.rsqrt(spread + 1e-05)
    return center * scale, scale


def embed_tokens(tok_ref, ids_ref, emb_ref):
    ids = ids_ref[...]
    hidden = tok_ref[...].astype(F32)
    for row in range(emb_ref.shape[0]):
        hidden = hidden + jnp.where(ids == row, emb_ref[row : row + 1, :].astype(F32), 0.0)
    return hidden


def whole(shape):
    return pl.BlockSpec(shape, lambda *_: (0,) * len(shape))


def params():
    return pltpu.CompilerParams(vmem_limit_bytes=VMEM_LIMIT)


def cost(flops, moved):
    return pl.CostEstimate(flops=int(flops), transcendentals=0, bytes_accessed=int(moved))


def qkv_send_kernel(pos, tok, ids, emb, gain, shift, weight, bias, normed_out, out):
    @pl.when(pl.program_id(0) == 0)
    def _():
        scaled, _ = center_and_scale(embed_tokens(tok, ids, emb))
        normed_out[...] = (scaled * gain[...] + shift[...]).astype(BF16)

    out[0] = (dot(normed_out[...], weight[...]) + bias[...]).astype(BF16)


def qkv_keep_kernel(pos, normed, weight, bias, out):
    out[0] = (dot(normed[...], weight[...]) + bias[...]).astype(BF16)


def qkv_send(pos, tok, ids, emb, gain, shift, weight, bias):
    rows, width = tok.shape
    half = width // 2
    return pl.pallas_call(
        qkv_send_kernel,
        grid_spec=pltpu.PrefetchScalarGridSpec(
            num_scalar_prefetch=1,
            grid=(3,),
            in_specs=[
                whole(tok.shape),
                whole(ids.shape),
                whole(emb.shape),
                whole(gain.shape),
                whole(shift.shape),
                pl.BlockSpec((width, half), lambda t, s: (0, 2 * t + 1 - s[0])),
                pl.BlockSpec((1, half), lambda t, s: (0, 2 * t + 1 - s[0])),
            ],
            out_specs=[
                whole(tok.shape),
                pl.BlockSpec((1, rows, half), lambda t, s: (t, 0, 0)),
            ],
        ),
        out_shape=[
            jax.ShapeDtypeStruct(tok.shape, BF16),
            jax.ShapeDtypeStruct((3, rows, half), BF16),
        ],
        compiler_params=params(),
        cost_estimate=cost(3 * rows * width * width, 6e6),
        name="qkv_send",
    )(pos, tok, ids, emb, gain, shift, weight, bias)


def qkv_keep(pos, normed, weight, bias):
    rows, width = normed.shape
    half = width // 2
    return pl.pallas_call(
        qkv_keep_kernel,
        grid_spec=pltpu.PrefetchScalarGridSpec(
            num_scalar_prefetch=1,
            grid=(3,),
            in_specs=[
                whole(normed.shape),
                pl.BlockSpec((width, half), lambda t, s: (0, 2 * t + s[0])),
                pl.BlockSpec((1, half), lambda t, s: (0, 2 * t + s[0])),
            ],
            out_specs=pl.BlockSpec((1, rows, half), lambda t, s: (t, 0, 0)),
        ),
        out_shape=jax.ShapeDtypeStruct((3, rows, half), BF16),
        compiler_params=params(),
        cost_estimate=cost(3 * rows * width * width, 4e6),
        name="qkv_keep",
    )(pos, normed, weight, bias)


def lane_masks():
    lane = lax.broadcasted_iota(jnp.int32, (1, PAIR), 1)
    first = (lane < HEAD_DIM).astype(F32).astype(BF16)
    return first, (1 - first).astype(BF16)


def row_split(values):
    row = lax.broadcasted_iota(jnp.int32, values.shape, 0)
    keep = row < HEAD_DIM
    wide = values.astype(F32)
    return jnp.concatenate(
        [jnp.where(keep, wide, 0.0).astype(BF16), jnp.where(keep, 0.0, wide).astype(BF16)], axis=1
    )


def gather_rows(mine, other, target, sems, core, rows):
    own = pl.ds(pl.multiple_of(core * rows, 128), rows)
    far = pl.ds(pl.multiple_of((1 - core) * rows, 128), rows)
    if len(mine.shape) == 3:
        return (
            pltpu.make_async_copy(mine, target.at[:, own, :], sems.at[0]),
            pltpu.make_async_copy(other, target.at[:, far, :], sems.at[1]),
        )
    return (
        pltpu.make_async_copy(mine, target.at[own, :], sems.at[0]),
        pltpu.make_async_copy(other, target.at[far, :], sems.at[1]),
    )


def valid_keys(start, q0, kb):
    key_at = lax.broadcasted_iota(jnp.int32, (BK, BQ), 0) + kb * BK
    query_at = lax.broadcasted_iota(jnp.int32, (BK, BQ), 1) + q0
    inside = (key_at >= start) & (key_at <= query_at)
    return jnp.concatenate([inside, inside], axis=1)


def attend_kernel(pos, start_ref, keep, recv, own_out, far_out, lse_out, qkv, qq, vm, sc, acc, joined, sems):
    core = pos[0]
    rows = own_out.shape[0]
    pairs = own_out.shape[1] // PAIR
    copies = gather_rows(keep, recv, qkv, sems, core, rows)
    for item in copies:
        item.start()
    for item in copies:
        item.wait()
    first, second = lane_masks()

    def prepare(kb, _):
        at = pl.ds(pl.multiple_of(kb * BK, BK), BK)
        for p in range(pairs):
            vm[kb, p] = row_split(qkv[2, at, p * PAIR : (p + 1) * PAIR].T)
        return 0

    lax.fori_loop(0, SEQ_LEN // BK, prepare, 0)

    def one_block(qi, _):
        q0 = pl.multiple_of(qi * BQ, BQ)
        at = pl.ds(q0, BQ)
        start = start_ref[:, at]
        low = pos[8 + qi]
        high = (qi + 1) * (BQ // BK)
        for p in range(pairs):
            q = qkv[0, at, p * PAIR : (p + 1) * PAIR] * jnp.asarray(0.125, BF16)
            qq[p, :BQ] = q * first
            qq[p, BQ:] = q * second
            acc[p] = jnp.zeros((PAIR, BQ), F32)

        def scores(kb, tops):
            inside = valid_keys(start, q0, kb)
            rows_at = pl.ds(pl.multiple_of(kb * BK, BK), BK)
            grown = []
            for p in range(pairs):
                s = dot_nt(qkv[1, rows_at, p * PAIR : (p + 1) * PAIR], qq[p])
                s = jnp.where(inside, s, NEG)
                sc[kb - low, p] = s
                grown.append(jnp.maximum(tops[p], jnp.max(s, axis=0, keepdims=True)))
            return tuple(grown)

        tops = lax.fori_loop(
            low, high, scores, tuple(jnp.full((1, 2 * BQ), NEG, F32) for _ in range(pairs))
        )

        def weigh(kb, sums):
            grown = []
            for p in range(pairs):
                raw = jnp.exp(sc[kb - low, p] - tops[p])
                grown.append(sums[p] + jnp.sum(raw, axis=0, keepdims=True))
                raw = raw.astype(BF16)
                acc[p] += dot(vm[kb, p], jnp.concatenate([raw[:, :BQ], raw[:, BQ:]], axis=0))
            return tuple(grown)

        sums = lax.fori_loop(
            low, high, weigh, tuple(jnp.zeros((1, 2 * BQ), F32) for _ in range(pairs))
        )
        for p in range(pairs):
            inv = 1.0 / sums[p]
            out = jnp.concatenate(
                [acc[p, :HEAD_DIM] * inv[:, :BQ], acc[p, HEAD_DIM:] * inv[:, BQ:]], axis=0
            )
            joined[at, p * PAIR : (p + 1) * PAIR] = out.T.astype(BF16)
            lse_out[qi, p] = tops[p] + jnp.log(sums[p])
        return 0

    lax.fori_loop(0, SEQ_LEN // BQ, one_block, 0)
    own_out[...] = joined[pl.ds(pl.multiple_of(core * rows, 128), rows), :]
    far_out[...] = joined[pl.ds(pl.multiple_of((1 - core) * rows, 128), rows), :]


def attend(pos, start, keep, recv):
    _, rows, half = keep.shape
    pairs = half // PAIR
    window = SEQ_LEN // BK
    return pl.pallas_call(
        attend_kernel,
        grid_spec=pltpu.PrefetchScalarGridSpec(
            num_scalar_prefetch=1,
            grid=(1,),
            in_specs=[
                whole(start.shape),
                pl.BlockSpec(memory_space=pl.ANY),
                pl.BlockSpec(memory_space=pl.ANY),
            ],
            out_specs=[
                whole((rows, half)),
                whole((rows, half)),
                whole((SEQ_LEN // BQ, pairs, 1, 2 * BQ)),
            ],
            scratch_shapes=[
                pltpu.VMEM((3, SEQ_LEN, half), BF16),
                pltpu.VMEM((pairs, 2 * BQ, PAIR), BF16),
                pltpu.VMEM((SEQ_LEN // BK, pairs, PAIR, 2 * BK), BF16),
                pltpu.VMEM((window, pairs, BK, 2 * BQ), F32),
                pltpu.VMEM((pairs, PAIR, BQ), F32),
                pltpu.VMEM((SEQ_LEN, half), BF16),
                pltpu.SemaphoreType.DMA((2,)),
            ],
        ),
        out_shape=[
            jax.ShapeDtypeStruct((rows, half), BF16),
            jax.ShapeDtypeStruct((rows, half), BF16),
            jax.ShapeDtypeStruct((SEQ_LEN // BQ, pairs, 1, 2 * BQ), F32),
        ],
        compiler_params=params(),
        cost_estimate=cost(8e9, 5e6),
        name="attend",
    )(pos, start, keep, recv)


def attend_back_kernel(
    pos, start_ref, lse_ref, keep, recv, own, far, grad_own, grad_far,
    keep_out, send_out,
    qkv, att, dout, qq, dd, km, delta, dq_t, dq, dk, dv, sems,
):
    core = pos[0]
    rows, half = own.shape
    pairs = half // PAIR
    copies = (
        gather_rows(keep, recv, qkv, sems.at[0], core, rows)
        + gather_rows(own, far, att, sems.at[1], core, rows)
        + gather_rows(grad_own, grad_far, dout, sems.at[2], core, rows)
    )
    for item in copies:
        item.start()
    for item in copies:
        item.wait()
    first, second = lane_masks()
    dk[...] = jnp.zeros_like(dk)
    dv[...] = jnp.zeros_like(dv)

    def prepare(kb, _):
        at = pl.ds(pl.multiple_of(kb * BK, BK), BK)
        for p in range(pairs):
            km[kb, p] = row_split(qkv[1, at, p * PAIR : (p + 1) * PAIR].T)
        return 0

    lax.fori_loop(0, SEQ_LEN // BK, prepare, 0)

    def one_block(qi, _):
        q0 = pl.multiple_of(qi * BQ, BQ)
        at = pl.ds(q0, BQ)
        start = start_ref[:, at]
        low = pos[8 + qi]
        high = (qi + 1) * (BQ // BK)
        for p in range(pairs):
            lanes = slice(p * PAIR, (p + 1) * PAIR)
            q = qkv[0, at, lanes] * jnp.asarray(0.125, BF16)
            qq[p, :BQ] = q * first
            qq[p, BQ:] = q * second
            g = dout[at, lanes]
            dd[p, :BQ] = g * first
            dd[p, BQ:] = g * second
            both = (g.astype(F32) * att[at, lanes].astype(F32)).T
            delta[p] = jnp.concatenate(
                [
                    jnp.sum(both[:HEAD_DIM], axis=0, keepdims=True),
                    jnp.sum(both[HEAD_DIM:], axis=0, keepdims=True),
                ],
                axis=1,
            )
            dq_t[p] = jnp.zeros((PAIR, BQ), F32)

        def step(kb, _):
            inside = valid_keys(start, q0, kb)
            rows_at = pl.ds(pl.multiple_of(kb * BK, BK), BK)
            for p in range(pairs):
                lanes = slice(p * PAIR, (p + 1) * PAIR)
                s = dot_nt(qkv[1, rows_at, lanes], qq[p])
                prob = jnp.where(inside, jnp.exp(s - lse_ref[qi, p]), 0.0)
                grad_prob = dot_nt(qkv[2, rows_at, lanes], dd[p])
                grad_s = (prob * (grad_prob - delta[p])).astype(BF16)
                dv[rows_at, lanes] += dot(prob.astype(BF16), dd[p])
                dk[rows_at, lanes] += dot(grad_s, qq[p])
                dq_t[p] += dot(km[kb, p], jnp.concatenate([grad_s[:, :BQ], grad_s[:, BQ:]], axis=0))
            return 0

        lax.fori_loop(low, high, step, 0)
        for p in range(pairs):
            dq[at, p * PAIR : (p + 1) * PAIR] = (dq_t[p] * 0.125).T.astype(BF16)
        return 0

    lax.fori_loop(0, SEQ_LEN // BQ, one_block, 0)
    here = pl.ds(pl.multiple_of(core * rows, 128), rows)
    there = pl.ds(pl.multiple_of((1 - core) * rows, 128), rows)
    for target, at in ((keep_out, here), (send_out, there)):
        target[0] = dq[at, :]
        target[1] = dk[at, :].astype(BF16)
        target[2] = dv[at, :].astype(BF16)


def attend_back(pos, start, lse, keep, recv, own, far, grad_own, grad_far):
    _, rows, half = keep.shape
    pairs = half // PAIR
    hbm = pl.BlockSpec(memory_space=pl.ANY)
    return pl.pallas_call(
        attend_back_kernel,
        grid_spec=pltpu.PrefetchScalarGridSpec(
            num_scalar_prefetch=1,
            grid=(1,),
            in_specs=[whole(start.shape), whole(lse.shape), hbm, hbm, hbm, hbm, hbm, hbm],
            out_specs=[whole(keep.shape), whole(keep.shape)],
            scratch_shapes=[
                pltpu.VMEM((3, SEQ_LEN, half), BF16),
                pltpu.VMEM((SEQ_LEN, half), BF16),
                pltpu.VMEM((SEQ_LEN, half), BF16),
                pltpu.VMEM((pairs, 2 * BQ, PAIR), BF16),
                pltpu.VMEM((pairs, 2 * BQ, PAIR), BF16),
                pltpu.VMEM((SEQ_LEN // BK, pairs, PAIR, 2 * BK), BF16),
                pltpu.VMEM((pairs, 1, 2 * BQ), F32),
                pltpu.VMEM((pairs, PAIR, BQ), F32),
                pltpu.VMEM((SEQ_LEN, half), BF16),
                pltpu.VMEM((SEQ_LEN, half), F32),
                pltpu.VMEM((SEQ_LEN, half), F32),
                pltpu.SemaphoreType.DMA((3, 2)),
            ],
        ),
        out_shape=[jax.ShapeDtypeStruct(keep.shape, BF16)] * 2,
        compiler_params=params(),
        cost_estimate=cost(20e9, 8e6),
        name="attend_back",
    )(pos, start, lse, keep, recv, own, far, grad_own, grad_far)


def out_proj_kernel(pos, tok, ids, emb, own, far, weight, bias, gain, shift, after_out, normed_out):
    core = pos[0]
    half = own.shape[1]
    here = pl.ds(pl.multiple_of(core * half, 128), half)
    there = pl.ds(pl.multiple_of((1 - core) * half, 128), half)
    after = (
        embed_tokens(tok, ids, emb)
        + (dot(own[...], weight[here, :]) + dot(far[...], weight[there, :]))
        + bias[...]
    )
    after_out[...] = after
    scaled, _ = center_and_scale(after)
    normed_out[...] = (scaled * gain[...] + shift[...]).astype(BF16)


def simple_call(kernel, outs, flops, name, scratch=()):
    def call(pos, *operands):
        return pl.pallas_call(
            kernel,
            grid_spec=pltpu.PrefetchScalarGridSpec(
                num_scalar_prefetch=1,
                grid=(1,),
                in_specs=[whole(item.shape) for item in operands],
                out_specs=[whole(item.shape) for item in outs],
                scratch_shapes=list(scratch),
            ),
            out_shape=outs,
            compiler_params=params(),
            cost_estimate=cost(flops, sum(o.size * o.dtype.itemsize for o in list(operands) + outs)),
            name=name,
        )(pos, *operands)

    return call


def ff_first_kernel(
    pos, normed, cot, perm, up, up_bias, down, act_out, grad_out, keep_out, send_out, bias_grad, cot_t
):
    @pl.when(pl.program_id(0) == 0)
    def _():
        cot_t[...] = dot_nt(perm[...], cot[...]).astype(BF16)

    u = dot(normed[...], up[...]) + up_bias[...]
    grad_act = dot_nt(cot[...], down[...])
    square = u * u
    t = jnp.tanh(0.7978845608028654 * u * (1.0 + 0.044715 * square))
    half = 0.5 * (1.0 + t)
    act = (u * half).astype(BF16)
    act_out[...] = act
    slope = half + 0.5 * u * (1.0 - t * t) * (0.7978845608028654 * (1.0 + 0.134145 * square))
    grad = (grad_act * slope).astype(BF16)
    grad_out[...] = grad
    bias_grad[...] = jnp.sum(grad.astype(F32), axis=0, keepdims=True)
    down_t = dot(cot_t[...], act).astype(BF16)
    part = keep_out.shape[0]
    keep_out[...] = down_t[:part]
    send_out[...] = down_t[part:]


def ff_first(pos, normed, cot, perm, up, up_bias, down):
    rows, width = normed.shape
    hidden = up.shape[1]
    block = hidden // BLOCKS
    half = width // 2
    cols = pl.BlockSpec((rows, block), lambda i, s: (0, i))
    grads = pl.BlockSpec((half, block), lambda i, s: (0, i))
    return pl.pallas_call(
        ff_first_kernel,
        grid_spec=pltpu.PrefetchScalarGridSpec(
            num_scalar_prefetch=1,
            grid=(BLOCKS,),
            in_specs=[
                whole(normed.shape),
                whole(cot.shape),
                whole(perm.shape),
                pl.BlockSpec((width, block), lambda i, s: (0, i)),
                pl.BlockSpec((1, block), lambda i, s: (0, i)),
                pl.BlockSpec((block, width), lambda i, s: (i, 0)),
            ],
            out_specs=[cols, cols, grads, grads, pl.BlockSpec((1, block), lambda i, s: (0, i))],
            scratch_shapes=[pltpu.VMEM((width, rows), BF16)],
        ),
        out_shape=[
            jax.ShapeDtypeStruct((rows, hidden), BF16),
            jax.ShapeDtypeStruct((rows, hidden), BF16),
            jax.ShapeDtypeStruct((half, hidden), BF16),
            jax.ShapeDtypeStruct((half, hidden), BF16),
            jax.ShapeDtypeStruct((1, hidden), F32),
        ],
        compiler_params=params(),
        cost_estimate=cost(6 * rows * width * hidden, 24e6),
        name="ff_first",
    )(pos, normed, cot, perm, up, up_bias, down)


def place_rows(pos, rows_f32, keep_out, send_out):
    core, x_bit = pos[1], pos[2]
    per = keep_out.shape[2]
    for rel in range(2):
        x = rel ^ x_bit
        keep_out[rel, 0] = rows_f32[pl.ds(pl.multiple_of((2 * x + core) * per, 8), per), :].astype(BF16)
        send_out[rel, 0] = rows_f32[pl.ds(pl.multiple_of((2 * x + 1 - core) * per, 8), per), :].astype(BF16)


def ff_second_kernel(pos, grad, normed, up, total, keep_out, send_out, rows_f32):
    part = dot_nt(grad[...], up[...])

    @pl.when(pl.program_id(0) == 0)
    def _():
        total[...] = part

    @pl.when(pl.program_id(0) > 0)
    def _():
        total[...] += part

    rows_f32[...] = dot(grad[...].T, normed[...])
    place_rows(pos, rows_f32, keep_out, send_out)


def ff_second(pos, grad, normed, up):
    rows, width = normed.shape
    hidden = up.shape[1]
    block = hidden // BLOCKS
    shard = pl.BlockSpec((2, 1, block // 4, width), lambda i, s: (0, i ^ s[3], 0, 0))
    return pl.pallas_call(
        ff_second_kernel,
        grid_spec=pltpu.PrefetchScalarGridSpec(
            num_scalar_prefetch=1,
            grid=(BLOCKS,),
            in_specs=[
                pl.BlockSpec((rows, block), lambda i, s: (0, i)),
                whole(normed.shape),
                pl.BlockSpec((width, block), lambda i, s: (0, i)),
            ],
            out_specs=[whole((rows, width)), shard, shard],
            scratch_shapes=[pltpu.VMEM((block, width), F32)],
        ),
        out_shape=[
            jax.ShapeDtypeStruct((rows, width), F32),
            jax.ShapeDtypeStruct((2, BLOCKS, block // 4, width), BF16),
            jax.ShapeDtypeStruct((2, BLOCKS, block // 4, width), BF16),
        ],
        compiler_params=params(),
        cost_estimate=cost(4 * rows * width * hidden, 16e6),
        name="ff_second",
    )(pos, grad, normed, up)


def mixed_kernel(pos, act, down, after, bias, out, total):
    part = dot(act[...], down[...])
    step = pl.program_id(0)

    @pl.when(step == 0)
    def _():
        total[...] = part + (after[...] + bias[...])

    @pl.when(step > 0)
    def _():
        total[...] += part

    @pl.when(step == pl.num_programs(0) - 1)
    def _():
        out[...] = total[...].astype(BF16)


def mixed_call(pos, act, down, after, bias):
    rows, width = after.shape
    hidden = down.shape[0]
    steps = 4
    block = hidden // steps
    return pl.pallas_call(
        mixed_kernel,
        grid_spec=pltpu.PrefetchScalarGridSpec(
            num_scalar_prefetch=1,
            grid=(steps,),
            in_specs=[
                pl.BlockSpec((rows, block), lambda i, s: (0, i)),
                pl.BlockSpec((block, width), lambda i, s: (i, 0)),
                whole(after.shape),
                whole(bias.shape),
            ],
            out_specs=whole((rows, width)),
            scratch_shapes=[pltpu.VMEM((rows, width), F32)],
        ),
        out_shape=jax.ShapeDtypeStruct((rows, width), BF16),
        compiler_params=params(),
        cost_estimate=cost(2 * rows * width * hidden, 12e6),
        name="mixed",
    )(pos, act, down, after, bias)


def out_back_kernel(pos, grad_normed, after, cot, gain, weight, grad_after, branch_out, own_out, far_out, sums):
    core = pos[0]
    half = own_out.shape[1]
    scaled, scale = center_and_scale(after[...])
    grad = grad_normed[...]
    inner = grad * gain[...]
    shift = jnp.mean(inner, -1, keepdims=True)
    slope = jnp.mean(inner * scaled, -1, keepdims=True)
    cot_f32 = cot[...].astype(F32)
    total = cot_f32 + scale * (inner - shift - scaled * slope)
    grad_after[...] = total
    branch = total.astype(BF16)
    branch_out[...] = branch
    far_out[...] = dot_nt(
        branch, weight[pl.ds(pl.multiple_of((1 - core) * half, 128), half), :]
    ).astype(BF16)
    own_out[...] = dot_nt(branch, weight[pl.ds(pl.multiple_of(core * half, 128), half), :]).astype(BF16)
    sums[0:1] = jnp.sum(grad * scaled, axis=0, keepdims=True)
    sums[1:2] = jnp.sum(grad, axis=0, keepdims=True)
    sums[2:3] = jnp.sum(branch.astype(F32), axis=0, keepdims=True)
    sums[3:4] = jnp.sum(cot_f32, axis=0, keepdims=True)


def out_weight_kernel(pos, branch, perm, own, far, keep_out, send_out):
    core = pos[0]
    half = own.shape[1]
    turned = dot_nt(perm[...], branch[...]).astype(BF16)
    for part, at in ((own, core), (far, 1 - core)):
        got = dot(turned, part[...]).astype(BF16)
        lanes = pl.ds(pl.multiple_of(at * half, 128), half)
        keep_out[:, lanes] = got[:half]
        send_out[:, lanes] = got[half:]


def qkv_weight_kernel(pos, own, far, normed, keep_out, send_out, sums, turned, rows_f32):
    core = pos[0]
    half = own.shape[2]
    block = rows_f32.shape[0]

    @pl.when(pl.program_id(0) == 0)
    def _():
        for part, at in ((own, core), (far, 1 - core)):
            lanes = pl.ds(pl.multiple_of(at * half, 128), half)
            for t in range(3):
                turned[pl.ds(pl.multiple_of(t * 2 * half + at * half, 128), half), :] = part[t].T
                sums[t : t + 1, lanes] = jnp.sum(part[t].astype(F32), axis=0, keepdims=True)

    at = pl.ds(pl.multiple_of(pl.program_id(0) * block, 32), block)
    rows_f32[...] = dot(turned[at, :], normed[...])
    place_rows(pos, rows_f32, keep_out, send_out)


def qkv_weight_call(pos, own, far, normed):
    rows, width = normed.shape
    block = 3 * width // BLOCKS
    shard = pl.BlockSpec((2, 1, block // 4, width), lambda i, s: (0, i ^ s[3], 0, 0))
    return pl.pallas_call(
        qkv_weight_kernel,
        grid_spec=pltpu.PrefetchScalarGridSpec(
            num_scalar_prefetch=1,
            grid=(BLOCKS,),
            in_specs=[whole(own.shape), whole(far.shape), whole(normed.shape)],
            out_specs=[shard, shard, whole((3, width))],
            scratch_shapes=[pltpu.VMEM((3 * width, rows), BF16), pltpu.VMEM((block, width), F32)],
        ),
        out_shape=[
            jax.ShapeDtypeStruct((2, BLOCKS, block // 4, width), BF16),
            jax.ShapeDtypeStruct((2, BLOCKS, block // 4, width), BF16),
            jax.ShapeDtypeStruct((3, width), F32),
        ],
        compiler_params=params(),
        cost_estimate=cost(6 * rows * width * width, 8e6),
        name="qkv_weight",
    )(pos, own, far, normed)


def input_back_kernel(pos, own, far, weight, tok, ids, emb, gain, grad_after, out, sums):
    core = pos[0]
    half = own.shape[2]
    grad = None
    for t in range(3):
        for part, at in ((own, core), (far, 1 - core)):
            lanes = pl.ds(pl.multiple_of(t * 2 * half + at * half, 128), half)
            got = dot_nt(part[t], weight[:, lanes])
            grad = got if grad is None else grad + got
    scaled, scale = center_and_scale(embed_tokens(tok, ids, emb))
    inner = grad * gain[...]
    shift = jnp.mean(inner, -1, keepdims=True)
    slope = jnp.mean(inner * scaled, -1, keepdims=True)
    total = grad_after[...] + scale * (inner - shift - scaled * slope)
    out[...] = total
    passes = emb.shape[0]
    for row in range(passes):
        sums[row : row + 1] = jnp.sum(jnp.where(ids[...] == row, total, 0.0), axis=0, keepdims=True)
    sums[passes : passes + 1] = jnp.sum(grad * scaled, axis=0, keepdims=True)
    sums[passes + 1 : passes + 2] = jnp.sum(grad, axis=0, keepdims=True)


def add(left, right):
    return (left.astype(F32) + right.astype(F32)).astype(BF16)


def swap_head(values, bit):
    size = lax.axis_size("head")
    return lax.ppermute(values, "head", [(i, i ^ bit) for i in range(size)])


def swap_batch(values, bit):
    size = lax.axis_size("batch")
    return lax.ppermute(values, "batch", [(i, i ^ bit) for i in range(size)])


def over_x(values):
    return add(values[0], swap_head(values[1], 2))


def over_y(values):
    shape = values.shape
    split = values.reshape(shape[:-3] + (shape[-3] // 2, 2) + shape[-2:])
    return add(split[..., 0, :, :], swap_batch(split[..., 1, :, :], 1))


def over_z(values):
    got = [swap_batch(values[k], 2 * k) for k in range(1, values.shape[0])]
    total = values[0].astype(F32)
    for item in got:
        total = total + item.astype(F32)
    return total


def scatter_sum(keep, send, order):
    both = add(keep, swap_head(send, 1))
    if order == "xy":
        return over_z(over_y(over_x(both)))
    if order == "yx":
        return over_z(over_x(over_y(both)))
    cut = both.shape[-1] // 2
    left = over_y(over_x(both[..., :cut]))
    right = over_x(over_y(both[..., cut:]))
    return over_z(jnp.concatenate([left, right], axis=-1))


def scatter_any(keep, send):
    both = jnp.stack([keep, send], 0)
    both = both.transpose(2, 1, 0, 3, 4)
    both = both.reshape(-1, both.shape[-1])
    return lax.psum_scatter(both.astype(F32), ("batch", "head"), scatter_dimension=0, tiled=True)


def sum_small(items):
    count = lax.axis_size("batch") * lax.axis_size("head")
    flat = [
        item.reshape(item.shape[0], count, -1).transpose(1, 0, 2).reshape(count, -1)
        for item in items
    ]
    sizes = [item.shape[1] for item in flat]
    joined = jnp.concatenate(flat, 1)
    got = lax.all_to_all(joined, ("batch", "head"), split_axis=0, concat_axis=0, tiled=True)
    total = jnp.sum(got, 0)
    out, at = [], 0
    for item, size in zip(items, sizes):
        out.append(total[at : at + size].reshape(item.shape[0], -1))
        at += size
    return out


def relative_rows(pos, width, rows):
    at = jnp.arange(width, dtype=jnp.int32)
    inner = at % rows
    block = at // rows
    batch = (block % BLOCKS) ^ pos[3]
    x = ((block // BLOCKS) % 2) ^ pos[2]
    core = (block // (2 * BLOCKS)) ^ pos[1]
    return (batch * 4 + x * 2 + core) * rows + inner


def on_device(
    tokens,
    pass_ids,
    segment_ids,
    pass_embed,
    norm1_gain,
    norm1_shift,
    qkv_weight,
    qv_bias,
    out_weight,
    out_bias,
    norm2_gain,
    norm2_shift,
    up_weight,
    up_bias,
    down_weight,
    down_bias,
    cotangent,
):
    rows, width = tokens.shape
    half = width // 2
    hidden_units = up_weight.shape[1]
    passes = pass_embed.shape[0]
    assert 2 * rows == SEQ_LEN and lax.axis_size("head") == 4
    direct = lax.axis_size("batch") == BLOCKS

    head = lax.axis_index("head").astype(jnp.int32)
    batch = lax.axis_index("batch").astype(jnp.int32)
    core, x_bit = head % 2, head // 2
    segments = lax.dynamic_index_in_dim(segment_ids, x_bit, 0, keepdims=False)
    start = jnp.zeros((SEQ_LEN,), jnp.int32)
    for number in range(1, 4):
        before = jnp.sum((segments < number).astype(jnp.int32))
        start = jnp.where(segments == number, before, start)
    low = start[::BQ] // BK
    zero = jnp.zeros((), jnp.int32)
    place = [core, x_bit, batch] if direct else [zero, zero, zero]
    pos = jnp.concatenate([jnp.stack([core] + place + [zero] * 4), low])
    start = start.reshape(1, SEQ_LEN)

    ids = pass_ids.reshape(rows, 1)
    row = lambda item: item.astype(F32).reshape(1, -1)
    gain_one, shift_one = row(norm1_gain), row(norm1_shift)
    gain_two, shift_two = row(norm2_gain), row(norm2_shift)
    zeros = jnp.zeros((width,), F32)
    bias_full = jnp.concatenate([qv_bias[0].astype(F32), zeros, qv_bias[1].astype(F32)]).reshape(1, -1)
    shard_rows = width // (4 * BLOCKS)
    perm = (
        relative_rows(pos, width, shard_rows)[:, None] == jnp.arange(width, dtype=jnp.int32)[None, :]
    ).astype(BF16)

    shape = jax.ShapeDtypeStruct
    normed, send = qkv_send(pos, tokens, ids, pass_embed, gain_one, shift_one, qkv_weight, bias_full)
    recv = swap_head(send, 1)
    keep = qkv_keep(pos, normed, qkv_weight, bias_full)
    own, far_send, lse = attend(pos, start, keep, recv)
    far = swap_head(far_send, 1)
    after, normed_two = simple_call(
        out_proj_kernel,
        [shape((rows, width), F32), shape((rows, width), BF16)],
        2 * rows * width * width,
        "out_proj",
    )(pos, tokens, ids, pass_embed, own, far, out_weight, row(out_bias), gain_two, shift_two)
    activated, grad_pre, down_keep, down_send, up_bias_grad = ff_first(
        pos, normed_two, cotangent, perm, up_weight, row(up_bias), down_weight
    )
    grad_normed_two, up_keep, up_send = ff_second(pos, grad_pre, normed_two, up_weight)
    grad_after, branch, grad_own, grad_send, sums_two = simple_call(
        out_back_kernel,
        [
            shape((rows, width), F32),
            shape((rows, width), BF16),
            shape((rows, half), BF16),
            shape((rows, half), BF16),
            shape((4, width), F32),
        ],
        2 * rows * width * width,
        "out_back",
    )(pos, grad_normed_two, after, cotangent, gain_two, out_weight)
    grad_far = swap_head(grad_send, 1)
    out_keep, out_send = simple_call(
        out_weight_kernel,
        [shape((half, width), BF16), shape((half, width), BF16)],
        4 * rows * width * width,
        "out_weight",
    )(pos, branch, perm, own, far)
    joined_keep, joined_send = attend_back(
        pos, start, lse, keep, recv, own, far_send, grad_own, grad_far
    )
    joined_recv = swap_head(joined_send, 1)
    qkv_keep_grad, qkv_send_grad, bias_sums = qkv_weight_call(pos, joined_keep, joined_recv, normed)
    input_grad, sums_one = simple_call(
        input_back_kernel,
        [shape((rows, width), F32), shape((passes + 2, width), F32)],
        6 * rows * width * width,
        "input_back",
    )(pos, joined_keep, joined_recv, qkv_weight, tokens, ids, pass_embed, gain_one, grad_after)
    result = mixed_call(pos, activated, down_weight, after, row(down_bias))

    def spread(item):
        return item.reshape(2, BLOCKS, shard_rows, -1)

    down_keep, down_send = spread(down_keep), spread(down_send)
    out_keep, out_send = spread(out_keep), spread(out_send)
    if direct:
        down_grad = scatter_sum(down_keep, down_send, "xy")
        up_grad = scatter_sum(up_keep, up_send, "yx")
        out_grad = scatter_sum(out_keep, out_send, "yx")
        qkv_grad = scatter_sum(qkv_keep_grad, qkv_send_grad, "both")
    else:
        down_grad = scatter_any(down_keep, down_send)
        up_grad = scatter_any(up_keep, up_send)
        out_grad = scatter_any(out_keep, out_send)
        qkv_grad = scatter_any(qkv_keep_grad, qkv_send_grad)
    small = sum_small([sums_one, bias_sums, sums_two, up_bias_grad])
    return (
        result,
        input_grad,
        small[0][:passes],
        small[0][passes],
        small[0][passes + 1],
        qkv_grad.T,
        jnp.stack([small[1][0], small[1][2]]),
        out_grad.T,
        small[2][2],
        small[2][0],
        small[2][1],
        up_grad.T,
        small[3][0],
        down_grad.T,
        small[2][3],
    )


def solution(mesh):
    both = ("batch", "head")
    copied = P()
    in_specs = (P(both, None), P(both), P("batch", None)) + (copied,) * 13 + (P(both, None),)
    out_specs = (
        P(both, None),
        P(both, None),
        P(None, both),
        P(both),
        P(both),
        P(None, both),
        P(None, both),
        P(None, both),
        P(both),
        P(both),
        P(both),
        P(None, both),
        P(both),
        P(None, both),
        P(both),
    )
    return jax.shard_map(
        on_device, mesh=mesh, in_specs=in_specs, out_specs=out_specs, check_vma=False
    )
```

```python
import jax
import jax.numpy as jnp
from jax import lax
from jax.experimental import pallas as pl
from jax.experimental.pallas import tpu as pltpu
from jax.sharding import PartitionSpec as P

HEAD_DIM = 64
SEQ_LEN = 1280
PAIR = 2 * HEAD_DIM
BQ = 256
BK = 128
BLOCKS = 8
SUB = 256
NEG = -1e30
F32 = jnp.float32
BF16 = jnp.bfloat16
VMEM_LIMIT = 56 * 1024 * 1024


def dot(left, right):
    return lax.dot_general(left, right, (((1,), (0,)), ((), ())), preferred_element_type=F32)


def dot_nt(left, right):
    return lax.dot_general(left, right, (((1,), (1,)), ((), ())), preferred_element_type=F32)


def center_and_scale(values):
    center = values - jnp.mean(values, -1, keepdims=True)
    spread = jnp.mean(center * center, -1, keepdims=True)
    scale = lax.rsqrt(spread + 1e-05)
    return center * scale, scale


def dot_tn(left, right):
    return lax.dot_general(left, right, (((0,), (0,)), ((), ())), preferred_element_type=F32)


def pass_rows(ids_ref, passes):
    ids = ids_ref[...]
    row = lax.broadcasted_iota(jnp.int32, (passes, ids.shape[1]), 0)
    return (row == ids).astype(F32).astype(BF16)


def embed_tokens(tok_ref, ids_ref, emb_ref):
    return tok_ref[...].astype(F32) + dot_tn(pass_rows(ids_ref, emb_ref.shape[0]), emb_ref[...])


def wide(item):
    return item[...].astype(F32)


def half_lanes(core, half):
    return pl.ds(pl.multiple_of(core * half, 128), half)


def whole(shape):
    return pl.BlockSpec(shape, lambda *_: (0,) * len(shape))


def carry(operands, outs, carried):
    return {1 + operands + at: outs + at for at in range(len(carried))}


def shapes(items):
    return [jax.ShapeDtypeStruct(item.shape, item.dtype) for item in items]


def params():
    return pltpu.CompilerParams(vmem_limit_bytes=VMEM_LIMIT)


def cost():
    return pl.CostEstimate(flops=1000, transcendentals=0, bytes_accessed=1000)


ANY = pl.BlockSpec(memory_space=pl.ANY)


def third_bias(bias):
    third = pl.program_id(0)
    rows = bias[...].astype(F32)
    return jnp.where(third == 0, rows[0:1], jnp.where(third == 2, rows[1:2], 0.0))


def qkv_send_kernel(pos, tok, ids, emb, gain, shift, weight, bias, normed_out, half_out, out):
    @pl.when(pl.program_id(0) == 0)
    def _():
        scaled, _ = center_and_scale(embed_tokens(tok, ids, emb))
        normed_out[...] = (scaled * wide(gain) + wide(shift)).astype(BF16)
        half_out[...] = normed_out[:, half_lanes(1 - pos[0], half_out.shape[1])]

    out[0] = (dot(normed_out[...], weight[...]) + third_bias(bias)).astype(BF16)


def qkv_keep_kernel(pos, normed, weight, bias, out):
    out[0] = (dot(normed[...], weight[...]) + third_bias(bias)).astype(BF16)


def qkv_send(pos, tok, ids, emb, gain, shift, weight, bias):
    rows, width = tok.shape
    half = width // 2
    return pl.pallas_call(
        qkv_send_kernel,
        grid_spec=pltpu.PrefetchScalarGridSpec(
            num_scalar_prefetch=1,
            grid=(3,),
            in_specs=[
                whole(tok.shape),
                whole(ids.shape),
                whole(emb.shape),
                whole(gain.shape),
                whole(shift.shape),
                pl.BlockSpec((width, half), lambda t, s: (0, 2 * t + 1 - s[0])),
                pl.BlockSpec((2, half), lambda t, s: (0, 1 - s[0])),
            ],
            out_specs=[
                whole(tok.shape),
                whole((rows, half)),
                pl.BlockSpec((1, rows, half), lambda t, s: (t, 0, 0)),
            ],
        ),
        out_shape=[
            jax.ShapeDtypeStruct(tok.shape, BF16),
            jax.ShapeDtypeStruct((rows, half), BF16),
            jax.ShapeDtypeStruct((3, rows, half), BF16),
        ],
        compiler_params=params(),
        cost_estimate=cost(),
        name="qkv_send",
    )(pos, tok, ids, emb, gain, shift, weight, bias)


def qkv_keep(pos, normed, weight, bias):
    rows, width = normed.shape
    half = width // 2
    return pl.pallas_call(
        qkv_keep_kernel,
        grid_spec=pltpu.PrefetchScalarGridSpec(
            num_scalar_prefetch=1,
            grid=(3,),
            in_specs=[
                whole(normed.shape),
                pl.BlockSpec((width, half), lambda t, s: (0, 2 * t + s[0])),
                pl.BlockSpec((2, half), lambda t, s: (0, s[0])),
            ],
            out_specs=pl.BlockSpec((1, rows, half), lambda t, s: (t, 0, 0)),
        ),
        out_shape=jax.ShapeDtypeStruct((3, rows, half), BF16),
        compiler_params=params(),
        cost_estimate=cost(),
        name="qkv_keep",
    )(pos, normed, weight, bias)


def lane_masks():
    lane = lax.broadcasted_iota(jnp.int32, (1, PAIR), 1)
    first = (lane < HEAD_DIM).astype(F32).astype(BF16)
    return first, (1 - first).astype(BF16)


def row_split(values):
    row = lax.broadcasted_iota(jnp.int32, values.shape, 0)
    keep = row < HEAD_DIM
    wide = values.astype(F32)
    return jnp.concatenate(
        [jnp.where(keep, wide, 0.0).astype(BF16), jnp.where(keep, 0.0, wide).astype(BF16)], axis=1
    )


def gather_rows(mine, other, target, sems, core, rows):
    own = pl.ds(pl.multiple_of(core * rows, 128), rows)
    far = pl.ds(pl.multiple_of((1 - core) * rows, 128), rows)
    if len(mine.shape) == 3:
        return (
            pltpu.make_async_copy(mine, target.at[:, own, :], sems.at[0]),
            pltpu.make_async_copy(other, target.at[:, far, :], sems.at[1]),
        )
    return (
        pltpu.make_async_copy(mine, target.at[own, :], sems.at[0]),
        pltpu.make_async_copy(other, target.at[far, :], sems.at[1]),
    )


def segment_firsts(seg_ref, x):
    row = seg_ref[pl.ds(x, 1), :]
    return [jnp.sum((row < number).astype(F32)).astype(jnp.int32) for number in (1, 2, 3)]


def fill_starts(firsts, start):
    at = lax.broadcasted_iota(jnp.int32, start.shape, 1)
    own = jnp.zeros(start.shape, jnp.int32)
    for first in firsts:
        own = jnp.where(at >= first, first, own)
    start[...] = own


def first_block(firsts, q0):
    own = jnp.int32(0)
    for first in firsts:
        own = jnp.where(first <= q0, first, own)
    return own // BK


def valid_keys(start, q0, kb):
    key_at = lax.broadcasted_iota(jnp.int32, (BK, BQ), 0) + kb * BK
    query_at = lax.broadcasted_iota(jnp.int32, (BK, BQ), 1) + q0
    inside = (key_at >= start) & (key_at <= query_at)
    return jnp.concatenate([inside, inside], axis=1)


def attend_kernel(pos, seg, keep, recv, own_out, far_out, lse_out, qkv, qq, vm, sc, acc, joined, start_ref, sems):
    core = pos[0]
    rows = own_out.shape[0]
    pairs = own_out.shape[1] // PAIR
    copies = gather_rows(keep, recv, qkv, sems, core, rows)
    for item in copies:
        item.start()
    firsts = segment_firsts(seg, pos[4])
    fill_starts(firsts, start_ref)
    for item in copies:
        item.wait()
    first, second = lane_masks()

    def prepare(kb, _):
        at = pl.ds(pl.multiple_of(kb * BK, BK), BK)
        for p in range(pairs):
            vm[kb, p] = row_split(qkv[2, at, p * PAIR : (p + 1) * PAIR].T)
        return 0

    lax.fori_loop(0, SEQ_LEN // BK, prepare, 0)

    def one_block(qi, _):
        q0 = pl.multiple_of(qi * BQ, BQ)
        at = pl.ds(q0, BQ)
        start = start_ref[:, at]
        low = first_block(firsts, q0)
        high = (qi + 1) * (BQ // BK)
        for p in range(pairs):
            q = qkv[0, at, p * PAIR : (p + 1) * PAIR] * jnp.asarray(0.125, BF16)
            qq[p, :BQ] = q * first
            qq[p, BQ:] = q * second
            acc[p] = jnp.zeros((PAIR, BQ), F32)

        def scores(kb, tops):
            inside = valid_keys(start, q0, kb)
            rows_at = pl.ds(pl.multiple_of(kb * BK, BK), BK)
            grown = []
            for p in range(pairs):
                s = dot_nt(qkv[1, rows_at, p * PAIR : (p + 1) * PAIR], qq[p])
                s = jnp.where(inside, s, NEG)
                sc[kb - low, p] = s
                grown.append(jnp.maximum(tops[p], jnp.max(s, axis=0, keepdims=True)))
            return tuple(grown)

        tops = lax.fori_loop(
            low, high, scores, tuple(jnp.full((1, 2 * BQ), NEG, F32) for _ in range(pairs))
        )

        def weigh(kb, sums):
            grown = []
            for p in range(pairs):
                raw = jnp.exp(sc[kb - low, p] - tops[p])
                grown.append(sums[p] + jnp.sum(raw, axis=0, keepdims=True))
                raw = raw.astype(BF16)
                acc[p] += dot(vm[kb, p], jnp.concatenate([raw[:, :BQ], raw[:, BQ:]], axis=0))
            return tuple(grown)

        sums = lax.fori_loop(
            low, high, weigh, tuple(jnp.zeros((1, 2 * BQ), F32) for _ in range(pairs))
        )
        for p in range(pairs):
            inv = 1.0 / sums[p]
            out = jnp.concatenate(
                [acc[p, :HEAD_DIM] * inv[:, :BQ], acc[p, HEAD_DIM:] * inv[:, BQ:]], axis=0
            )
            joined[at, p * PAIR : (p + 1) * PAIR] = out.T.astype(BF16)
            lse_out[qi, p] = tops[p] + jnp.log(sums[p])
        return 0

    lax.fori_loop(0, SEQ_LEN // BQ, one_block, 0)
    own_out[...] = joined[pl.ds(pl.multiple_of(core * rows, 128), rows), :]
    far_out[...] = joined[pl.ds(pl.multiple_of((1 - core) * rows, 128), rows), :]


def attend(pos, seg, keep, recv):
    _, rows, half = keep.shape
    pairs = half // PAIR
    window = SEQ_LEN // BK
    return pl.pallas_call(
        attend_kernel,
        grid_spec=pltpu.PrefetchScalarGridSpec(
            num_scalar_prefetch=1,
            grid=(1,),
            in_specs=[whole(seg.shape), ANY, ANY],
            out_specs=[
                whole((rows, half)),
                whole((rows, half)),
                whole((SEQ_LEN // BQ, pairs, 1, 2 * BQ)),
            ],
            scratch_shapes=[
                pltpu.VMEM((3, SEQ_LEN, half), BF16),
                pltpu.VMEM((pairs, 2 * BQ, PAIR), BF16),
                pltpu.VMEM((SEQ_LEN // BK, pairs, PAIR, 2 * BK), BF16),
                pltpu.VMEM((window, pairs, BK, 2 * BQ), F32),
                pltpu.VMEM((pairs, PAIR, BQ), F32),
                pltpu.VMEM((SEQ_LEN, half), BF16),
                pltpu.VMEM((1, SEQ_LEN), jnp.int32),
                pltpu.SemaphoreType.DMA((2,)),
            ],
        ),
        out_shape=[
            jax.ShapeDtypeStruct((rows, half), BF16),
            jax.ShapeDtypeStruct((rows, half), BF16),
            jax.ShapeDtypeStruct((SEQ_LEN // BQ, pairs, 1, 2 * BQ), F32),
        ],
        compiler_params=params(),
        cost_estimate=cost(),
        name="attend",
    )(pos, seg, keep, recv)


def attend_back_kernel(
    pos, seg, lse_ref, keep, recv, own, far, grad_own, grad_far, *rest, ties
):
    keep_out, send_out, qkv, att, dout, qq, dd, km, delta, dq_t, dq, dk, dv, start_ref, sems = rest[ties:]
    core = pos[0]
    rows, half = own.shape
    pairs = half // PAIR
    copies = (
        gather_rows(keep, recv, qkv, sems.at[0], core, rows)
        + gather_rows(own, far, att, sems.at[1], core, rows)
        + gather_rows(grad_own, grad_far, dout, sems.at[2], core, rows)
    )
    for item in copies:
        item.start()
    firsts = segment_firsts(seg, pos[4])
    fill_starts(firsts, start_ref)
    dk[...] = jnp.zeros_like(dk)
    dv[...] = jnp.zeros_like(dv)
    for item in copies:
        item.wait()
    first, second = lane_masks()

    def prepare(kb, _):
        at = pl.ds(pl.multiple_of(kb * BK, BK), BK)
        for p in range(pairs):
            km[kb, p] = row_split(qkv[1, at, p * PAIR : (p + 1) * PAIR].T)
        return 0

    lax.fori_loop(0, SEQ_LEN // BK, prepare, 0)

    def one_block(qi, _):
        q0 = pl.multiple_of(qi * BQ, BQ)
        at = pl.ds(q0, BQ)
        start = start_ref[:, at]
        low = first_block(firsts, q0)
        high = (qi + 1) * (BQ // BK)
        for p in range(pairs):
            lanes = slice(p * PAIR, (p + 1) * PAIR)
            q = qkv[0, at, lanes] * jnp.asarray(0.125, BF16)
            qq[p, :BQ] = q * first
            qq[p, BQ:] = q * second
            g = dout[at, lanes]
            dd[p, :BQ] = g * first
            dd[p, BQ:] = g * second
            both = (g.astype(F32) * att[at, lanes].astype(F32)).T
            delta[p] = jnp.concatenate(
                [
                    jnp.sum(both[:HEAD_DIM], axis=0, keepdims=True),
                    jnp.sum(both[HEAD_DIM:], axis=0, keepdims=True),
                ],
                axis=1,
            )
            dq_t[p] = jnp.zeros((PAIR, BQ), F32)

        def step(kb, _):
            inside = valid_keys(start, q0, kb)
            rows_at = pl.ds(pl.multiple_of(kb * BK, BK), BK)
            for p in range(pairs):
                lanes = slice(p * PAIR, (p + 1) * PAIR)
                s = dot_nt(qkv[1, rows_at, lanes], qq[p])
                prob = jnp.where(inside, jnp.exp(s - lse_ref[qi, p]), 0.0)
                grad_prob = dot_nt(qkv[2, rows_at, lanes], dd[p])
                grad_s = (prob * (grad_prob - delta[p])).astype(BF16)
                dv[rows_at, lanes] += dot(prob.astype(BF16), dd[p])
                dk[rows_at, lanes] += dot(grad_s, qq[p])
                dq_t[p] += dot(km[kb, p], jnp.concatenate([grad_s[:, :BQ], grad_s[:, BQ:]], axis=0))
            return 0

        lax.fori_loop(low, high, step, 0)
        for p in range(pairs):
            dq[p * PAIR : (p + 1) * PAIR, at] = (dq_t[p] * 0.125).astype(BF16)
        return 0

    lax.fori_loop(0, SEQ_LEN // BQ, one_block, 0)
    for target, at in ((keep_out, core), (send_out, 1 - core)):
        tokens = pl.ds(pl.multiple_of(at * rows, 128), rows)
        target[0] = dq[:, tokens]
        target[1] = dk[tokens, :].astype(BF16).T
        target[2] = dv[tokens, :].astype(BF16).T


def attend_back(ties, pos, seg, lse, keep, recv, own, far, grad_own, grad_far):
    _, rows, half = keep.shape
    pairs = half // PAIR
    out = (3, half, rows)

    def kernel(*refs):
        attend_back_kernel(*refs, ties=len(ties))

    return pl.pallas_call(
        kernel,
        grid_spec=pltpu.PrefetchScalarGridSpec(
            num_scalar_prefetch=1,
            grid=(1,),
            in_specs=[whole(seg.shape), whole(lse.shape)] + [ANY] * (6 + len(ties)),
            out_specs=[whole(out), whole(out)],
            scratch_shapes=[
                pltpu.VMEM((3, SEQ_LEN, half), BF16),
                pltpu.VMEM((SEQ_LEN, half), BF16),
                pltpu.VMEM((SEQ_LEN, half), BF16),
                pltpu.VMEM((pairs, 2 * BQ, PAIR), BF16),
                pltpu.VMEM((pairs, 2 * BQ, PAIR), BF16),
                pltpu.VMEM((SEQ_LEN // BK, pairs, PAIR, 2 * BK), BF16),
                pltpu.VMEM((pairs, 1, 2 * BQ), F32),
                pltpu.VMEM((pairs, PAIR, BQ), F32),
                pltpu.VMEM((half, SEQ_LEN), BF16),
                pltpu.VMEM((SEQ_LEN, half), F32),
                pltpu.VMEM((SEQ_LEN, half), F32),
                pltpu.VMEM((1, SEQ_LEN), jnp.int32),
                pltpu.SemaphoreType.DMA((3, 2)),
            ],
        ),
        out_shape=[jax.ShapeDtypeStruct(out, BF16)] * 2,
        compiler_params=params(),
        cost_estimate=cost(),
        name="attend_back",
    )(pos, seg, lse, keep, recv, own, far, grad_own, grad_far, *ties)


def gather_lanes(core, own, far, target):
    half = own.shape[1]
    target[:, half_lanes(core, half)] = own[...]
    target[:, half_lanes(1 - core, half)] = far[...]


def hidden_block(i, core):
    late = i >> 1
    return 2 * (late * core + (1 - late) * (1 - core)) + (i & 1)


def early(i):
    return jnp.minimum(i, 1)


def late(i):
    return jnp.maximum(i - 2, 0)


def ff_first_kernel(
    pos, tok, ids, emb, own, far, weight, bias, gain, shift, cot, up, up_bias, down,
    after_out, normed_out, half_out, act_own, act_send, grad_out, bias_grad, attended, act,
):
    step = pl.program_id(0)

    @pl.when(step == 0)
    def _():
        gather_lanes(pos[0], own, far, attended)
        after = embed_tokens(tok, ids, emb) + dot(attended[...], weight[...]) + wide(bias)
        after_out[...] = after
        scaled, _ = center_and_scale(after)
        normed_out[...] = (scaled * wide(gain) + wide(shift)).astype(BF16)
        half_out[...] = normed_out[:, half_lanes(1 - pos[0], half_out.shape[1])]

    for part in range(up.shape[1] // SUB):
        cols = slice(part * SUB, (part + 1) * SUB)
        u = dot(normed_out[...], up[:, cols]) + up_bias[:, cols].astype(F32)
        grad_act = dot_nt(cot[...], down[cols, :])
        square = u * u
        t = jnp.tanh(0.7978845608028654 * u * (1.0 + 0.044715 * square))
        half = 0.5 * (1.0 + t)
        act[:, cols] = (u * half).astype(BF16)
        slope = half + 0.5 * u * (1.0 - t * t) * (0.7978845608028654 * (1.0 + 0.134145 * square))
        grad = (grad_act * slope).astype(BF16)
        grad_out[:, cols] = grad
        bias_grad[:, cols] = jnp.sum(grad.astype(F32), axis=0, keepdims=True)

    @pl.when(step < 2)
    def _():
        act_send[...] = act[...]

    @pl.when(step >= 2)
    def _():
        act_own[...] = act[...]


def ff_first(pos, tok, ids, emb, own, far, weight, bias, gain, shift, cot, up, up_bias, down):
    rows, width = tok.shape
    hidden = up.shape[1]
    first = (tok, ids, emb, own, far, weight, bias, gain, shift, cot)
    shape = jax.ShapeDtypeStruct
    return pl.pallas_call(
        ff_first_kernel,
        grid_spec=pltpu.PrefetchScalarGridSpec(
            num_scalar_prefetch=1,
            grid=(4,),
            in_specs=[whole(item.shape) for item in first]
            + [
                pl.BlockSpec((width, width), lambda i, s: (0, hidden_block(i, s[0]))),
                pl.BlockSpec((1, width), lambda i, s: (0, hidden_block(i, s[0]))),
                pl.BlockSpec((width, width), lambda i, s: (hidden_block(i, s[0]), 0)),
            ],
            out_specs=[
                whole((rows, width)),
                whole((rows, width)),
                whole((rows, width // 2)),
                pl.BlockSpec((rows, width), lambda i, s: (0, late(i))),
                pl.BlockSpec((rows, width), lambda i, s: (0, early(i))),
                pl.BlockSpec((rows, width), lambda i, s: (0, hidden_block(i, s[0]))),
                pl.BlockSpec((1, width), lambda i, s: (0, hidden_block(i, s[0]))),
            ],
            scratch_shapes=[pltpu.VMEM((rows, width), BF16), pltpu.VMEM((rows, width), BF16)],
        ),
        out_shape=[
            shape((rows, width), F32),
            shape((rows, width), BF16),
            shape((rows, width // 2), BF16),
            shape((rows, hidden // 2), BF16),
            shape((rows, hidden // 2), BF16),
            shape((rows, hidden), BF16),
            shape((1, hidden), F32),
        ],
        compiler_params=params(),
        cost_estimate=cost(),
        name="ff_first",
    )(pos, *first, up, up_bias, down)


def ff_back_kernel(
    pos, grad_pre, up, after, cot, gain, weight,
    grad_after, branch_out, own_out, far_out, sums, total,
):
    step = pl.program_id(0)
    part = dot_nt(grad_pre[...], up[...])

    @pl.when(step == 0)
    def _():
        total[...] = part

    @pl.when(step > 0)
    def _():
        total[...] += part

    @pl.when(step == pl.num_programs(0) - 1)
    def _():
        core = pos[0]
        half = own_out.shape[1]
        scaled, scale = center_and_scale(after[...])
        grad = total[...]
        inner = grad * wide(gain)
        shift = jnp.mean(inner, -1, keepdims=True)
        slope = jnp.mean(inner * scaled, -1, keepdims=True)
        cot_f32 = wide(cot)
        result = cot_f32 + scale * (inner - shift - scaled * slope)
        grad_after[...] = result
        branch_out[...] = result.astype(BF16)
        branch = branch_out[...]
        for target, at in ((far_out, 1 - core), (own_out, core)):
            rows = pl.ds(pl.multiple_of(at * half, 128), half)
            target[...] = dot_nt(branch, weight[rows, :]).astype(BF16)
        sums[0:1] = jnp.sum(grad * scaled, axis=0, keepdims=True)
        sums[1:2] = jnp.sum(grad, axis=0, keepdims=True)
        sums[2:3] = jnp.sum(branch.astype(F32), axis=0, keepdims=True)
        sums[3:4] = jnp.sum(cot_f32, axis=0, keepdims=True)


def ff_back(pos, grad_pre, up, after, cot, gain, weight):
    rows, width = after.shape
    half = width // 2
    last = (after, cot, gain, weight)
    outs = [
        jax.ShapeDtypeStruct((rows, width), F32),
        jax.ShapeDtypeStruct((rows, width), BF16),
        jax.ShapeDtypeStruct((rows, half), BF16),
        jax.ShapeDtypeStruct((rows, half), BF16),
        jax.ShapeDtypeStruct((4, width), F32),
    ]
    return pl.pallas_call(
        ff_back_kernel,
        grid_spec=pltpu.PrefetchScalarGridSpec(
            num_scalar_prefetch=1,
            grid=(grad_pre.shape[1] // width,),
            in_specs=[
                pl.BlockSpec((rows, width), lambda i, s: (0, i)),
                pl.BlockSpec((width, width), lambda i, s: (0, i)),
            ]
            + [whole(item.shape) for item in last],
            out_specs=[whole(item.shape) for item in outs],
            scratch_shapes=[pltpu.VMEM((rows, width), F32)],
        ),
        out_shape=outs,
        compiler_params=params(),
        cost_estimate=cost(),
        name="ff_back",
    )(pos, grad_pre, up, *last)


def z_place(z):
    return (z & 1) * 2 + (z >> 1)


def chips():
    return [(x, y, z) for x in range(2) for y in range(2) for z in range(4)]


def chip_row(pos, x, y, z):
    return ((2 * z_place(z) + y) ^ pos[3]) * 2 + (x ^ pos[2])


def rows_of(values, chip, per, at=0, count=None):
    count = per if count is None else count
    return values[pl.ds(pl.multiple_of(chip * per + at, 8), count), :].astype(BF16)


def middle_weights_kernel(
    pos, act, act_far, grad, grad_far, cot, cot_far, normed, normed_far, *rest, ties
):
    left_keep, left_send, right_keep, right_send, rows_f32 = rest[ties:]
    step = pl.program_id(0)
    half = normed_far.shape[1]
    left, right = (left_keep, left_send), (right_keep, right_send)

    @pl.when(step < 2)
    def _():
        per = rows_f32.shape[0] // 16
        for part in range(2):
            cols = slice(part * half, (part + 1) * half)
            rows_f32[...] = dot_tn(cot[...], act[:, cols]) + dot_tn(cot_far[...], act_far[:, cols])
            for x, y, z in chips():
                left[x][y, z, part * per : (part + 1) * per, :] = rows_of(
                    rows_f32, chip_row(pos, x, y, z), per
                )

    @pl.when(step >= 2)
    def _():
        per = rows_f32.shape[0] // 4
        own = normed[:, half_lanes(pos[0], half)]
        rows_f32[...] = dot_tn(grad[...], own) + dot_tn(grad_far[...], normed_far[...])
        for x in range(2):
            for y in range(2):
                chip = (y ^ (pos[3] & 1)) * 2 + (x ^ pos[2])
                right[y][x, 0, :per, :] = rows_of(rows_f32, chip, per)


def middle_weights(pos, ties, act, act_far, grad, grad_far, cot, cot_far, normed, normed_far):
    rows, width = normed.shape
    half = width // 2
    per = width // 16
    left = jax.ShapeDtypeStruct((2, 4, 4 * per, half), BF16)
    right = jax.ShapeDtypeStruct((2, 4, 5 * per, half), BF16)
    fixed = (cot, cot_far, normed, normed_far)

    def kernel(*refs):
        middle_weights_kernel(*refs, ties=len(ties))

    def left_at(i, s):
        return 0, 0, early(i), 0

    def right_at(i, s):
        return 0, z_place(late(i) ^ (s[3] >> 1)), 0, 0

    return pl.pallas_call(
        kernel,
        grid_spec=pltpu.PrefetchScalarGridSpec(
            num_scalar_prefetch=1,
            grid=(6,),
            in_specs=[pl.BlockSpec((rows, width), lambda i, s: (0, early(i)))] * 2
            + [pl.BlockSpec((rows, width), lambda i, s: (0, late(i)))] * 2
            + [whole(item.shape) for item in fixed]
            + [ANY] * len(ties),
            out_specs=[pl.BlockSpec((2, 4, 2 * per, half), left_at)] * 2
            + [pl.BlockSpec((2, 1, 4 * per, half), right_at)] * 2,
            scratch_shapes=[pltpu.VMEM((width, half), F32)],
        ),
        out_shape=[left, left, right, right],
        compiler_params=params(),
        cost_estimate=cost(),
        name="middle_weights",
    )(pos, act, act_far, grad, grad_far, *fixed, *ties)


def out_weight_kernel(pos, branch, branch_far, own, far, keep_in, send_in, keep_out, send_out, rows_f32):
    per = rows_f32.shape[0] // 16
    rows_f32[...] = dot_tn(branch[...], own[...]) + dot_tn(branch_far[...], far[...])
    for x, y, z in chips():
        (keep_out, send_out)[y][x, z] = rows_of(rows_f32, chip_row(pos, x, y, z), per)


def out_weight_call(pos, branch, branch_far, own, far, keep, send):
    rows, width = branch.shape
    half = width // 2
    block = pl.BlockSpec((2, 4, width // 16, half), lambda i, s: (0, 0, 4, 0))
    return pl.pallas_call(
        out_weight_kernel,
        grid_spec=pltpu.PrefetchScalarGridSpec(
            num_scalar_prefetch=1,
            grid=(1,),
            in_specs=[whole(branch.shape)] * 2 + [whole(own.shape)] * 2 + [ANY, ANY],
            out_specs=[block, block],
            scratch_shapes=[pltpu.VMEM((width, half), F32)],
        ),
        out_shape=[jax.ShapeDtypeStruct(keep.shape, BF16)] * 2,
        input_output_aliases={5: 0, 6: 1},
        compiler_params=params(),
        cost_estimate=cost(),
        name="out_weight",
    )(pos, branch, branch_far, own, far, keep, send)


def pack_sums(tables, long, packed):
    count, _, share = packed.shape
    for device in range(count):
        low = 0
        for table in tables:
            rows = table.shape[0]
            packed[device, low : low + rows, :] = table[:, device * share : (device + 1) * share]
            low += rows
        for part in range(4):
            at = (4 * device + part) * share
            packed[device, low + part : low + part + 1, :] = long[:, at : at + share]


def mixed_kernel(pos, act_send, act_own, down, after, bias, one, two, three, four, *rest, ties, carried):
    out, packed = rest[ties + carried : ties + carried + 2]
    total = rest[-1]
    step = pl.program_id(0)

    @pl.when(step == 0)
    def _():
        total[...] = after[...] + wide(bias)

    @pl.when(step < 2)
    def _():
        total[...] += dot(act_send[...], down[...])

    @pl.when(step >= 2)
    def _():
        total[...] += dot(act_own[...], down[...])

    @pl.when(step == pl.num_programs(0) - 1)
    def _():
        out[...] = total[...].astype(BF16)
        pack_sums((one, two, three), four, packed)


def mixed_call(pos, ties, carried, act_send, act_own, down, after, bias, *sums):
    rows, width = after.shape
    devices = lax.axis_size("batch") * lax.axis_size("head")
    packed = (devices, sum(item.shape[0] for item in sums[:3]) + 4, width // devices)

    def kernel(*refs):
        mixed_kernel(*refs, ties=len(ties), carried=len(carried))

    return pl.pallas_call(
        kernel,
        grid_spec=pltpu.PrefetchScalarGridSpec(
            num_scalar_prefetch=1,
            grid=(4,),
            in_specs=[
                pl.BlockSpec((rows, width), lambda i, s: (0, early(i))),
                pl.BlockSpec((rows, width), lambda i, s: (0, late(i))),
                pl.BlockSpec((width, width), lambda i, s: (hidden_block(i, s[0]), 0)),
                whole(after.shape),
                whole(bias.shape),
            ]
            + [whole(item.shape) for item in sums]
            + [ANY] * (len(ties) + len(carried)),
            out_specs=[whole((rows, width)), whole(packed)] + [ANY] * len(carried),
            scratch_shapes=[pltpu.VMEM((rows, width), F32)],
        ),
        out_shape=[jax.ShapeDtypeStruct((rows, width), BF16), jax.ShapeDtypeStruct(packed, F32)]
        + shapes(carried),
        input_output_aliases=carry(5 + len(sums) + len(ties), 2, carried),
        compiler_params=params(),
        cost_estimate=cost(),
        name="mixed",
    )(pos, act_send, act_own, down, after, bias, *sums, *ties, *carried)


def qkv_weight_kernel(
    pos, mine, mine_far, other, other_far, normed, normed_far, *rest, ties
):
    left_keep, left_send, right_keep, right_send, sums, rows_f32 = rest[ties:]
    core = pos[0]
    half = normed_far.shape[1]
    third = pl.program_id(0)
    own = normed[:, half_lanes(core, half)]
    ones = jnp.ones((8, own.shape[0]), BF16)

    @pl.when(third == 0)
    def _():
        sums[...] = jnp.zeros_like(sums)

    for near, far, at in ((mine, mine_far, core), (other, other_far, 1 - core)):
        rows = pl.ds(pl.multiple_of((2 * third + at) * half, 128), half)
        rows_f32[rows, :] = dot(near[0], own) + dot(far[0], normed_far[...])
    row = (dot_nt(ones, mine[0]) + dot_nt(ones, mine_far[0]))[:1]
    lanes = half_lanes(core, half)
    for t in range(3):
        sums[t : t + 1, lanes] += jnp.where(third == t, row, 0.0)

    @pl.when(third == pl.num_programs(0) - 1)
    def _():
        per = rows_f32.shape[0] // 32
        for x, y, z in chips():
            chip = chip_row(pos, x, y, z)
            (left_keep, left_send)[x][y, z] = rows_of(rows_f32, chip, 2 * per, 0, per)
            (right_keep, right_send)[y][x, z] = rows_of(rows_f32, chip, 2 * per, per, per)


def qkv_weight_call(pos, ties, mine, mine_far, other, other_far, normed, normed_far):
    rows, width = normed.shape
    half = width // 2
    third = pl.BlockSpec((1, half, rows), lambda t, s: (t, 0, 0))
    out = jax.ShapeDtypeStruct((2, 4, 3 * width // 32, half), BF16)

    def kernel(*refs):
        qkv_weight_kernel(*refs, ties=len(ties))

    return pl.pallas_call(
        kernel,
        grid_spec=pltpu.PrefetchScalarGridSpec(
            num_scalar_prefetch=1,
            grid=(3,),
            in_specs=[third] * 4 + [whole(normed.shape), whole(normed_far.shape)] + [ANY] * len(ties),
            out_specs=[whole(out.shape)] * 4 + [whole((3, width))],
            scratch_shapes=[pltpu.VMEM((3 * width, half), F32)],
        ),
        out_shape=[out] * 4 + [jax.ShapeDtypeStruct((3, width), F32)],
        compiler_params=params(),
        cost_estimate=cost(),
        name="qkv_weight",
    )(pos, mine, mine_far, other, other_far, normed, normed_far, *ties)


def input_back_kernel(pos, mine, other, weight, tok, ids, emb, gain, grad_after, *rest, ties, carried):
    out, sums = rest[ties + carried : ties + carried + 2]
    joined, total = rest[-2:]
    core = pos[0]
    step = pl.program_id(0)
    half = mine.shape[1]
    joined[half_lanes(core, half), :] = mine[0]
    joined[half_lanes(1 - core, half), :] = other[0]
    part = lax.dot_general(
        joined[...], weight[...], (((0,), (1,)), ((), ())), preferred_element_type=F32
    )

    @pl.when(step == 0)
    def _():
        total[...] = part

    @pl.when(step > 0)
    def _():
        total[...] += part

    @pl.when(step == pl.num_programs(0) - 1)
    def _():
        grad = total[...]
        scaled, scale = center_and_scale(embed_tokens(tok, ids, emb))
        inner = grad * wide(gain)
        shift = jnp.mean(inner, -1, keepdims=True)
        slope = jnp.mean(inner * scaled, -1, keepdims=True)
        result = grad_after[...] + scale * (inner - shift - scaled * slope)
        out[...] = result
        passes = emb.shape[0]
        chosen = pass_rows(ids, passes)
        high = result.astype(BF16)
        less = result - high.astype(F32)
        middle = less.astype(BF16)
        least = (less - middle.astype(F32)).astype(BF16)
        sums[0:passes] = dot(chosen, high) + (dot(chosen, middle) + dot(chosen, least))
        sums[passes : passes + 1] = jnp.sum(grad * scaled, axis=0, keepdims=True)
        sums[passes + 1 : passes + 2] = jnp.sum(grad, axis=0, keepdims=True)


def input_back(pos, ties, carried, mine, other, weight, tok, ids, emb, gain, grad_after):
    rows, width = tok.shape
    third = pl.BlockSpec((1, width // 2, rows), lambda t, s: (t, 0, 0))
    fixed = (tok, ids, emb, gain, grad_after)
    outs = [
        jax.ShapeDtypeStruct((rows, width), F32),
        jax.ShapeDtypeStruct((emb.shape[0] + 2, width), F32),
    ]

    def kernel(*refs):
        input_back_kernel(*refs, ties=len(ties), carried=len(carried))

    return pl.pallas_call(
        kernel,
        grid_spec=pltpu.PrefetchScalarGridSpec(
            num_scalar_prefetch=1,
            grid=(3,),
            in_specs=[third, third, pl.BlockSpec((width, width), lambda t, s: (0, t))]
            + [whole(item.shape) for item in fixed]
            + [ANY] * (len(ties) + len(carried)),
            out_specs=[whole(item.shape) for item in outs] + [ANY] * len(carried),
            scratch_shapes=[pltpu.VMEM((width, rows), BF16), pltpu.VMEM((rows, width), F32)],
        ),
        out_shape=outs + shapes(carried),
        input_output_aliases=carry(3 + len(fixed) + len(ties), len(outs), carried),
        compiler_params=params(),
        cost_estimate=cost(),
        name="input_back",
    )(pos, mine, other, weight, *fixed, *ties, *carried)


def swap_head(values, bit):
    size = lax.axis_size("head")
    return lax.ppermute(values, "head", [(i, i ^ bit) for i in range(size)])


def swap_batch(values, bit):
    size = lax.axis_size("batch")
    return lax.ppermute(values, "batch", [(i, i ^ bit) for i in range(size)])


class Sum:
    def __init__(self, *parts):
        self.parts = parts

    def __getitem__(self, index):
        return Sum(*[part[index] for part in self.parts])

    def wide(self):
        total = self.parts[0].astype(F32)
        for part in self.parts[1:]:
            total = total + part.astype(F32)
        return total

    def sent(self):
        return self.wide().astype(BF16)


def swap_x(values):
    return swap_head(values, 2)


def swap_y(values):
    return swap_batch(values, 1)


def z_step(left, right):
    cut = left.parts[0].shape[0] // 2
    split = left.parts[0].shape[1]
    sent = jnp.concatenate([left[cut:].sent(), right[cut:].sent()], 1)

    def finish():
        got = swap_batch(sent, 2 if cut == 2 else 4)
        return Sum(*left[:cut].parts, got[:, :split]), Sum(*right[:cut].parts, got[:, split:])

    return sent, finish


def chip_sums(core, *items):
    flat = [jnp.where(core == 0, item[..., 1, :, :], item[..., 0, :, :]) for item in items]
    width = flat[0].shape[-1]
    got = swap_head(jnp.concatenate([item.reshape(-1, width) for item in flat], 0), 1)
    out, at = [], 0
    for item, sent in zip(items, flat):
        count = sent.size // width
        far = got[at : at + count].reshape(sent.shape)
        near = jnp.where(core == 0, item[..., 0, :, :], item[..., 1, :, :])
        out.append((jnp.where(core == 0, near, far), jnp.where(core == 0, far, near)))
        at += count
    return out


def scatter_any(core, values):
    half = values.shape[-1]
    rows = values.reshape(-1, half).astype(F32)
    both = lax.dynamic_update_slice(jnp.zeros((rows.shape[0], 2 * half), F32), rows, (0, core * half))
    return lax.psum_scatter(both, ("batch", "head"), scatter_dimension=0, tiled=True)


def by_chip(values):
    rest = values.shape[3:]
    split = values.reshape((2, 2, 2, 2) + rest)
    order = (3, 2, 1, 0) + tuple(range(4, split.ndim))
    return split.transpose(order).reshape((16,) + rest)


def on_device(
    tokens,
    pass_ids,
    segment_ids,
    pass_embed,
    norm1_gain,
    norm1_shift,
    qkv_weight,
    qv_bias,
    out_weight,
    out_bias,
    norm2_gain,
    norm2_shift,
    up_weight,
    up_bias,
    down_weight,
    down_bias,
    cotangent,
):
    rows, width = tokens.shape
    hidden_units = up_weight.shape[1]
    passes = pass_embed.shape[0]
    pairs = width // 2 // PAIR
    assert 2 * rows == SEQ_LEN and lax.axis_size("head") == 4 and hidden_units == 4 * width
    direct = lax.axis_size("batch") == BLOCKS

    head = lax.axis_index("head").astype(jnp.int32)
    batch = lax.axis_index("batch").astype(jnp.int32)
    core, x_bit = head % 2, head // 2
    zero = jnp.zeros((), jnp.int32)
    place = [core, x_bit, batch] if direct else [zero, zero, zero]
    pos = jnp.stack([core] + place + [x_bit])

    row = lambda item: item.reshape(1, -1)
    ids = row(pass_ids)
    gain_one, gain_two = row(norm1_gain), row(norm2_gain)
    cot_far = swap_head(cotangent, 1)
    normed, normed_send, send = qkv_send(
        pos, tokens, ids, pass_embed, gain_one, row(norm1_shift), qkv_weight, qv_bias
    )
    recv = swap_head(send, 1)
    normed_far = swap_head(normed_send, 1)
    keep = qkv_keep(pos, normed, qkv_weight, qv_bias)
    own, far_send, lse = attend(pos, segment_ids, keep, recv)
    far = swap_head(far_send, 1)
    after, normed_two, normed_two_send, act_own, act_send, grad_pre, up_bias_grad = ff_first(
        pos, tokens, ids, pass_embed, own, far, out_weight, row(out_bias), gain_two, row(norm2_shift),
        cotangent, up_weight, row(up_bias), down_weight,
    )
    act_far = swap_head(act_send, 1)
    grad_pre_far = swap_head(grad_pre, 1)
    normed_two_far = swap_head(normed_two_send, 1)
    grad_after, branch, grad_own, grad_send, sums_two = ff_back(
        pos, grad_pre, up_weight, after, cotangent, gain_two, out_weight
    )
    grad_far = swap_head(grad_send, 1)
    branch_far = swap_head(branch, 1)
    down_keep, down_send, up_keep, up_send = middle_weights(
        pos, (), act_own, act_far, grad_pre, grad_pre_far, cotangent, cot_far, normed_two, normed_two_far
    )
    up_keep, up_send = out_weight_call(pos, branch, branch_far, own, far_send, up_keep, up_send)
    if direct:
        left = Sum(down_keep, swap_x(down_send))
        right = Sum(up_keep, swap_y(up_send))
    mine, mine_send = attend_back(
        (down_send, up_send), pos, segment_ids, lse, keep, recv, own, far_send, grad_own, grad_far
    )
    other = swap_head(mine_send, 1)
    other_far = swap_head(mine, 1)
    ties, carried = (), ()
    if direct:
        left_sent, right_sent = left[1].sent(), right[1].sent()
        ties = (left_sent, right_sent)
    left_keep, left_send, right_keep, right_send, bias_sums = qkv_weight_call(
        pos, ties, mine, mine_send, other, other_far, normed, normed_far
    )
    if direct:
        one_got, two_got = swap_x(left_send), swap_y(right_send)
        left = Sum(*left[0].parts, swap_y(left_sent))
        right = Sum(*right[0].parts, swap_x(right_sent))
        mid_sent, mid_next = z_step(left, right)
        ties, carried = (mid_sent,), (left_keep, right_keep)
    input_grad, sums_one, *carried = input_back(
        pos, ties, carried, mine, other, qkv_weight, tokens, ids, pass_embed, gain_one, grad_after
    )
    if direct:
        one, two = Sum(carried[0], one_got), Sum(carried[1], two_got)
        one_sent, two_sent = one[1].sent(), two[1].sent()
        one_last, two_last = swap_y(one_sent), swap_x(two_sent)
        mid_sent, mid_next = z_step(*mid_next())
        qkv_sent, qkv_next = z_step(Sum(*one[0].parts, one_last), Sum(*two[0].parts, two_last))
        ties = (mid_sent, qkv_sent)
    result, packed, *carried = mixed_call(
        pos, ties, carried, act_send, act_own, down_weight, after, row(down_bias),
        sums_one, bias_sums, sums_two, up_bias_grad,
    )

    per = width // 32
    if direct:
        one, two = qkv_next()
        one = Sum(carried[0][0][:2], *one.parts[1:])
        two = Sum(carried[1][0][:2], *two.parts[1:])
        _, qkv_next = z_step(one, two)
        left, right = [item.wide()[0] for item in mid_next()]
        cut = 8 * per
        down, up, out = chip_sums(
            core,
            left.reshape(4, 2, per, -1),
            right[:cut].reshape(2, 4 * per, -1),
            right[cut:].reshape(2, per, -1),
        )
        (qkv,) = chip_sums(core, jnp.stack([item.wide()[0] for item in qkv_next()]))
        down_grad = jnp.concatenate(down, 0).transpose(0, 2, 1).reshape(hidden_units, -1)
        up_grad, out_grad, qkv_grad = [jnp.concatenate(item, -1) for item in (up, out, qkv)]
    else:
        down = by_chip(jnp.stack([down_keep, down_send])).reshape(16, 4, 2 * per, -1)
        down = down.transpose(0, 2, 1, 3).reshape(16, 2 * per, -1)
        up = by_chip(jnp.stack([up_keep, up_send], 1))
        left = by_chip(jnp.stack([left_keep, left_send]))
        right = by_chip(jnp.stack([right_keep, right_send], 1))
        cut = 8 * per
        down_grad = scatter_any(core, down).T
        up_grad = scatter_any(core, up[:, :cut])
        out_grad = scatter_any(core, up[:, cut:])
        qkv_grad = scatter_any(core, jnp.concatenate([left, right], 1))
    got = lax.all_to_all(packed, ("batch", "head"), split_axis=0, concat_axis=0, tiled=True)
    small = jnp.sum(got, 0)
    bias_at, two_at, up_at = passes + 2, passes + 5, passes + 9
    return (
        result,
        input_grad,
        small[:passes],
        small[passes],
        small[passes + 1],
        qkv_grad.T,
        jnp.stack([small[bias_at], small[bias_at + 2]]),
        out_grad.T,
        small[two_at + 2],
        small[two_at],
        small[two_at + 1],
        up_grad.T,
        small[up_at:].reshape(-1),
        down_grad,
        small[two_at + 3],
    )


def solution(mesh):
    both = ("batch", "head")
    copied = P()
    in_specs = (P(both, None), P(both), P("batch", None)) + (copied,) * 13 + (P(both, None),)
    out_specs = (
        P(both, None),
        P(both, None),
        P(None, both),
        P(both),
        P(both),
        P(None, both),
        P(None, both),
        P(None, both),
        P(both),
        P(both),
        P(both),
        P(None, both),
        P(both),
        P(None, both),
        P(both),
    )
    return jax.shard_map(
        on_device, mesh=mesh, in_specs=in_specs, out_specs=out_specs, check_vma=False
    )
```

```python
import jax
import jax.numpy as jnp
from jax import lax
from jax.experimental import pallas as pl
from jax.experimental.pallas import tpu as pltpu
from jax.sharding import PartitionSpec as P

HEAD_DIM = 64
SEQ_LEN = 1280
PAIR = 2 * HEAD_DIM
BQ = 256
BK = 128
BLOCKS = 8
SUB = 256
NEG = -1e30
F32 = jnp.float32
BF16 = jnp.bfloat16
VMEM_LIMIT = 24 * 1024 * 1024


def dot(left, right):
    return lax.dot_general(left, right, (((1,), (0,)), ((), ())), preferred_element_type=F32)


def dot_nt(left, right):
    return lax.dot_general(left, right, (((1,), (1,)), ((), ())), preferred_element_type=F32)


def center_and_scale(values):
    center = values - jnp.mean(values, -1, keepdims=True)
    spread = jnp.mean(center * center, -1, keepdims=True)
    scale = lax.rsqrt(spread + 1e-05)
    return center * scale, scale


def dot_tn(left, right):
    return lax.dot_general(left, right, (((0,), (0,)), ((), ())), preferred_element_type=F32)


def pass_rows(ids_ref, passes):
    ids = ids_ref[...].reshape(1, -1)
    row = lax.broadcasted_iota(jnp.int32, (passes, ids.shape[1]), 0)
    return (row == ids).astype(F32).astype(BF16)


def embed_tokens(tok_ref, ids_ref, emb_ref):
    return tok_ref[...].astype(F32) + dot_tn(pass_rows(ids_ref, emb_ref.shape[0]), emb_ref[...])


def wide(item):
    values = item[...].astype(F32)
    return values if values.ndim == 2 else values.reshape(1, -1)


def half_lanes(core, half):
    return pl.ds(pl.multiple_of(core * half, 128), half)


def whole(shape):
    return pl.BlockSpec(shape, lambda *_: (0,) * len(shape))


def carry(operands, outs, carried):
    return {1 + operands + at: outs + at for at in range(len(carried))}


def shapes(items):
    return [jax.ShapeDtypeStruct(item.shape, item.dtype) for item in items]


def params():
    return pltpu.CompilerParams(vmem_limit_bytes=VMEM_LIMIT)


def cost():
    return pl.CostEstimate(flops=1000, transcendentals=0, bytes_accessed=1000)


ANY = pl.BlockSpec(memory_space=pl.ANY)


def third_bias(bias):
    third = pl.program_id(0)
    rows = bias[...].astype(F32)
    return jnp.where(third == 0, rows[0:1], jnp.where(third == 2, rows[1:2], 0.0))


def qkv_send_kernel(pos, tok, ids, emb, gain, shift, weight, bias, normed_out, half_out, out):
    @pl.when(pl.program_id(0) == 0)
    def _():
        scaled, _ = center_and_scale(embed_tokens(tok, ids, emb))
        normed_out[...] = (scaled * wide(gain) + wide(shift)).astype(BF16)
        half_out[...] = normed_out[:, half_lanes(1 - pos[0], half_out.shape[1])]

    out[0] = (dot(normed_out[...], weight[...]) + third_bias(bias)).astype(BF16)


def qkv_keep_kernel(pos, normed, weight, bias, out):
    out[0] = (dot(normed[...], weight[...]) + third_bias(bias)).astype(BF16)


def qkv_send(pos, tok, ids, emb, gain, shift, weight, bias):
    rows, width = tok.shape
    half = width // 2
    return pl.pallas_call(
        qkv_send_kernel,
        grid_spec=pltpu.PrefetchScalarGridSpec(
            num_scalar_prefetch=1,
            grid=(3,),
            in_specs=[
                whole(tok.shape),
                whole(ids.shape),
                whole(emb.shape),
                whole(gain.shape),
                whole(shift.shape),
                pl.BlockSpec((width, half), lambda t, s: (0, 2 * t + 1 - s[0])),
                pl.BlockSpec((2, half), lambda t, s: (0, 1 - s[0])),
            ],
            out_specs=[
                whole(tok.shape),
                whole((rows, half)),
                pl.BlockSpec((1, rows, half), lambda t, s: (t, 0, 0)),
            ],
        ),
        out_shape=[
            jax.ShapeDtypeStruct(tok.shape, BF16),
            jax.ShapeDtypeStruct((rows, half), BF16),
            jax.ShapeDtypeStruct((3, rows, half), BF16),
        ],
        compiler_params=params(),
        cost_estimate=cost(),
        name="qkv_send",
    )(pos, tok, ids, emb, gain, shift, weight, bias)


def qkv_keep(pos, normed, weight, bias):
    rows, width = normed.shape
    half = width // 2
    return pl.pallas_call(
        qkv_keep_kernel,
        grid_spec=pltpu.PrefetchScalarGridSpec(
            num_scalar_prefetch=1,
            grid=(3,),
            in_specs=[
                whole(normed.shape),
                pl.BlockSpec((width, half), lambda t, s: (0, 2 * t + s[0])),
                pl.BlockSpec((2, half), lambda t, s: (0, s[0])),
            ],
            out_specs=pl.BlockSpec((1, rows, half), lambda t, s: (t, 0, 0)),
        ),
        out_shape=jax.ShapeDtypeStruct((3, rows, half), BF16),
        compiler_params=params(),
        cost_estimate=cost(),
        name="qkv_keep",
    )(pos, normed, weight, bias)


def lane_masks():
    lane = lax.broadcasted_iota(jnp.int32, (1, PAIR), 1)
    first = (lane < HEAD_DIM).astype(F32).astype(BF16)
    return first, (1 - first).astype(BF16)


def row_split(values):
    row = lax.broadcasted_iota(jnp.int32, values.shape, 0)
    keep = row < HEAD_DIM
    wide = values.astype(F32)
    return jnp.concatenate(
        [jnp.where(keep, wide, 0.0).astype(BF16), jnp.where(keep, 0.0, wide).astype(BF16)], axis=1
    )


def gather_rows(mine, other, target, sems, core, rows):
    own = pl.ds(pl.multiple_of(core * rows, 128), rows)
    far = pl.ds(pl.multiple_of((1 - core) * rows, 128), rows)
    if len(mine.shape) == 3:
        return (
            pltpu.make_async_copy(mine, target.at[:, own, :], sems.at[0]),
            pltpu.make_async_copy(other, target.at[:, far, :], sems.at[1]),
        )
    return (
        pltpu.make_async_copy(mine, target.at[own, :], sems.at[0]),
        pltpu.make_async_copy(other, target.at[far, :], sems.at[1]),
    )


def segment_firsts(seg_ref, x):
    row = seg_ref[pl.ds(x, 1), :]
    return [jnp.sum((row < number).astype(F32)).astype(jnp.int32) for number in (1, 2, 3)]


def fill_starts(firsts, start):
    at = lax.broadcasted_iota(jnp.int32, start.shape, 1)
    own = jnp.zeros(start.shape, jnp.int32)
    for first in firsts:
        own = jnp.where(at >= first, first, own)
    start[...] = own


def first_block(firsts, q0):
    own = jnp.int32(0)
    for first in firsts:
        own = jnp.where(first <= q0, first, own)
    return own // BK


def valid_keys(start, q0, kb):
    key_at = lax.broadcasted_iota(jnp.int32, (BK, BQ), 0) + kb * BK
    query_at = lax.broadcasted_iota(jnp.int32, (BK, BQ), 1) + q0
    inside = (key_at >= start) & (key_at <= query_at)
    return jnp.concatenate([inside, inside], axis=1)


def attend_kernel(pos, seg, keep, recv, *rest, ties):
    own_out, far_out, lse_out, qkv, qq, vm, sc, acc, joined, start_ref, sems = rest[ties:]
    core = pos[0]
    rows = own_out.shape[0]
    pairs = own_out.shape[1] // PAIR
    copies = gather_rows(keep, recv, qkv, sems, core, rows)
    for item in copies:
        item.start()
    firsts = segment_firsts(seg, pos[4])
    fill_starts(firsts, start_ref)
    for item in copies:
        item.wait()
    first, second = lane_masks()

    def prepare(kb, _):
        at = pl.ds(pl.multiple_of(kb * BK, BK), BK)
        for p in range(pairs):
            vm[kb, p] = row_split(qkv[2, at, p * PAIR : (p + 1) * PAIR].T)
        return 0

    lax.fori_loop(0, SEQ_LEN // BK, prepare, 0)

    def one_block(qi, _):
        q0 = pl.multiple_of(qi * BQ, BQ)
        at = pl.ds(q0, BQ)
        start = start_ref[:, at]
        low = first_block(firsts, q0)
        high = (qi + 1) * (BQ // BK)
        for p in range(pairs):
            q = qkv[0, at, p * PAIR : (p + 1) * PAIR] * jnp.asarray(0.125, BF16)
            qq[p, :BQ] = q * first
            qq[p, BQ:] = q * second
            acc[p] = jnp.zeros((PAIR, BQ), F32)

        def scores(kb, tops):
            inside = valid_keys(start, q0, kb)
            rows_at = pl.ds(pl.multiple_of(kb * BK, BK), BK)
            grown = []
            for p in range(pairs):
                s = dot_nt(qkv[1, rows_at, p * PAIR : (p + 1) * PAIR], qq[p])
                s = jnp.where(inside, s, NEG)
                sc[kb - low, p] = s
                grown.append(jnp.maximum(tops[p], jnp.max(s, axis=0, keepdims=True)))
            return tuple(grown)

        tops = lax.fori_loop(
            low, high, scores, tuple(jnp.full((1, 2 * BQ), NEG, F32) for _ in range(pairs))
        )

        def weigh(kb, sums):
            grown = []
            for p in range(pairs):
                raw = jnp.exp(sc[kb - low, p] - tops[p])
                grown.append(sums[p] + jnp.sum(raw, axis=0, keepdims=True))
                raw = raw.astype(BF16)
                acc[p] += dot(vm[kb, p], jnp.concatenate([raw[:, :BQ], raw[:, BQ:]], axis=0))
            return tuple(grown)

        sums = lax.fori_loop(
            low, high, weigh, tuple(jnp.zeros((1, 2 * BQ), F32) for _ in range(pairs))
        )
        for p in range(pairs):
            inv = 1.0 / sums[p]
            out = jnp.concatenate(
                [acc[p, :HEAD_DIM] * inv[:, :BQ], acc[p, HEAD_DIM:] * inv[:, BQ:]], axis=0
            )
            joined[at, p * PAIR : (p + 1) * PAIR] = out.T.astype(BF16)
            lse_out[qi, p] = tops[p] + jnp.log(sums[p])
        return 0

    lax.fori_loop(0, SEQ_LEN // BQ, one_block, 0)
    own_out[...] = joined[pl.ds(pl.multiple_of(core * rows, 128), rows), :]
    far_out[...] = joined[pl.ds(pl.multiple_of((1 - core) * rows, 128), rows), :]


def attend(pos, ties, seg, keep, recv):
    _, rows, half = keep.shape
    pairs = half // PAIR
    window = SEQ_LEN // BK

    def kernel(*refs):
        attend_kernel(*refs, ties=len(ties))

    return pl.pallas_call(
        kernel,
        grid_spec=pltpu.PrefetchScalarGridSpec(
            num_scalar_prefetch=1,
            grid=(1,),
            in_specs=[whole(seg.shape)] + [ANY] * (2 + len(ties)),
            out_specs=[
                whole((rows, half)),
                whole((rows, half)),
                whole((SEQ_LEN // BQ, pairs, 1, 2 * BQ)),
            ],
            scratch_shapes=[
                pltpu.VMEM((3, SEQ_LEN, half), BF16),
                pltpu.VMEM((pairs, 2 * BQ, PAIR), BF16),
                pltpu.VMEM((SEQ_LEN // BK, pairs, PAIR, 2 * BK), BF16),
                pltpu.VMEM((window, pairs, BK, 2 * BQ), F32),
                pltpu.VMEM((pairs, PAIR, BQ), F32),
                pltpu.VMEM((SEQ_LEN, half), BF16),
                pltpu.VMEM((1, SEQ_LEN), jnp.int32),
                pltpu.SemaphoreType.DMA((2,)),
            ],
        ),
        out_shape=[
            jax.ShapeDtypeStruct((rows, half), BF16),
            jax.ShapeDtypeStruct((rows, half), BF16),
            jax.ShapeDtypeStruct((SEQ_LEN // BQ, pairs, 1, 2 * BQ), F32),
        ],
        compiler_params=params(),
        cost_estimate=cost(),
        name="attend",
    )(pos, seg, keep, recv, *ties)


def attend_back_kernel(
    pos, seg, lse_ref, keep, recv, own, far, grad_own, grad_far, *rest, ties
):
    keep_out, send_out, qkv, att, dout, qq, dd, km, delta, dq_t, dq, dk, dv, start_ref, sems = rest[ties:]
    core = pos[0]
    rows, half = own.shape
    pairs = half // PAIR
    copies = (
        gather_rows(keep, recv, qkv, sems.at[0], core, rows)
        + gather_rows(own, far, att, sems.at[1], core, rows)
        + gather_rows(grad_own, grad_far, dout, sems.at[2], core, rows)
    )
    for item in copies:
        item.start()
    firsts = segment_firsts(seg, pos[4])
    fill_starts(firsts, start_ref)
    dk[...] = jnp.zeros_like(dk)
    dv[...] = jnp.zeros_like(dv)
    for item in copies:
        item.wait()
    first, second = lane_masks()

    def prepare(kb, _):
        at = pl.ds(pl.multiple_of(kb * BK, BK), BK)
        for p in range(pairs):
            km[kb, p] = row_split(qkv[1, at, p * PAIR : (p + 1) * PAIR].T)
        return 0

    lax.fori_loop(0, SEQ_LEN // BK, prepare, 0)

    def one_block(qi, _):
        q0 = pl.multiple_of(qi * BQ, BQ)
        at = pl.ds(q0, BQ)
        start = start_ref[:, at]
        low = first_block(firsts, q0)
        high = (qi + 1) * (BQ // BK)
        for p in range(pairs):
            lanes = slice(p * PAIR, (p + 1) * PAIR)
            q = qkv[0, at, lanes] * jnp.asarray(0.125, BF16)
            qq[p, :BQ] = q * first
            qq[p, BQ:] = q * second
            g = dout[at, lanes]
            dd[p, :BQ] = g * first
            dd[p, BQ:] = g * second
            both = (g.astype(F32) * att[at, lanes].astype(F32)).T
            delta[p] = jnp.concatenate(
                [
                    jnp.sum(both[:HEAD_DIM], axis=0, keepdims=True),
                    jnp.sum(both[HEAD_DIM:], axis=0, keepdims=True),
                ],
                axis=1,
            )
            dq_t[p] = jnp.zeros((PAIR, BQ), F32)

        def step(kb, _):
            inside = valid_keys(start, q0, kb)
            rows_at = pl.ds(pl.multiple_of(kb * BK, BK), BK)
            for p in range(pairs):
                lanes = slice(p * PAIR, (p + 1) * PAIR)
                s = dot_nt(qkv[1, rows_at, lanes], qq[p])
                prob = jnp.where(inside, jnp.exp(s - lse_ref[qi, p]), 0.0)
                grad_prob = dot_nt(qkv[2, rows_at, lanes], dd[p])
                grad_s = (prob * (grad_prob - delta[p])).astype(BF16)
                dv[rows_at, lanes] += dot(prob.astype(BF16), dd[p])
                dk[rows_at, lanes] += dot(grad_s, qq[p])
                dq_t[p] += dot(km[kb, p], jnp.concatenate([grad_s[:, :BQ], grad_s[:, BQ:]], axis=0))
            return 0

        lax.fori_loop(low, high, step, 0)
        for p in range(pairs):
            dq[p * PAIR : (p + 1) * PAIR, at] = (dq_t[p] * 0.125).astype(BF16)
        return 0

    lax.fori_loop(0, SEQ_LEN // BQ, one_block, 0)
    for target, at in ((keep_out, core), (send_out, 1 - core)):
        tokens = pl.ds(pl.multiple_of(at * rows, 128), rows)
        target[0] = dq[:, tokens]
        target[1] = dk[tokens, :].astype(BF16).T
        target[2] = dv[tokens, :].astype(BF16).T


def attend_back(ties, pos, seg, lse, keep, recv, own, far, grad_own, grad_far):
    _, rows, half = keep.shape
    pairs = half // PAIR
    out = (3, half, rows)

    def kernel(*refs):
        attend_back_kernel(*refs, ties=len(ties))

    return pl.pallas_call(
        kernel,
        grid_spec=pltpu.PrefetchScalarGridSpec(
            num_scalar_prefetch=1,
            grid=(1,),
            in_specs=[whole(seg.shape), whole(lse.shape)] + [ANY] * (6 + len(ties)),
            out_specs=[whole(out), whole(out)],
            scratch_shapes=[
                pltpu.VMEM((3, SEQ_LEN, half), BF16),
                pltpu.VMEM((SEQ_LEN, half), BF16),
                pltpu.VMEM((SEQ_LEN, half), BF16),
                pltpu.VMEM((pairs, 2 * BQ, PAIR), BF16),
                pltpu.VMEM((pairs, 2 * BQ, PAIR), BF16),
                pltpu.VMEM((SEQ_LEN // BK, pairs, PAIR, 2 * BK), BF16),
                pltpu.VMEM((pairs, 1, 2 * BQ), F32),
                pltpu.VMEM((pairs, PAIR, BQ), F32),
                pltpu.VMEM((half, SEQ_LEN), BF16),
                pltpu.VMEM((SEQ_LEN, half), F32),
                pltpu.VMEM((SEQ_LEN, half), F32),
                pltpu.VMEM((1, SEQ_LEN), jnp.int32),
                pltpu.SemaphoreType.DMA((3, 2)),
            ],
        ),
        out_shape=[jax.ShapeDtypeStruct(out, BF16)] * 2,
        compiler_params=params(),
        cost_estimate=cost(),
        name="attend_back",
    )(pos, seg, lse, keep, recv, own, far, grad_own, grad_far, *ties)


def gather_lanes(core, own, far, target):
    half = own.shape[1]
    target[:, half_lanes(core, half)] = own[...]
    target[:, half_lanes(1 - core, half)] = far[...]


def hidden_block(i, core):
    late = i >> 1
    return 2 * (late * core + (1 - late) * (1 - core)) + (i & 1)


def early(i):
    return jnp.minimum(i, 1)


def late(i):
    return jnp.maximum(i - 2, 0)


def ff_first_kernel(
    pos, tok, ids, emb, own, far, weight, bias, gain, shift, cot, up, up_bias, down,
    after_out, normed_out, half_out, act_own, act_send, grad_out, bias_grad, attended, act,
):
    step = pl.program_id(0)

    @pl.when(step == 0)
    def _():
        gather_lanes(pos[0], own, far, attended)
        after = embed_tokens(tok, ids, emb) + dot(attended[...], weight[...]) + wide(bias)
        after_out[...] = after
        scaled, _ = center_and_scale(after)
        normed_out[...] = (scaled * wide(gain) + wide(shift)).astype(BF16)
        half_out[...] = normed_out[:, half_lanes(1 - pos[0], half_out.shape[1])]

    for part in range(up.shape[1] // SUB):
        cols = slice(part * SUB, (part + 1) * SUB)
        u = dot(normed_out[...], up[:, cols]) + up_bias[:, cols].astype(F32)
        grad_act = dot_nt(cot[...], down[cols, :])
        square = u * u
        t = jnp.tanh(0.7978845608028654 * u * (1.0 + 0.044715 * square))
        half = 0.5 * (1.0 + t)
        act[:, cols] = (u * half).astype(BF16)
        slope = half + 0.5 * u * (1.0 - t * t) * (0.7978845608028654 * (1.0 + 0.134145 * square))
        grad = (grad_act * slope).astype(BF16)
        grad_out[:, cols] = grad
        bias_grad[:, cols] = jnp.sum(grad.astype(F32), axis=0, keepdims=True)

    @pl.when(step < 2)
    def _():
        act_send[...] = act[...]

    @pl.when(step >= 2)
    def _():
        act_own[...] = act[...]


def ff_first(pos, tok, ids, emb, own, far, weight, bias, gain, shift, cot, up, up_bias, down):
    rows, width = tok.shape
    hidden = up.shape[1]
    first = (tok, ids, emb, own, far, weight, bias, gain, shift, cot)
    shape = jax.ShapeDtypeStruct
    return pl.pallas_call(
        ff_first_kernel,
        grid_spec=pltpu.PrefetchScalarGridSpec(
            num_scalar_prefetch=1,
            grid=(4,),
            in_specs=[whole(item.shape) for item in first]
            + [
                pl.BlockSpec((width, width), lambda i, s: (0, hidden_block(i, s[0]))),
                pl.BlockSpec((1, width), lambda i, s: (0, hidden_block(i, s[0]))),
                pl.BlockSpec((width, width), lambda i, s: (hidden_block(i, s[0]), 0)),
            ],
            out_specs=[
                whole((rows, width)),
                whole((rows, width)),
                whole((rows, width // 2)),
                pl.BlockSpec((rows, width), lambda i, s: (0, late(i))),
                pl.BlockSpec((rows, width), lambda i, s: (0, early(i))),
                pl.BlockSpec((rows, width), lambda i, s: (0, hidden_block(i, s[0]))),
                pl.BlockSpec((1, width), lambda i, s: (0, hidden_block(i, s[0]))),
            ],
            scratch_shapes=[pltpu.VMEM((rows, width), BF16), pltpu.VMEM((rows, width), BF16)],
        ),
        out_shape=[
            shape((rows, width), F32),
            shape((rows, width), BF16),
            shape((rows, width // 2), BF16),
            shape((rows, hidden // 2), BF16),
            shape((rows, hidden // 2), BF16),
            shape((rows, hidden), BF16),
            shape((1, hidden), F32),
        ],
        compiler_params=params(),
        cost_estimate=cost(),
        name="ff_first",
    )(pos, *first, up, up_bias, down)


def ff_back_kernel(
    pos, grad_pre, up, after, cot, gain, weight,
    grad_after, branch_out, own_out, far_out, sums, total,
):
    step = pl.program_id(0)
    part = dot_nt(grad_pre[...], up[...])

    @pl.when(step == 0)
    def _():
        total[...] = part

    @pl.when(step > 0)
    def _():
        total[...] += part

    @pl.when(step == pl.num_programs(0) - 1)
    def _():
        core = pos[0]
        half = own_out.shape[1]
        scaled, scale = center_and_scale(after[...])
        grad = total[...]
        inner = grad * wide(gain)
        shift = jnp.mean(inner, -1, keepdims=True)
        slope = jnp.mean(inner * scaled, -1, keepdims=True)
        cot_f32 = wide(cot)
        result = cot_f32 + scale * (inner - shift - scaled * slope)
        grad_after[...] = result
        branch_out[...] = result.astype(BF16)
        branch = branch_out[...]
        for target, at in ((far_out, 1 - core), (own_out, core)):
            rows = pl.ds(pl.multiple_of(at * half, 128), half)
            target[...] = dot_nt(branch, weight[rows, :]).astype(BF16)
        sums[0:1] = jnp.sum(grad * scaled, axis=0, keepdims=True)
        sums[1:2] = jnp.sum(grad, axis=0, keepdims=True)
        sums[2:3] = jnp.sum(branch.astype(F32), axis=0, keepdims=True)
        sums[3:4] = jnp.sum(cot_f32, axis=0, keepdims=True)


def ff_back(pos, grad_pre, up, after, cot, gain, weight):
    rows, width = after.shape
    half = width // 2
    last = (after, cot, gain, weight)
    outs = [
        jax.ShapeDtypeStruct((rows, width), F32),
        jax.ShapeDtypeStruct((rows, width), BF16),
        jax.ShapeDtypeStruct((rows, half), BF16),
        jax.ShapeDtypeStruct((rows, half), BF16),
        jax.ShapeDtypeStruct((4, width), F32),
    ]
    return pl.pallas_call(
        ff_back_kernel,
        grid_spec=pltpu.PrefetchScalarGridSpec(
            num_scalar_prefetch=1,
            grid=(grad_pre.shape[1] // width,),
            in_specs=[
                pl.BlockSpec((rows, width), lambda i, s: (0, i)),
                pl.BlockSpec((width, width), lambda i, s: (0, i)),
            ]
            + [whole(item.shape) for item in last],
            out_specs=[whole(item.shape) for item in outs],
            scratch_shapes=[pltpu.VMEM((rows, width), F32)],
        ),
        out_shape=outs,
        compiler_params=params(),
        cost_estimate=cost(),
        name="ff_back",
    )(pos, grad_pre, up, *last)


def z_place(z):
    return (z & 1) * 2 + (z >> 1)


def chips():
    return [(x, y, z) for x in range(2) for y in range(2) for z in range(4)]


def chip_row(pos, x, y, z):
    return ((2 * z_place(z) + y) ^ pos[3]) * 2 + (x ^ pos[2])


def rows_of(values, chip, per, at=0, count=None):
    count = per if count is None else count
    return values[pl.ds(pl.multiple_of(chip * per + at, 8), count), :].astype(BF16)


def middle_weights_kernel(
    pos, act, act_far, grad, grad_far, cot, cot_far, normed, normed_far, *rest, ties
):
    left_keep, left_send, right_keep, right_send, rows_f32 = rest[ties:]
    step = pl.program_id(0)
    half = normed_far.shape[1]
    left, right = (left_keep, left_send), (right_keep, right_send)

    @pl.when(step < 2)
    def _():
        per = rows_f32.shape[0] // 16
        for part in range(2):
            cols = slice(part * half, (part + 1) * half)
            rows_f32[...] = dot_tn(cot[...], act[:, cols]) + dot_tn(cot_far[...], act_far[:, cols])
            for x, y, z in chips():
                left[x][y, z, part * per : (part + 1) * per, :] = rows_of(
                    rows_f32, chip_row(pos, x, y, z), per
                )

    @pl.when(step >= 2)
    def _():
        per = rows_f32.shape[0] // 4
        own = normed[:, half_lanes(pos[0], half)]
        rows_f32[...] = dot_tn(grad[...], own) + dot_tn(grad_far[...], normed_far[...])
        for x in range(2):
            for y in range(2):
                chip = (y ^ (pos[3] & 1)) * 2 + (x ^ pos[2])
                right[y][x, 0, :per, :] = rows_of(rows_f32, chip, per)


def middle_weights(pos, ties, act, act_far, grad, grad_far, cot, cot_far, normed, normed_far):
    rows, width = normed.shape
    half = width // 2
    per = width // 16
    left = jax.ShapeDtypeStruct((2, 4, 4 * per, half), BF16)
    right = jax.ShapeDtypeStruct((2, 4, 5 * per, half), BF16)
    fixed = (cot, cot_far, normed, normed_far)

    def kernel(*refs):
        middle_weights_kernel(*refs, ties=len(ties))

    def left_at(i, s):
        return 0, 0, early(i), 0

    def right_at(i, s):
        return 0, z_place(late(i) ^ (s[3] >> 1)), 0, 0

    return pl.pallas_call(
        kernel,
        grid_spec=pltpu.PrefetchScalarGridSpec(
            num_scalar_prefetch=1,
            grid=(6,),
            in_specs=[pl.BlockSpec((rows, width), lambda i, s: (0, early(i)))] * 2
            + [pl.BlockSpec((rows, width), lambda i, s: (0, late(i)))] * 2
            + [whole(item.shape) for item in fixed]
            + [ANY] * len(ties),
            out_specs=[pl.BlockSpec((2, 4, 2 * per, half), left_at)] * 2
            + [pl.BlockSpec((2, 1, 4 * per, half), right_at)] * 2,
            scratch_shapes=[pltpu.VMEM((width, half), F32)],
        ),
        out_shape=[left, left, right, right],
        compiler_params=params(),
        cost_estimate=cost(),
        name="middle_weights",
    )(pos, act, act_far, grad, grad_far, *fixed, *ties)


def out_weight_kernel(pos, branch, branch_far, own, far, keep_in, send_in, tie, keep_out, send_out, rows_f32):
    per = rows_f32.shape[0] // 16
    rows_f32[...] = dot_tn(branch[...], own[...]) + dot_tn(branch_far[...], far[...])
    for x, y, z in chips():
        (keep_out, send_out)[y][x, z] = rows_of(rows_f32, chip_row(pos, x, y, z), per)


def out_weight_call(pos, tie, branch, branch_far, own, far, keep, send):
    rows, width = branch.shape
    half = width // 2
    block = pl.BlockSpec((2, 4, width // 16, half), lambda i, s: (0, 0, 4, 0))
    return pl.pallas_call(
        out_weight_kernel,
        grid_spec=pltpu.PrefetchScalarGridSpec(
            num_scalar_prefetch=1,
            grid=(1,),
            in_specs=[whole(branch.shape)] * 2 + [whole(own.shape)] * 2 + [ANY] * 3,
            out_specs=[block, block],
            scratch_shapes=[pltpu.VMEM((width, half), F32)],
        ),
        out_shape=[jax.ShapeDtypeStruct(keep.shape, BF16)] * 2,
        input_output_aliases={5: 0, 6: 1},
        compiler_params=params(),
        cost_estimate=cost(),
        name="out_weight",
    )(pos, branch, branch_far, own, far, keep, send, tie)


def pack_sums(tables, long, packed):
    count, _, share = packed.shape
    for device in range(count):
        low = 0
        for table in tables:
            rows = table.shape[0]
            packed[device, low : low + rows, :] = table[:, device * share : (device + 1) * share]
            low += rows
        for part in range(4):
            at = (4 * device + part) * share
            packed[device, low + part : low + part + 1, :] = long[:, at : at + share]


def mixed_kernel(pos, act_send, act_own, down, after, bias, one, two, three, four, *rest, ties, carried):
    out, packed = rest[ties + carried : ties + carried + 2]
    total = rest[-1]
    step = pl.program_id(0)

    @pl.when(step == 0)
    def _():
        total[...] = after[...] + wide(bias)

    @pl.when(step < 2)
    def _():
        total[...] += dot(act_send[...], down[...])

    @pl.when(step >= 2)
    def _():
        total[...] += dot(act_own[...], down[...])

    @pl.when(step == pl.num_programs(0) - 1)
    def _():
        out[...] = total[...].astype(BF16)
        pack_sums((one, two, three), four, packed)


def mixed_call(pos, ties, carried, act_send, act_own, down, after, bias, *sums):
    rows, width = after.shape
    devices = lax.axis_size("batch") * lax.axis_size("head")
    packed = (devices, sum(item.shape[0] for item in sums[:3]) + 4, width // devices)

    def kernel(*refs):
        mixed_kernel(*refs, ties=len(ties), carried=len(carried))

    return pl.pallas_call(
        kernel,
        grid_spec=pltpu.PrefetchScalarGridSpec(
            num_scalar_prefetch=1,
            grid=(4,),
            in_specs=[
                pl.BlockSpec((rows, width), lambda i, s: (0, early(i))),
                pl.BlockSpec((rows, width), lambda i, s: (0, late(i))),
                pl.BlockSpec((width, width), lambda i, s: (hidden_block(i, s[0]), 0)),
                whole(after.shape),
                whole(bias.shape),
            ]
            + [whole(item.shape) for item in sums]
            + [ANY] * (len(ties) + len(carried)),
            out_specs=[whole((rows, width)), whole(packed)] + [ANY] * len(carried),
            scratch_shapes=[pltpu.VMEM((rows, width), F32)],
        ),
        out_shape=[jax.ShapeDtypeStruct((rows, width), BF16), jax.ShapeDtypeStruct(packed, F32)]
        + shapes(carried),
        input_output_aliases=carry(5 + len(sums) + len(ties), 2, carried),
        compiler_params=params(),
        cost_estimate=cost(),
        name="mixed",
    )(pos, act_send, act_own, down, after, bias, *sums, *ties, *carried)


def qkv_weight_kernel(
    pos, mine, mine_far, other, other_far, normed, normed_far, *rest, ties
):
    left_keep, left_send, right_keep, right_send, sums, rows_f32 = rest[ties:]
    core = pos[0]
    half = normed_far.shape[1]
    third = pl.program_id(0)
    own = normed[:, half_lanes(core, half)]
    ones = jnp.ones((8, own.shape[0]), BF16)

    @pl.when(third == 0)
    def _():
        sums[...] = jnp.zeros_like(sums)

    for near, far, at in ((mine, mine_far, core), (other, other_far, 1 - core)):
        rows = pl.ds(pl.multiple_of((2 * third + at) * half, 128), half)
        rows_f32[rows, :] = dot(near[0], own) + dot(far[0], normed_far[...])
    row = (dot_nt(ones, mine[0]) + dot_nt(ones, mine_far[0]))[:1]
    lanes = half_lanes(core, half)
    for t in range(3):
        sums[t : t + 1, lanes] += jnp.where(third == t, row, 0.0)

    @pl.when(third == pl.num_programs(0) - 1)
    def _():
        per = rows_f32.shape[0] // 32
        for x, y, z in chips():
            chip = chip_row(pos, x, y, z)
            (left_keep, left_send)[x][y, z] = rows_of(rows_f32, chip, 2 * per, 0, per)
            (right_keep, right_send)[y][x, z] = rows_of(rows_f32, chip, 2 * per, per, per)


def qkv_weight_call(pos, ties, mine, mine_far, other, other_far, normed, normed_far):
    rows, width = normed.shape
    half = width // 2
    third = pl.BlockSpec((1, half, rows), lambda t, s: (t, 0, 0))
    out = jax.ShapeDtypeStruct((2, 4, 3 * width // 32, half), BF16)

    def kernel(*refs):
        qkv_weight_kernel(*refs, ties=len(ties))

    return pl.pallas_call(
        kernel,
        grid_spec=pltpu.PrefetchScalarGridSpec(
            num_scalar_prefetch=1,
            grid=(3,),
            in_specs=[third] * 4 + [whole(normed.shape), whole(normed_far.shape)] + [ANY] * len(ties),
            out_specs=[whole(out.shape)] * 4 + [whole((3, width))],
            scratch_shapes=[pltpu.VMEM((3 * width, half), F32)],
        ),
        out_shape=[out] * 4 + [jax.ShapeDtypeStruct((3, width), F32)],
        compiler_params=params(),
        cost_estimate=cost(),
        name="qkv_weight",
    )(pos, mine, mine_far, other, other_far, normed, normed_far, *ties)


def input_back_kernel(pos, mine, other, weight, tok, ids, emb, gain, grad_after, *rest, ties, carried):
    out, sums = rest[ties + carried : ties + carried + 2]
    joined, total = rest[-2:]
    core = pos[0]
    step = pl.program_id(0)
    half = mine.shape[1]
    joined[half_lanes(core, half), :] = mine[0]
    joined[half_lanes(1 - core, half), :] = other[0]
    part = lax.dot_general(
        joined[...], weight[...], (((0,), (1,)), ((), ())), preferred_element_type=F32
    )

    @pl.when(step == 0)
    def _():
        total[...] = part

    @pl.when(step > 0)
    def _():
        total[...] += part

    @pl.when(step == pl.num_programs(0) - 1)
    def _():
        grad = total[...]
        scaled, scale = center_and_scale(embed_tokens(tok, ids, emb))
        inner = grad * wide(gain)
        shift = jnp.mean(inner, -1, keepdims=True)
        slope = jnp.mean(inner * scaled, -1, keepdims=True)
        result = grad_after[...] + scale * (inner - shift - scaled * slope)
        out[...] = result
        passes = emb.shape[0]
        chosen = pass_rows(ids, passes)
        high = result.astype(BF16)
        less = result - high.astype(F32)
        middle = less.astype(BF16)
        least = (less - middle.astype(F32)).astype(BF16)
        sums[0:passes] = dot(chosen, high) + (dot(chosen, middle) + dot(chosen, least))
        sums[passes : passes + 1] = jnp.sum(grad * scaled, axis=0, keepdims=True)
        sums[passes + 1 : passes + 2] = jnp.sum(grad, axis=0, keepdims=True)


def input_back(pos, ties, carried, mine, other, weight, tok, ids, emb, gain, grad_after):
    rows, width = tok.shape
    third = pl.BlockSpec((1, width // 2, rows), lambda t, s: (t, 0, 0))
    fixed = (tok, ids, emb, gain, grad_after)
    outs = [
        jax.ShapeDtypeStruct((rows, width), F32),
        jax.ShapeDtypeStruct((emb.shape[0] + 2, width), F32),
    ]

    def kernel(*refs):
        input_back_kernel(*refs, ties=len(ties), carried=len(carried))

    return pl.pallas_call(
        kernel,
        grid_spec=pltpu.PrefetchScalarGridSpec(
            num_scalar_prefetch=1,
            grid=(3,),
            in_specs=[third, third, pl.BlockSpec((width, width), lambda t, s: (0, t))]
            + [whole(item.shape) for item in fixed]
            + [ANY] * (len(ties) + len(carried)),
            out_specs=[whole(item.shape) for item in outs] + [ANY] * len(carried),
            scratch_shapes=[pltpu.VMEM((width, rows), BF16), pltpu.VMEM((rows, width), F32)],
        ),
        out_shape=outs + shapes(carried),
        input_output_aliases=carry(3 + len(fixed) + len(ties), len(outs), carried),
        compiler_params=params(),
        cost_estimate=cost(),
        name="input_back",
    )(pos, mine, other, weight, *fixed, *ties, *carried)


def swap_head(values, bit):
    size = lax.axis_size("head")
    return lax.ppermute(values, "head", [(i, i ^ bit) for i in range(size)])


def swap_batch(values, bit):
    size = lax.axis_size("batch")
    return lax.ppermute(values, "batch", [(i, i ^ bit) for i in range(size)])


class Sum:
    def __init__(self, *parts):
        self.parts = parts

    def __getitem__(self, index):
        return Sum(*[part[index] for part in self.parts])

    def wide(self):
        total = self.parts[0].astype(F32)
        for part in self.parts[1:]:
            total = total + part.astype(F32)
        return total

    def sent(self):
        return self.wide().astype(BF16)


def swap_x(values):
    return swap_head(values, 2)


def swap_y(values):
    return swap_batch(values, 1)


def z_step(left, right):
    cut = left.parts[0].shape[0] // 2
    split = left.parts[0].shape[1]
    sent = jnp.concatenate([left[cut:].sent(), right[cut:].sent()], 1)

    def finish():
        got = swap_batch(sent, 2 if cut == 2 else 4)
        return Sum(*left[:cut].parts, got[:, :split]), Sum(*right[:cut].parts, got[:, split:])

    return sent, finish


def chip_sums(core, *items):
    flat = [jnp.where(core == 0, item[..., 1, :, :], item[..., 0, :, :]) for item in items]
    width = flat[0].shape[-1]
    got = swap_head(jnp.concatenate([item.reshape(-1, width) for item in flat], 0), 1)
    out, at = [], 0
    for item, sent in zip(items, flat):
        count = sent.size // width
        far = got[at : at + count].reshape(sent.shape)
        near = jnp.where(core == 0, item[..., 0, :, :], item[..., 1, :, :])
        out.append((jnp.where(core == 0, near, far), jnp.where(core == 0, far, near)))
        at += count
    return out


def scatter_any(core, values):
    half = values.shape[-1]
    rows = values.reshape(-1, half).astype(F32)
    both = lax.dynamic_update_slice(jnp.zeros((rows.shape[0], 2 * half), F32), rows, (0, core * half))
    return lax.psum_scatter(both, ("batch", "head"), scatter_dimension=0, tiled=True)


def by_chip(values):
    rest = values.shape[3:]
    split = values.reshape((2, 2, 2, 2) + rest)
    order = (3, 2, 1, 0) + tuple(range(4, split.ndim))
    return split.transpose(order).reshape((16,) + rest)


def on_device(
    tokens,
    pass_ids,
    segment_ids,
    pass_embed,
    norm1_gain,
    norm1_shift,
    qkv_weight,
    qv_bias,
    out_weight,
    out_bias,
    norm2_gain,
    norm2_shift,
    up_weight,
    up_bias,
    down_weight,
    down_bias,
    cotangent,
):
    rows, width = tokens.shape
    hidden_units = up_weight.shape[1]
    passes = pass_embed.shape[0]
    pairs = width // 2 // PAIR
    assert 2 * rows == SEQ_LEN and lax.axis_size("head") == 4 and hidden_units == 4 * width
    direct = lax.axis_size("batch") == BLOCKS

    head = lax.axis_index("head").astype(jnp.int32)
    batch = lax.axis_index("batch").astype(jnp.int32)
    core, x_bit = head % 2, head // 2
    zero = jnp.zeros((), jnp.int32)
    place = [core, x_bit, batch] if direct else [zero, zero, zero]
    pos = jnp.stack([core] + place + [x_bit])

    row = lambda item: item
    ids = row(pass_ids)
    gain_one, gain_two = row(norm1_gain), row(norm2_gain)
    cot_far = swap_head(cotangent, 1)
    normed, normed_send, send = qkv_send(
        pos, tokens, ids, pass_embed, gain_one, row(norm1_shift), qkv_weight, qv_bias
    )
    recv = swap_head(send, 1)
    normed_far = swap_head(normed_send, 1)
    keep = qkv_keep(pos, normed, qkv_weight, qv_bias)
    own, far_send, lse = attend(pos, (cot_far, normed_far), segment_ids, keep, recv)
    far = swap_head(far_send, 1)
    after, normed_two, normed_two_send, act_own, act_send, grad_pre, up_bias_grad = ff_first(
        pos, tokens, ids, pass_embed, own, far, out_weight, row(out_bias), gain_two, row(norm2_shift),
        cotangent, up_weight, up_bias.reshape(1, -1), down_weight,
    )
    act_far = swap_head(act_send, 1)
    grad_pre_far = swap_head(grad_pre, 1)
    normed_two_far = swap_head(normed_two_send, 1)
    grad_after, branch, grad_own, grad_send, sums_two = ff_back(
        pos, grad_pre, up_weight, after, cotangent, gain_two, out_weight
    )
    grad_far = swap_head(grad_send, 1)
    branch_far = swap_head(branch, 1)
    down_keep, down_send, up_keep, up_send = middle_weights(
        pos, (), act_own, act_far, grad_pre, grad_pre_far, cotangent, cot_far, normed_two, normed_two_far
    )
    up_keep, up_send = out_weight_call(pos, grad_far, branch, branch_far, own, far_send, up_keep, up_send)
    if direct:
        left = Sum(down_keep, swap_x(down_send))
        right = Sum(up_keep, swap_y(up_send))
    mine, mine_send = attend_back(
        (down_send, up_send), pos, segment_ids, lse, keep, recv, own, far_send, grad_own, grad_far
    )
    other = swap_head(mine_send, 1)
    other_far = swap_head(mine, 1)
    ties, carried = (), ()
    if direct:
        left_sent, right_sent = left[1].sent(), right[1].sent()
        ties = (left_sent, right_sent)
    left_keep, left_send, right_keep, right_send, bias_sums = qkv_weight_call(
        pos, ties, mine, mine_send, other, other_far, normed, normed_far
    )
    if direct:
        one_got, two_got = swap_x(left_send), swap_y(right_send)
        left = Sum(*left[0].parts, swap_y(left_sent))
        right = Sum(*right[0].parts, swap_x(right_sent))
        mid_sent, mid_next = z_step(left, right)
        ties, carried = (mid_sent,), (left_keep, right_keep)
    input_grad, sums_one, *carried = input_back(
        pos, ties, carried, mine, other, qkv_weight, tokens, ids, pass_embed, gain_one, grad_after
    )
    if direct:
        one, two = Sum(carried[0], one_got), Sum(carried[1], two_got)
        one_sent, two_sent = one[1].sent(), two[1].sent()
        one_last, two_last = swap_y(one_sent), swap_x(two_sent)
        mid_sent, mid_next = z_step(*mid_next())
        qkv_sent, qkv_next = z_step(Sum(*one[0].parts, one_last), Sum(*two[0].parts, two_last))
        ties = (mid_sent, qkv_sent)
    result, packed, *carried = mixed_call(
        pos, ties, carried, act_send, act_own, down_weight, after, row(down_bias),
        sums_one, bias_sums, sums_two, up_bias_grad,
    )

    per = width // 32
    if direct:
        one, two = qkv_next()
        one = Sum(carried[0][0][:2], *one.parts[1:])
        two = Sum(carried[1][0][:2], *two.parts[1:])
        _, qkv_next = z_step(one, two)
        left, right = [item.wide()[0] for item in mid_next()]
        cut = 8 * per
        down, up, out = chip_sums(
            core,
            left.reshape(4, 2, per, -1),
            right[:cut].reshape(2, 4 * per, -1),
            right[cut:].reshape(2, per, -1),
        )
        (qkv,) = chip_sums(core, jnp.stack([item.wide()[0] for item in qkv_next()]))
        down_grad = jnp.concatenate(down, 0).transpose(0, 2, 1).reshape(hidden_units, -1)
        up_grad, out_grad, qkv_grad = [jnp.concatenate(item, -1) for item in (up, out, qkv)]
    else:
        down = by_chip(jnp.stack([down_keep, down_send])).reshape(16, 4, 2 * per, -1)
        down = down.transpose(0, 2, 1, 3).reshape(16, 2 * per, -1)
        up = by_chip(jnp.stack([up_keep, up_send], 1))
        left = by_chip(jnp.stack([left_keep, left_send]))
        right = by_chip(jnp.stack([right_keep, right_send], 1))
        cut = 8 * per
        down_grad = scatter_any(core, down).T
        up_grad = scatter_any(core, up[:, :cut])
        out_grad = scatter_any(core, up[:, cut:])
        qkv_grad = scatter_any(core, jnp.concatenate([left, right], 1))
    got = lax.all_to_all(packed, ("batch", "head"), split_axis=0, concat_axis=0, tiled=True)
    small = jnp.sum(got, 0)
    bias_at, two_at, up_at = passes + 2, passes + 5, passes + 9
    return (
        result,
        input_grad,
        small[:passes],
        small[passes],
        small[passes + 1],
        qkv_grad.T,
        jnp.stack([small[bias_at], small[bias_at + 2]]),
        out_grad.T,
        small[two_at + 2],
        small[two_at],
        small[two_at + 1],
        up_grad.T,
        small[up_at:].reshape(-1),
        down_grad,
        small[two_at + 3],
    )


def solution(mesh):
    both = ("batch", "head")
    copied = P()
    in_specs = (P(both, None), P(both), P("batch", None)) + (copied,) * 13 + (P(both, None),)
    out_specs = (
        P(both, None),
        P(both, None),
        P(None, both),
        P(both),
        P(both),
        P(None, both),
        P(None, both),
        P(None, both),
        P(both),
        P(both),
        P(both),
        P(None, both),
        P(both),
        P(None, both),
        P(both),
    )
    return jax.shard_map(
        on_device, mesh=mesh, in_specs=in_specs, out_specs=out_specs, check_vma=False
    )
```

```python
import jax
import jax.numpy as jnp
from jax import lax
from jax.experimental import pallas as pl
from jax.experimental.pallas import tpu as pltpu
from jax.sharding import PartitionSpec as P

HEAD_DIM = 64
SEQ_LEN = 1280
PAIR = 2 * HEAD_DIM
BQ = 256
BK = 256
BLOCKS = 8
SUB = 256
NEG = -1e30
F32 = jnp.float32
BF16 = jnp.bfloat16
VMEM_LIMIT = 24 * 1024 * 1024


def dot(left, right):
    return lax.dot_general(left, right, (((1,), (0,)), ((), ())), preferred_element_type=F32)


def dot_nt(left, right):
    return lax.dot_general(left, right, (((1,), (1,)), ((), ())), preferred_element_type=F32)


def center_and_scale(values):
    center = values - jnp.mean(values, -1, keepdims=True)
    spread = jnp.mean(center * center, -1, keepdims=True)
    scale = lax.rsqrt(spread + 1e-05)
    return center * scale, scale


def dot_tn(left, right):
    return lax.dot_general(left, right, (((0,), (0,)), ((), ())), preferred_element_type=F32)


def pass_rows(ids_ref, passes):
    ids = ids_ref[...].reshape(1, -1)
    row = lax.broadcasted_iota(jnp.int32, (passes, ids.shape[1]), 0)
    return (row == ids).astype(F32).astype(BF16)


def embed_tokens(tok_ref, ids_ref, emb_ref):
    return tok_ref[...].astype(F32) + dot_tn(pass_rows(ids_ref, emb_ref.shape[0]), emb_ref[...])


def wide(item):
    values = item[...].astype(F32)
    return values if values.ndim == 2 else values.reshape(1, -1)


def half_lanes(core, half):
    return pl.ds(pl.multiple_of(core * half, 128), half)


def whole(shape):
    return pl.BlockSpec(shape, lambda *_: (0,) * len(shape))


def carry(operands, outs, carried):
    return {1 + operands + at: outs + at for at in range(len(carried))}


def shapes(items):
    return [jax.ShapeDtypeStruct(item.shape, item.dtype) for item in items]


def params(limit=VMEM_LIMIT):
    return pltpu.CompilerParams(vmem_limit_bytes=limit)


def cost():
    return pl.CostEstimate(flops=1000, transcendentals=0, bytes_accessed=1000)


ANY = pl.BlockSpec(memory_space=pl.ANY)


def third_bias(bias):
    third = pl.program_id(0)
    rows = bias[...].astype(F32)
    return jnp.where(third == 0, rows[0:1], jnp.where(third == 2, rows[1:2], 0.0))


def qkv_send_kernel(pos, tok, ids, emb, gain, shift, weight, bias, normed_out, half_out, out):
    @pl.when(pl.program_id(0) == 0)
    def _():
        scaled, _ = center_and_scale(embed_tokens(tok, ids, emb))
        normed_out[...] = (scaled * wide(gain) + wide(shift)).astype(BF16)
        half_out[...] = normed_out[:, half_lanes(1 - pos[0], half_out.shape[1])]

    out[0] = (dot(normed_out[...], weight[...]) + third_bias(bias)).astype(BF16)


def qkv_keep_kernel(pos, normed, weight, bias, out):
    out[0] = (dot(normed[...], weight[...]) + third_bias(bias)).astype(BF16)


def qkv_send(pos, tok, ids, emb, gain, shift, weight, bias):
    rows, width = tok.shape
    half = width // 2
    return pl.pallas_call(
        qkv_send_kernel,
        grid_spec=pltpu.PrefetchScalarGridSpec(
            num_scalar_prefetch=1,
            grid=(3,),
            in_specs=[
                whole(tok.shape),
                whole(ids.shape),
                whole(emb.shape),
                whole(gain.shape),
                whole(shift.shape),
                pl.BlockSpec((width, half), lambda t, s: (0, 2 * t + 1 - s[0])),
                pl.BlockSpec((2, half), lambda t, s: (0, 1 - s[0])),
            ],
            out_specs=[
                whole(tok.shape),
                whole((rows, half)),
                pl.BlockSpec((1, rows, half), lambda t, s: (t, 0, 0)),
            ],
        ),
        out_shape=[
            jax.ShapeDtypeStruct(tok.shape, BF16),
            jax.ShapeDtypeStruct((rows, half), BF16),
            jax.ShapeDtypeStruct((3, rows, half), BF16),
        ],
        compiler_params=params(58 * 1024 * 1024),
        cost_estimate=cost(),
        name="qkv_send",
    )(pos, tok, ids, emb, gain, shift, weight, bias)


def qkv_keep(pos, normed, weight, bias):
    rows, width = normed.shape
    half = width // 2
    return pl.pallas_call(
        qkv_keep_kernel,
        grid_spec=pltpu.PrefetchScalarGridSpec(
            num_scalar_prefetch=1,
            grid=(3,),
            in_specs=[
                whole(normed.shape),
                pl.BlockSpec((width, half), lambda t, s: (0, 2 * t + s[0])),
                pl.BlockSpec((2, half), lambda t, s: (0, s[0])),
            ],
            out_specs=pl.BlockSpec((1, rows, half), lambda t, s: (t, 0, 0)),
        ),
        out_shape=jax.ShapeDtypeStruct((3, rows, half), BF16),
        compiler_params=params(),
        cost_estimate=cost(),
        name="qkv_keep",
    )(pos, normed, weight, bias)


def lane_masks():
    lane = lax.broadcasted_iota(jnp.int32, (1, PAIR), 1)
    first = (lane < HEAD_DIM).astype(F32).astype(BF16)
    return first, (1 - first).astype(BF16)


def row_split(values):
    row = lax.broadcasted_iota(jnp.int32, values.shape, 0)
    keep = row < HEAD_DIM
    wide = values.astype(F32)
    return jnp.concatenate(
        [jnp.where(keep, wide, 0.0).astype(BF16), jnp.where(keep, 0.0, wide).astype(BF16)], axis=1
    )


def gather_rows(mine, other, target, sems, core, rows):
    own = pl.ds(pl.multiple_of(core * rows, 128), rows)
    far = pl.ds(pl.multiple_of((1 - core) * rows, 128), rows)
    if len(mine.shape) == 3:
        return (
            pltpu.make_async_copy(mine, target.at[:, own, :], sems.at[0]),
            pltpu.make_async_copy(other, target.at[:, far, :], sems.at[1]),
        )
    return (
        pltpu.make_async_copy(mine, target.at[own, :], sems.at[0]),
        pltpu.make_async_copy(other, target.at[far, :], sems.at[1]),
    )


def segment_firsts(seg_ref, x):
    row = seg_ref[pl.ds(x, 1), :]
    return [jnp.sum((row < number).astype(F32)).astype(jnp.int32) for number in (1, 2, 3)]


def fill_starts(firsts, start):
    at = lax.broadcasted_iota(jnp.int32, start.shape, 1)
    own = jnp.zeros(start.shape, jnp.int32)
    for first in firsts:
        own = jnp.where(at >= first, first, own)
    start[...] = own


def first_block(firsts, q0):
    own = jnp.int32(0)
    for first in firsts:
        own = jnp.where(first <= q0, first, own)
    return own // BK


def valid_keys(start, q0, kb):
    key_at = lax.broadcasted_iota(jnp.int32, (BK, BQ), 0) + kb * BK
    query_at = lax.broadcasted_iota(jnp.int32, (BK, BQ), 1) + q0
    inside = (key_at >= start) & (key_at <= query_at)
    return jnp.concatenate([inside, inside], axis=1)


def attend_kernel(pos, seg, keep, recv, *rest, ties):
    own_out, far_out, lse_out, qkv, qq, vm, sc, acc, joined, start_ref, sems = rest[ties:]
    core = pos[0]
    rows = own_out.shape[0]
    pairs = own_out.shape[1] // PAIR
    copies = gather_rows(keep, recv, qkv, sems, core, rows)
    for item in copies:
        item.start()
    firsts = segment_firsts(seg, pos[4])
    fill_starts(firsts, start_ref)
    for item in copies:
        item.wait()
    first, second = lane_masks()

    def prepare(kb, _):
        at = pl.ds(pl.multiple_of(kb * BK, BK), BK)
        for p in range(pairs):
            vm[kb, p] = row_split(qkv[2, at, p * PAIR : (p + 1) * PAIR].T)
        return 0

    lax.fori_loop(0, SEQ_LEN // BK, prepare, 0)

    def one_block(qi, _):
        q0 = pl.multiple_of(qi * BQ, BQ)
        at = pl.ds(q0, BQ)
        start = start_ref[:, at]
        low = first_block(firsts, q0)
        high = (qi + 1) * (BQ // BK)
        for p in range(pairs):
            q = qkv[0, at, p * PAIR : (p + 1) * PAIR] * jnp.asarray(0.125, BF16)
            qq[p, :BQ] = q * first
            qq[p, BQ:] = q * second
            acc[p] = jnp.zeros((PAIR, BQ), F32)

        def scores(kb, tops):
            inside = valid_keys(start, q0, kb)
            rows_at = pl.ds(pl.multiple_of(kb * BK, BK), BK)
            grown = []
            for p in range(pairs):
                s = dot_nt(qkv[1, rows_at, p * PAIR : (p + 1) * PAIR], qq[p])
                s = jnp.where(inside, s, NEG)
                sc[kb - low, p] = s
                grown.append(jnp.maximum(tops[p], jnp.max(s, axis=0, keepdims=True)))
            return tuple(grown)

        tops = lax.fori_loop(
            low, high, scores, tuple(jnp.full((1, 2 * BQ), NEG, F32) for _ in range(pairs))
        )

        def weigh(kb, sums):
            grown = []
            for p in range(pairs):
                raw = jnp.exp(sc[kb - low, p] - tops[p])
                grown.append(sums[p] + jnp.sum(raw, axis=0, keepdims=True))
                raw = raw.astype(BF16)
                acc[p] += dot(vm[kb, p], jnp.concatenate([raw[:, :BQ], raw[:, BQ:]], axis=0))
            return tuple(grown)

        sums = lax.fori_loop(
            low, high, weigh, tuple(jnp.zeros((1, 2 * BQ), F32) for _ in range(pairs))
        )
        for p in range(pairs):
            inv = 1.0 / sums[p]
            out = jnp.concatenate(
                [acc[p, :HEAD_DIM] * inv[:, :BQ], acc[p, HEAD_DIM:] * inv[:, BQ:]], axis=0
            )
            joined[at, p * PAIR : (p + 1) * PAIR] = out.T.astype(BF16)
            lse_out[qi, p] = tops[p] + jnp.log(sums[p])
        return 0

    lax.fori_loop(0, SEQ_LEN // BQ, one_block, 0)
    own_out[...] = joined[pl.ds(pl.multiple_of(core * rows, 128), rows), :]
    far_out[...] = joined[pl.ds(pl.multiple_of((1 - core) * rows, 128), rows), :]


def attend(pos, ties, seg, keep, recv):
    _, rows, half = keep.shape
    pairs = half // PAIR
    window = SEQ_LEN // BK

    def kernel(*refs):
        attend_kernel(*refs, ties=len(ties))

    return pl.pallas_call(
        kernel,
        grid_spec=pltpu.PrefetchScalarGridSpec(
            num_scalar_prefetch=1,
            grid=(1,),
            in_specs=[whole(seg.shape)] + [ANY] * (2 + len(ties)),
            out_specs=[
                whole((rows, half)),
                whole((rows, half)),
                whole((SEQ_LEN // BQ, pairs, 1, 2 * BQ)),
            ],
            scratch_shapes=[
                pltpu.VMEM((3, SEQ_LEN, half), BF16),
                pltpu.VMEM((pairs, 2 * BQ, PAIR), BF16),
                pltpu.VMEM((SEQ_LEN // BK, pairs, PAIR, 2 * BK), BF16),
                pltpu.VMEM((window, pairs, BK, 2 * BQ), F32),
                pltpu.VMEM((pairs, PAIR, BQ), F32),
                pltpu.VMEM((SEQ_LEN, half), BF16),
                pltpu.VMEM((1, SEQ_LEN), jnp.int32),
                pltpu.SemaphoreType.DMA((2,)),
            ],
        ),
        out_shape=[
            jax.ShapeDtypeStruct((rows, half), BF16),
            jax.ShapeDtypeStruct((rows, half), BF16),
            jax.ShapeDtypeStruct((SEQ_LEN // BQ, pairs, 1, 2 * BQ), F32),
        ],
        compiler_params=params(),
        cost_estimate=cost(),
        name="attend",
    )(pos, seg, keep, recv, *ties)


def attend_back_kernel(
    pos, seg, lse_ref, keep, recv, own, far, grad_own, grad_far, *rest, ties
):
    keep_out, send_out, qkv, att, dout, qq, dd, km, delta, dq_t, dq, dk, dv, start_ref, sems = rest[ties:]
    core = pos[0]
    rows, half = own.shape
    pairs = half // PAIR
    copies = (
        gather_rows(keep, recv, qkv, sems.at[0], core, rows)
        + gather_rows(own, far, att, sems.at[1], core, rows)
        + gather_rows(grad_own, grad_far, dout, sems.at[2], core, rows)
    )
    for item in copies:
        item.start()
    firsts = segment_firsts(seg, pos[4])
    fill_starts(firsts, start_ref)
    dk[...] = jnp.zeros_like(dk)
    dv[...] = jnp.zeros_like(dv)
    for item in copies:
        item.wait()
    first, second = lane_masks()

    def prepare(kb, _):
        at = pl.ds(pl.multiple_of(kb * BK, BK), BK)
        for p in range(pairs):
            km[kb, p] = row_split(qkv[1, at, p * PAIR : (p + 1) * PAIR].T)
        return 0

    lax.fori_loop(0, SEQ_LEN // BK, prepare, 0)

    def one_block(qi, _):
        q0 = pl.multiple_of(qi * BQ, BQ)
        at = pl.ds(q0, BQ)
        start = start_ref[:, at]
        low = first_block(firsts, q0)
        high = (qi + 1) * (BQ // BK)
        for p in range(pairs):
            lanes = slice(p * PAIR, (p + 1) * PAIR)
            q = qkv[0, at, lanes] * jnp.asarray(0.125, BF16)
            qq[p, :BQ] = q * first
            qq[p, BQ:] = q * second
            g = dout[at, lanes]
            dd[p, :BQ] = g * first
            dd[p, BQ:] = g * second
            both = (g.astype(F32) * att[at, lanes].astype(F32)).T
            delta[p] = jnp.concatenate(
                [
                    jnp.sum(both[:HEAD_DIM], axis=0, keepdims=True),
                    jnp.sum(both[HEAD_DIM:], axis=0, keepdims=True),
                ],
                axis=1,
            )
            dq_t[p] = jnp.zeros((PAIR, BQ), F32)

        def step(kb, _):
            inside = valid_keys(start, q0, kb)
            rows_at = pl.ds(pl.multiple_of(kb * BK, BK), BK)
            for p in range(pairs):
                lanes = slice(p * PAIR, (p + 1) * PAIR)
                s = dot_nt(qkv[1, rows_at, lanes], qq[p])
                prob = jnp.where(inside, jnp.exp(s - lse_ref[qi, p]), 0.0)
                grad_prob = dot_nt(qkv[2, rows_at, lanes], dd[p])
                grad_s = (prob * (grad_prob - delta[p])).astype(BF16)
                dv[rows_at, lanes] += dot(prob.astype(BF16), dd[p])
                dk[rows_at, lanes] += dot(grad_s, qq[p])
                dq_t[p] += dot(km[kb, p], jnp.concatenate([grad_s[:, :BQ], grad_s[:, BQ:]], axis=0))
            return 0

        lax.fori_loop(low, high, step, 0)
        for p in range(pairs):
            dq[p * PAIR : (p + 1) * PAIR, at] = (dq_t[p] * 0.125).astype(BF16)
        return 0

    lax.fori_loop(0, SEQ_LEN // BQ, one_block, 0)
    for target, at in ((keep_out, core), (send_out, 1 - core)):
        tokens = pl.ds(pl.multiple_of(at * rows, 128), rows)
        target[0] = dq[:, tokens]
        target[1] = dk[tokens, :].astype(BF16).T
        target[2] = dv[tokens, :].astype(BF16).T


def attend_back(ties, pos, seg, lse, keep, recv, own, far, grad_own, grad_far):
    _, rows, half = keep.shape
    pairs = half // PAIR
    out = (3, half, rows)

    def kernel(*refs):
        attend_back_kernel(*refs, ties=len(ties))

    return pl.pallas_call(
        kernel,
        grid_spec=pltpu.PrefetchScalarGridSpec(
            num_scalar_prefetch=1,
            grid=(1,),
            in_specs=[whole(seg.shape), whole(lse.shape)] + [ANY] * (6 + len(ties)),
            out_specs=[whole(out), whole(out)],
            scratch_shapes=[
                pltpu.VMEM((3, SEQ_LEN, half), BF16),
                pltpu.VMEM((SEQ_LEN, half), BF16),
                pltpu.VMEM((SEQ_LEN, half), BF16),
                pltpu.VMEM((pairs, 2 * BQ, PAIR), BF16),
                pltpu.VMEM((pairs, 2 * BQ, PAIR), BF16),
                pltpu.VMEM((SEQ_LEN // BK, pairs, PAIR, 2 * BK), BF16),
                pltpu.VMEM((pairs, 1, 2 * BQ), F32),
                pltpu.VMEM((pairs, PAIR, BQ), F32),
                pltpu.VMEM((half, SEQ_LEN), BF16),
                pltpu.VMEM((SEQ_LEN, half), F32),
                pltpu.VMEM((SEQ_LEN, half), F32),
                pltpu.VMEM((1, SEQ_LEN), jnp.int32),
                pltpu.SemaphoreType.DMA((3, 2)),
            ],
        ),
        out_shape=[jax.ShapeDtypeStruct(out, BF16)] * 2,
        compiler_params=params(),
        cost_estimate=cost(),
        name="attend_back",
    )(pos, seg, lse, keep, recv, own, far, grad_own, grad_far, *ties)


def gather_lanes(core, own, far, target):
    half = own.shape[1]
    target[:, half_lanes(core, half)] = own[...]
    target[:, half_lanes(1 - core, half)] = far[...]


def hidden_block(i, core):
    late = i >> 1
    return 2 * (late * core + (1 - late) * (1 - core)) + (i & 1)


def early(i):
    return jnp.minimum(i, 1)


def late(i):
    return jnp.maximum(i - 2, 0)


def ff_first_kernel(
    pos, tok, ids, emb, own, far, weight, bias, gain, shift, cot, up, up_bias, down,
    after_out, normed_out, half_out, act_own, act_send, grad_out, bias_grad, attended, act,
):
    step = pl.program_id(0)

    @pl.when(step == 0)
    def _():
        gather_lanes(pos[0], own, far, attended)
        after = embed_tokens(tok, ids, emb) + dot(attended[...], weight[...]) + wide(bias)
        after_out[...] = after
        scaled, _ = center_and_scale(after)
        normed_out[...] = (scaled * wide(gain) + wide(shift)).astype(BF16)
        half_out[...] = normed_out[:, half_lanes(1 - pos[0], half_out.shape[1])]

    for part in range(up.shape[1] // SUB):
        cols = slice(part * SUB, (part + 1) * SUB)
        u = dot(normed_out[...], up[:, cols]) + up_bias[:, cols].astype(F32)
        grad_act = dot_nt(cot[...], down[cols, :])
        square = u * u
        t = jnp.tanh(0.7978845608028654 * u * (1.0 + 0.044715 * square))
        half = 0.5 * (1.0 + t)
        act[:, cols] = (u * half).astype(BF16)
        slope = half + 0.5 * u * (1.0 - t * t) * (0.7978845608028654 * (1.0 + 0.134145 * square))
        grad = (grad_act * slope).astype(BF16)
        grad_out[:, cols] = grad
        bias_grad[:, cols] = jnp.sum(grad.astype(F32), axis=0, keepdims=True)

    @pl.when(step < 2)
    def _():
        act_send[...] = act[...]

    @pl.when(step >= 2)
    def _():
        act_own[...] = act[...]


def ff_first(pos, tok, ids, emb, own, far, weight, bias, gain, shift, cot, up, up_bias, down):
    rows, width = tok.shape
    hidden = up.shape[1]
    first = (tok, ids, emb, own, far, weight, bias, gain, shift, cot)
    shape = jax.ShapeDtypeStruct
    return pl.pallas_call(
        ff_first_kernel,
        grid_spec=pltpu.PrefetchScalarGridSpec(
            num_scalar_prefetch=1,
            grid=(4,),
            in_specs=[whole(item.shape) for item in first]
            + [
                pl.BlockSpec((width, width), lambda i, s: (0, hidden_block(i, s[0]))),
                pl.BlockSpec((1, width), lambda i, s: (0, hidden_block(i, s[0]))),
                pl.BlockSpec((width, width), lambda i, s: (hidden_block(i, s[0]), 0)),
            ],
            out_specs=[
                whole((rows, width)),
                whole((rows, width)),
                whole((rows, width // 2)),
                pl.BlockSpec((rows, width), lambda i, s: (0, late(i))),
                pl.BlockSpec((rows, width), lambda i, s: (0, early(i))),
                pl.BlockSpec((rows, width), lambda i, s: (0, hidden_block(i, s[0]))),
                pl.BlockSpec((1, width), lambda i, s: (0, hidden_block(i, s[0]))),
            ],
            scratch_shapes=[pltpu.VMEM((rows, width), BF16), pltpu.VMEM((rows, width), BF16)],
        ),
        out_shape=[
            shape((rows, width), F32),
            shape((rows, width), BF16),
            shape((rows, width // 2), BF16),
            shape((rows, hidden // 2), BF16),
            shape((rows, hidden // 2), BF16),
            shape((rows, hidden), BF16),
            shape((1, hidden), F32),
        ],
        compiler_params=params(),
        cost_estimate=cost(),
        name="ff_first",
    )(pos, *first, up, up_bias, down)


def ff_back_kernel(
    pos, grad_pre, up, after, cot, gain, weight,
    grad_after, branch_out, own_out, far_out, sums, total,
):
    step = pl.program_id(0)
    part = dot_nt(grad_pre[...], up[...])

    @pl.when(step == 0)
    def _():
        total[...] = part

    @pl.when(step > 0)
    def _():
        total[...] += part

    @pl.when(step == pl.num_programs(0) - 1)
    def _():
        core = pos[0]
        half = own_out.shape[1]
        scaled, scale = center_and_scale(after[...])
        grad = total[...]
        inner = grad * wide(gain)
        shift = jnp.mean(inner, -1, keepdims=True)
        slope = jnp.mean(inner * scaled, -1, keepdims=True)
        cot_f32 = wide(cot)
        result = cot_f32 + scale * (inner - shift - scaled * slope)
        grad_after[...] = result
        branch_out[...] = result.astype(BF16)
        branch = branch_out[...]
        for target, at in ((far_out, 1 - core), (own_out, core)):
            rows = pl.ds(pl.multiple_of(at * half, 128), half)
            target[...] = dot_nt(branch, weight[rows, :]).astype(BF16)
        sums[0:1] = jnp.sum(grad * scaled, axis=0, keepdims=True)
        sums[1:2] = jnp.sum(grad, axis=0, keepdims=True)
        sums[2:3] = jnp.sum(branch.astype(F32), axis=0, keepdims=True)
        sums[3:4] = jnp.sum(cot_f32, axis=0, keepdims=True)


def ff_back(pos, grad_pre, up, after, cot, gain, weight):
    rows, width = after.shape
    half = width // 2
    last = (after, cot, gain, weight)
    outs = [
        jax.ShapeDtypeStruct((rows, width), F32),
        jax.ShapeDtypeStruct((rows, width), BF16),
        jax.ShapeDtypeStruct((rows, half), BF16),
        jax.ShapeDtypeStruct((rows, half), BF16),
        jax.ShapeDtypeStruct((4, width), F32),
    ]
    return pl.pallas_call(
        ff_back_kernel,
        grid_spec=pltpu.PrefetchScalarGridSpec(
            num_scalar_prefetch=1,
            grid=(grad_pre.shape[1] // width,),
            in_specs=[
                pl.BlockSpec((rows, width), lambda i, s: (0, i)),
                pl.BlockSpec((width, width), lambda i, s: (0, i)),
            ]
            + [whole(item.shape) for item in last],
            out_specs=[whole(item.shape) for item in outs],
            scratch_shapes=[pltpu.VMEM((rows, width), F32)],
        ),
        out_shape=outs,
        compiler_params=params(),
        cost_estimate=cost(),
        name="ff_back",
    )(pos, grad_pre, up, *last)


def z_place(z):
    return (z & 1) * 2 + (z >> 1)


def chips():
    return [(x, y, z) for x in range(2) for y in range(2) for z in range(4)]


def chip_row(pos, x, y, z):
    return ((2 * z_place(z) + y) ^ pos[3]) * 2 + (x ^ pos[2])


def rows_of(values, chip, per, at=0, count=None):
    count = per if count is None else count
    return values[pl.ds(pl.multiple_of(chip * per + at, 8), count), :].astype(BF16)


def down_weight_kernel(pos, act, act_far, cot, cot_far, *rest, ties):
    keep, send, rows_f32 = rest[ties:]
    per = rows_f32.shape[0] // 16
    half = rows_f32.shape[1] // 2
    rows_f32[...] = dot_tn(cot[...], act[...]) + dot_tn(cot_far[...], act_far[...])
    for x, y, z in chips():
        rows = rows_of(rows_f32, chip_row(pos, x, y, z), per)
        (keep, send)[x][y, z, :per, :] = rows[:, :half]
        (keep, send)[x][y, z, per:, :] = rows[:, half:]


def down_weight_call(pos, ties, act, act_far, cot, cot_far):
    rows, width = cot.shape
    half = width // 2
    per = width // 16
    out = jax.ShapeDtypeStruct((2, 4, 4 * per, half), BF16)

    def kernel(*refs):
        down_weight_kernel(*refs, ties=len(ties))

    return pl.pallas_call(
        kernel,
        grid_spec=pltpu.PrefetchScalarGridSpec(
            num_scalar_prefetch=1,
            grid=(2,),
            in_specs=[pl.BlockSpec((rows, width), lambda i, s: (0, i))] * 2
            + [whole(cot.shape)] * 2
            + [ANY] * len(ties),
            out_specs=[pl.BlockSpec((2, 4, 2 * per, half), lambda i, s: (0, 0, i, 0))] * 2,
            scratch_shapes=[pltpu.VMEM((width, width), F32)],
        ),
        out_shape=[out, out],
        compiler_params=params(),
        cost_estimate=cost(),
        name="down_weight",
    )(pos, act, act_far, cot, cot_far, *ties)


def up_weight_kernel(pos, grad, grad_far, normed, normed_far, keep, send, rows_f32):
    per = rows_f32.shape[0] // 4
    own = normed[:, half_lanes(pos[0], rows_f32.shape[1])]
    far = normed_far[:, half_lanes(pos[0], rows_f32.shape[1])]
    rows_f32[...] = dot_tn(grad[...], own) + dot_tn(grad_far[...], far)
    for x in range(2):
        for y in range(2):
            chip = (y ^ (pos[3] & 1)) * 2 + (x ^ pos[2])
            (keep, send)[y][x, 0, :per, :] = rows_of(rows_f32, chip, per)


def up_weight_call(pos, grad, grad_far, normed, normed_far):
    rows, width = normed.shape
    half = width // 2
    per = width // 16
    out = jax.ShapeDtypeStruct((2, 4, 5 * per, half), BF16)

    def at(i, s):
        return 0, z_place(i ^ (s[3] >> 1)), 0, 0

    return pl.pallas_call(
        up_weight_kernel,
        grid_spec=pltpu.PrefetchScalarGridSpec(
            num_scalar_prefetch=1,
            grid=(4,),
            in_specs=[pl.BlockSpec((rows, width), lambda i, s: (0, i))] * 2
            + [whole(normed.shape), whole(normed_far.shape)],
            out_specs=[pl.BlockSpec((2, 1, 4 * per, half), at)] * 2,
            scratch_shapes=[pltpu.VMEM((width, half), F32)],
        ),
        out_shape=[out, out],
        compiler_params=params(),
        cost_estimate=cost(),
        name="up_weight",
    )(pos, grad, grad_far, normed, normed_far)


def out_weight_kernel(pos, branch, branch_far, own, far, keep_in, send_in, tie, keep_out, send_out, rows_f32):
    per = rows_f32.shape[0] // 16
    rows_f32[...] = dot_tn(branch[...], own[...]) + dot_tn(branch_far[...], far[...])
    for x, y, z in chips():
        (keep_out, send_out)[y][x, z] = rows_of(rows_f32, chip_row(pos, x, y, z), per)


def out_weight_call(pos, tie, branch, branch_far, own, far, keep, send):
    rows, width = branch.shape
    half = width // 2
    block = pl.BlockSpec((2, 4, width // 16, half), lambda i, s: (0, 0, 4, 0))
    return pl.pallas_call(
        out_weight_kernel,
        grid_spec=pltpu.PrefetchScalarGridSpec(
            num_scalar_prefetch=1,
            grid=(1,),
            in_specs=[whole(branch.shape)] * 2 + [whole(own.shape)] * 2 + [ANY] * 3,
            out_specs=[block, block],
            scratch_shapes=[pltpu.VMEM((width, half), F32)],
        ),
        out_shape=[jax.ShapeDtypeStruct(keep.shape, BF16)] * 2,
        input_output_aliases={5: 0, 6: 1},
        compiler_params=params(),
        cost_estimate=cost(),
        name="out_weight",
    )(pos, branch, branch_far, own, far, keep, send, tie)


def pack_sums(tables, long, packed):
    count, _, share = packed.shape
    for device in range(count):
        low = 0
        for table in tables:
            rows = table.shape[0]
            packed[device, low : low + rows, :] = table[:, device * share : (device + 1) * share]
            low += rows
        for part in range(4):
            at = (4 * device + part) * share
            packed[device, low + part : low + part + 1, :] = long[:, at : at + share]


def mixed_kernel(pos, act_send, act_own, down, after, bias, one, two, three, four, *rest, ties, carried):
    out, packed = rest[ties + carried : ties + carried + 2]
    total = rest[-1]
    step = pl.program_id(0)

    @pl.when(step == 0)
    def _():
        total[...] = after[...] + wide(bias)

    @pl.when(step < 2)
    def _():
        total[...] += dot(act_send[...], down[...])

    @pl.when(step >= 2)
    def _():
        total[...] += dot(act_own[...], down[...])

    @pl.when(step == pl.num_programs(0) - 1)
    def _():
        out[...] = total[...].astype(BF16)
        pack_sums((one, two, three), four, packed)


def mixed_call(pos, ties, carried, act_send, act_own, down, after, bias, *sums):
    rows, width = after.shape
    devices = lax.axis_size("batch") * lax.axis_size("head")
    packed = (devices, sum(item.shape[0] for item in sums[:3]) + 4, width // devices)

    def kernel(*refs):
        mixed_kernel(*refs, ties=len(ties), carried=len(carried))

    return pl.pallas_call(
        kernel,
        grid_spec=pltpu.PrefetchScalarGridSpec(
            num_scalar_prefetch=1,
            grid=(4,),
            in_specs=[
                pl.BlockSpec((rows, width), lambda i, s: (0, early(i))),
                pl.BlockSpec((rows, width), lambda i, s: (0, late(i))),
                pl.BlockSpec((width, width), lambda i, s: (hidden_block(i, s[0]), 0)),
                whole(after.shape),
                whole(bias.shape),
            ]
            + [whole(item.shape) for item in sums]
            + [ANY] * (len(ties) + len(carried)),
            out_specs=[whole((rows, width)), whole(packed)] + [ANY] * len(carried),
            scratch_shapes=[pltpu.VMEM((rows, width), F32)],
        ),
        out_shape=[jax.ShapeDtypeStruct((rows, width), BF16), jax.ShapeDtypeStruct(packed, F32)]
        + shapes(carried),
        input_output_aliases=carry(5 + len(sums) + len(ties), 2, carried),
        compiler_params=params(),
        cost_estimate=cost(),
        name="mixed",
    )(pos, act_send, act_own, down, after, bias, *sums, *ties, *carried)


def qkv_weight_kernel(
    pos, mine, mine_far, other, other_far, normed, normed_far, *rest, ties
):
    left_keep, left_send, right_keep, right_send, sums, rows_f32 = rest[ties:]
    core = pos[0]
    half = normed_far.shape[1]
    third = pl.program_id(0)
    own = normed[:, half_lanes(core, half)]
    ones = jnp.ones((8, own.shape[0]), BF16)

    @pl.when(third == 0)
    def _():
        sums[...] = jnp.zeros_like(sums)

    for near, far, at in ((mine, mine_far, core), (other, other_far, 1 - core)):
        rows = pl.ds(pl.multiple_of((2 * third + at) * half, 128), half)
        rows_f32[rows, :] = dot(near[0], own) + dot(far[0], normed_far[...])
    row = (dot_nt(ones, mine[0]) + dot_nt(ones, mine_far[0]))[:1]
    lanes = half_lanes(core, half)
    for t in range(3):
        sums[t : t + 1, lanes] += jnp.where(third == t, row, 0.0)

    @pl.when(third == pl.num_programs(0) - 1)
    def _():
        per = rows_f32.shape[0] // 32
        for x, y, z in chips():
            chip = chip_row(pos, x, y, z)
            (left_keep, left_send)[x][y, z] = rows_of(rows_f32, chip, 2 * per, 0, per)
            (right_keep, right_send)[y][x, z] = rows_of(rows_f32, chip, 2 * per, per, per)


def qkv_weight_call(pos, ties, mine, mine_far, other, other_far, normed, normed_far):
    rows, width = normed.shape
    half = width // 2
    third = pl.BlockSpec((1, half, rows), lambda t, s: (t, 0, 0))
    out = jax.ShapeDtypeStruct((2, 4, 3 * width // 32, half), BF16)

    def kernel(*refs):
        qkv_weight_kernel(*refs, ties=len(ties))

    return pl.pallas_call(
        kernel,
        grid_spec=pltpu.PrefetchScalarGridSpec(
            num_scalar_prefetch=1,
            grid=(3,),
            in_specs=[third] * 4 + [whole(normed.shape), whole(normed_far.shape)] + [ANY] * len(ties),
            out_specs=[whole(out.shape)] * 4 + [whole((3, width))],
            scratch_shapes=[pltpu.VMEM((3 * width, half), F32)],
        ),
        out_shape=[out] * 4 + [jax.ShapeDtypeStruct((3, width), F32)],
        compiler_params=params(),
        cost_estimate=cost(),
        name="qkv_weight",
    )(pos, mine, mine_far, other, other_far, normed, normed_far, *ties)


def input_back_kernel(pos, mine, other, weight, tok, ids, emb, gain, grad_after, *rest, ties, carried):
    out, sums = rest[ties + carried : ties + carried + 2]
    joined, total = rest[-2:]
    core = pos[0]
    step = pl.program_id(0)
    half = mine.shape[1]
    joined[half_lanes(core, half), :] = mine[0]
    joined[half_lanes(1 - core, half), :] = other[0]
    part = lax.dot_general(
        joined[...], weight[...], (((0,), (1,)), ((), ())), preferred_element_type=F32
    )

    @pl.when(step == 0)
    def _():
        total[...] = part

    @pl.when(step > 0)
    def _():
        total[...] += part

    @pl.when(step == pl.num_programs(0) - 1)
    def _():
        grad = total[...]
        scaled, scale = center_and_scale(embed_tokens(tok, ids, emb))
        inner = grad * wide(gain)
        shift = jnp.mean(inner, -1, keepdims=True)
        slope = jnp.mean(inner * scaled, -1, keepdims=True)
        result = grad_after[...] + scale * (inner - shift - scaled * slope)
        out[...] = result
        passes = emb.shape[0]
        chosen = pass_rows(ids, passes)
        high = result.astype(BF16)
        less = result - high.astype(F32)
        middle = less.astype(BF16)
        least = (less - middle.astype(F32)).astype(BF16)
        sums[0:passes] = dot(chosen, high) + (dot(chosen, middle) + dot(chosen, least))
        sums[passes : passes + 1] = jnp.sum(grad * scaled, axis=0, keepdims=True)
        sums[passes + 1 : passes + 2] = jnp.sum(grad, axis=0, keepdims=True)


def input_back(pos, ties, carried, mine, other, weight, tok, ids, emb, gain, grad_after):
    rows, width = tok.shape
    third = pl.BlockSpec((1, width // 2, rows), lambda t, s: (t, 0, 0))
    fixed = (tok, ids, emb, gain, grad_after)
    outs = [
        jax.ShapeDtypeStruct((rows, width), F32),
        jax.ShapeDtypeStruct((emb.shape[0] + 2, width), F32),
    ]

    def kernel(*refs):
        input_back_kernel(*refs, ties=len(ties), carried=len(carried))

    return pl.pallas_call(
        kernel,
        grid_spec=pltpu.PrefetchScalarGridSpec(
            num_scalar_prefetch=1,
            grid=(3,),
            in_specs=[third, third, pl.BlockSpec((width, width), lambda t, s: (0, t))]
            + [whole(item.shape) for item in fixed]
            + [ANY] * (len(ties) + len(carried)),
            out_specs=[whole(item.shape) for item in outs] + [ANY] * len(carried),
            scratch_shapes=[pltpu.VMEM((width, rows), BF16), pltpu.VMEM((rows, width), F32)],
        ),
        out_shape=outs + shapes(carried),
        input_output_aliases=carry(3 + len(fixed) + len(ties), len(outs), carried),
        compiler_params=params(),
        cost_estimate=cost(),
        name="input_back",
    )(pos, mine, other, weight, *fixed, *ties, *carried)


def swap_head(values, bit):
    size = lax.axis_size("head")
    return lax.ppermute(values, "head", [(i, i ^ bit) for i in range(size)])


def swap_batch(values, bit):
    size = lax.axis_size("batch")
    return lax.ppermute(values, "batch", [(i, i ^ bit) for i in range(size)])


class Sum:
    def __init__(self, *parts):
        self.parts = parts

    def __getitem__(self, index):
        return Sum(*[part[index] for part in self.parts])

    def wide(self):
        total = self.parts[0].astype(F32)
        for part in self.parts[1:]:
            total = total + part.astype(F32)
        return total

    def sent(self):
        return self.wide().astype(BF16)


def swap_x(values):
    return swap_head(values, 2)


def swap_y(values):
    return swap_batch(values, 1)


def z_step(left, right):
    cut = left.parts[0].shape[0] // 2
    split = left.parts[0].shape[1]
    sent = jnp.concatenate([left[cut:].sent(), right[cut:].sent()], 1)

    def finish():
        got = swap_batch(sent, 2 if cut == 2 else 4)
        return Sum(*left[:cut].parts, got[:, :split]), Sum(*right[:cut].parts, got[:, split:])

    return sent, finish


def chip_sums(core, *items):
    flat = [jnp.where(core == 0, item[..., 1, :, :], item[..., 0, :, :]) for item in items]
    width = flat[0].shape[-1]
    got = swap_head(jnp.concatenate([item.reshape(-1, width) for item in flat], 0), 1)
    out, at = [], 0
    for item, sent in zip(items, flat):
        count = sent.size // width
        far = got[at : at + count].reshape(sent.shape)
        near = jnp.where(core == 0, item[..., 0, :, :], item[..., 1, :, :])
        out.append((jnp.where(core == 0, near, far), jnp.where(core == 0, far, near)))
        at += count
    return out


def scatter_any(core, values):
    half = values.shape[-1]
    rows = values.reshape(-1, half).astype(F32)
    both = lax.dynamic_update_slice(jnp.zeros((rows.shape[0], 2 * half), F32), rows, (0, core * half))
    return lax.psum_scatter(both, ("batch", "head"), scatter_dimension=0, tiled=True)


def by_chip(values):
    rest = values.shape[3:]
    split = values.reshape((2, 2, 2, 2) + rest)
    order = (3, 2, 1, 0) + tuple(range(4, split.ndim))
    return split.transpose(order).reshape((16,) + rest)


def on_device(
    tokens,
    pass_ids,
    segment_ids,
    pass_embed,
    norm1_gain,
    norm1_shift,
    qkv_weight,
    qv_bias,
    out_weight,
    out_bias,
    norm2_gain,
    norm2_shift,
    up_weight,
    up_bias,
    down_weight,
    down_bias,
    cotangent,
):
    rows, width = tokens.shape
    hidden_units = up_weight.shape[1]
    passes = pass_embed.shape[0]
    pairs = width // 2 // PAIR
    assert 2 * rows == SEQ_LEN and lax.axis_size("head") == 4 and hidden_units == 4 * width
    direct = lax.axis_size("batch") == BLOCKS

    head = lax.axis_index("head").astype(jnp.int32)
    batch = lax.axis_index("batch").astype(jnp.int32)
    core, x_bit = head % 2, head // 2
    zero = jnp.zeros((), jnp.int32)
    place = [core, x_bit, batch] if direct else [zero, zero, zero]
    pos = jnp.stack([core] + place + [x_bit])

    row = lambda item: item
    ids = row(pass_ids)
    gain_one, gain_two = row(norm1_gain), row(norm2_gain)
    cot_far = swap_head(cotangent, 1)
    normed, normed_send, send = qkv_send(
        pos, tokens, ids, pass_embed, gain_one, row(norm1_shift), qkv_weight, qv_bias
    )
    recv = swap_head(send, 1)
    normed_far = swap_head(normed_send, 1)
    keep = qkv_keep(pos, normed, qkv_weight, qv_bias)
    own, far_send, lse = attend(pos, (cot_far, normed_far), segment_ids, keep, recv)
    far = swap_head(far_send, 1)
    after, normed_two, normed_two_send, act_own, act_send, grad_pre, up_bias_grad = ff_first(
        pos, tokens, ids, pass_embed, own, far, out_weight, row(out_bias), gain_two, row(norm2_shift),
        cotangent, up_weight, up_bias.reshape(1, -1), down_weight,
    )
    act_far = swap_head(act_send, 1)
    grad_pre_far = swap_head(grad_pre, 1)
    normed_two_far = swap_head(normed_two, 1)
    grad_after, branch, grad_own, grad_send, sums_two = ff_back(
        pos, grad_pre, up_weight, after, cotangent, gain_two, out_weight
    )
    grad_far = swap_head(grad_send, 1)
    branch_far = swap_head(branch, 1)
    up_keep, up_send = up_weight_call(pos, grad_pre, grad_pre_far, normed_two, normed_two_far)
    up_keep, up_send = out_weight_call(pos, grad_far, branch, branch_far, own, far_send, up_keep, up_send)
    down_keep, down_send = down_weight_call(pos, (up_send,), act_own, act_far, cotangent, cot_far)
    if direct:
        left = Sum(down_keep, swap_x(down_send))
        right = Sum(up_keep, swap_y(up_send))
    mine, mine_send = attend_back(
        (down_send, up_send), pos, segment_ids, lse, keep, recv, own, far_send, grad_own, grad_far
    )
    other = swap_head(mine_send, 1)
    other_far = swap_head(mine, 1)
    ties, carried = (), ()
    if direct:
        left_sent, right_sent = left[1].sent(), right[1].sent()
        ties = (left_sent, right_sent)
    left_keep, left_send, right_keep, right_send, bias_sums = qkv_weight_call(
        pos, ties, mine, mine_send, other, other_far, normed, normed_far
    )
    if direct:
        one_got, two_got = swap_x(left_send), swap_y(right_send)
        left = Sum(*left[0].parts, swap_y(left_sent))
        right = Sum(*right[0].parts, swap_x(right_sent))
        mid_sent, mid_next = z_step(left, right)
        ties, carried = (mid_sent,), (left_keep, right_keep)
    input_grad, sums_one, *carried = input_back(
        pos, ties, carried, mine, other, qkv_weight, tokens, ids, pass_embed, gain_one, grad_after
    )
    if direct:
        one, two = Sum(carried[0], one_got), Sum(carried[1], two_got)
        one_sent, two_sent = one[1].sent(), two[1].sent()
        one_last, two_last = swap_y(one_sent), swap_x(two_sent)
        mid_sent, mid_next = z_step(*mid_next())
        qkv_sent, qkv_next = z_step(Sum(*one[0].parts, one_last), Sum(*two[0].parts, two_last))
        ties = (mid_sent, qkv_sent)
    result, packed, *carried = mixed_call(
        pos, ties, carried, act_send, act_own, down_weight, after, row(down_bias),
        sums_one, bias_sums, sums_two, up_bias_grad,
    )

    per = width // 32
    if direct:
        one, two = qkv_next()
        one = Sum(carried[0][0][:2], *one.parts[1:])
        two = Sum(carried[1][0][:2], *two.parts[1:])
        _, qkv_next = z_step(one, two)
        left, right = [item.wide()[0] for item in mid_next()]
        cut = 8 * per
        down, up, out = chip_sums(
            core,
            left.reshape(4, 2, per, -1),
            right[:cut].reshape(2, 4 * per, -1),
            right[cut:].reshape(2, per, -1),
        )
        (qkv,) = chip_sums(core, jnp.stack([item.wide()[0] for item in qkv_next()]))
        down_grad = jnp.concatenate(down, 0).transpose(0, 2, 1).reshape(hidden_units, -1)
        up_grad, out_grad, qkv_grad = [jnp.concatenate(item, -1) for item in (up, out, qkv)]
    else:
        down = by_chip(jnp.stack([down_keep, down_send])).reshape(16, 4, 2 * per, -1)
        down = down.transpose(0, 2, 1, 3).reshape(16, 2 * per, -1)
        up = by_chip(jnp.stack([up_keep, up_send], 1))
        left = by_chip(jnp.stack([left_keep, left_send]))
        right = by_chip(jnp.stack([right_keep, right_send], 1))
        cut = 8 * per
        down_grad = scatter_any(core, down).T
        up_grad = scatter_any(core, up[:, :cut])
        out_grad = scatter_any(core, up[:, cut:])
        qkv_grad = scatter_any(core, jnp.concatenate([left, right], 1))
    got = lax.all_to_all(packed, ("batch", "head"), split_axis=0, concat_axis=0, tiled=True)
    small = jnp.sum(got, 0)
    bias_at, two_at, up_at = passes + 2, passes + 5, passes + 9
    return (
        result,
        input_grad,
        small[:passes],
        small[passes],
        small[passes + 1],
        qkv_grad.T,
        jnp.stack([small[bias_at], small[bias_at + 2]]),
        out_grad.T,
        small[two_at + 2],
        small[two_at],
        small[two_at + 1],
        up_grad.T,
        small[up_at:].reshape(-1),
        down_grad,
        small[two_at + 3],
    )


def solution(mesh):
    both = ("batch", "head")
    copied = P()
    in_specs = (P(both, None), P(both), P("batch", None)) + (copied,) * 13 + (P(both, None),)
    out_specs = (
        P(both, None),
        P(both, None),
        P(None, both),
        P(both),
        P(both),
        P(None, both),
        P(None, both),
        P(None, both),
        P(both),
        P(both),
        P(both),
        P(None, both),
        P(both),
        P(None, both),
        P(both),
    )
    return jax.shard_map(
        on_device, mesh=mesh, in_specs=in_specs, out_specs=out_specs, check_vma=False
    )
```

```python
import jax
import jax.numpy as jnp
from jax import lax
from jax.experimental import pallas as pl
from jax.experimental.pallas import tpu as pltpu
from jax.sharding import PartitionSpec as P

HEAD_DIM = 64
SEQ_LEN = 1280
PAIR = 2 * HEAD_DIM
BQ = 256
BK = 256
BLOCKS = 8
SUB = 768
NEG = -1e30
F32 = jnp.float32
BF16 = jnp.bfloat16
VMEM_LIMIT = 24 * 1024 * 1024


def dot(left, right):
    return lax.dot_general(left, right, (((1,), (0,)), ((), ())), preferred_element_type=F32)


def dot_nt(left, right):
    return lax.dot_general(left, right, (((1,), (1,)), ((), ())), preferred_element_type=F32)


def center_and_scale(values):
    center = values - jnp.mean(values, -1, keepdims=True)
    spread = jnp.mean(center * center, -1, keepdims=True)
    scale = lax.rsqrt(spread + 1e-05)
    return center * scale, scale


def dot_tn(left, right):
    return lax.dot_general(left, right, (((0,), (0,)), ((), ())), preferred_element_type=F32)


def pass_rows(ids_ref, passes):
    ids = ids_ref[...].reshape(1, -1)
    row = lax.broadcasted_iota(jnp.int32, (passes, ids.shape[1]), 0)
    return (row == ids).astype(F32).astype(BF16)


def embed_tokens(tok_ref, ids_ref, emb_ref):
    return tok_ref[...].astype(F32) + dot_tn(pass_rows(ids_ref, emb_ref.shape[0]), emb_ref[...])


def wide(item):
    values = item[...].astype(F32)
    return values if values.ndim == 2 else values.reshape(1, -1)


def half_lanes(core, half):
    return pl.ds(pl.multiple_of(core * half, 128), half)


def whole(shape):
    return pl.BlockSpec(shape, lambda *_: (0,) * len(shape))


def carry(operands, outs, carried):
    return {1 + operands + at: outs + at for at in range(len(carried))}


def shapes(items):
    return [jax.ShapeDtypeStruct(item.shape, item.dtype) for item in items]


def params(limit=VMEM_LIMIT):
    return pltpu.CompilerParams(vmem_limit_bytes=limit)


def cost():
    return pl.CostEstimate(flops=1000, transcendentals=0, bytes_accessed=1000)


ANY = pl.BlockSpec(memory_space=pl.ANY)


def third_bias(bias):
    third = pl.program_id(0)
    rows = bias[...].astype(F32)
    return jnp.where(third == 0, rows[0:1], jnp.where(third == 2, rows[1:2], 0.0))


def qkv_send_kernel(pos, tok, ids, emb, gain, shift, weight, bias, normed_out, half_out, out):
    @pl.when(pl.program_id(0) == 0)
    def _():
        scaled, _ = center_and_scale(embed_tokens(tok, ids, emb))
        normed_out[...] = (scaled * wide(gain) + wide(shift)).astype(BF16)
        half_out[...] = normed_out[:, half_lanes(1 - pos[0], half_out.shape[1])]

    out[0] = (dot(normed_out[...], weight[...]) + third_bias(bias)).astype(BF16)


def qkv_keep_kernel(pos, normed, weight, bias, out):
    out[0] = (dot(normed[...], weight[...]) + third_bias(bias)).astype(BF16)


def qkv_send(pos, tok, ids, emb, gain, shift, weight, bias):
    rows, width = tok.shape
    half = width // 2
    return pl.pallas_call(
        qkv_send_kernel,
        grid_spec=pltpu.PrefetchScalarGridSpec(
            num_scalar_prefetch=1,
            grid=(3,),
            in_specs=[
                whole(tok.shape),
                whole(ids.shape),
                whole(emb.shape),
                whole(gain.shape),
                whole(shift.shape),
                pl.BlockSpec((width, half), lambda t, s: (0, 2 * t + 1 - s[0])),
                pl.BlockSpec((2, half), lambda t, s: (0, 1 - s[0])),
            ],
            out_specs=[
                whole(tok.shape),
                whole((rows, half)),
                pl.BlockSpec((1, rows, half), lambda t, s: (t, 0, 0)),
            ],
        ),
        out_shape=[
            jax.ShapeDtypeStruct(tok.shape, BF16),
            jax.ShapeDtypeStruct((rows, half), BF16),
            jax.ShapeDtypeStruct((3, rows, half), BF16),
        ],
        compiler_params=params(58 * 1024 * 1024),
        cost_estimate=cost(),
        name="qkv_send",
    )(pos, tok, ids, emb, gain, shift, weight, bias)


def qkv_keep(pos, normed, weight, bias):
    rows, width = normed.shape
    half = width // 2
    return pl.pallas_call(
        qkv_keep_kernel,
        grid_spec=pltpu.PrefetchScalarGridSpec(
            num_scalar_prefetch=1,
            grid=(3,),
            in_specs=[
                whole(normed.shape),
                pl.BlockSpec((width, half), lambda t, s: (0, 2 * t + s[0])),
                pl.BlockSpec((2, half), lambda t, s: (0, s[0])),
            ],
            out_specs=pl.BlockSpec((1, rows, half), lambda t, s: (t, 0, 0)),
        ),
        out_shape=jax.ShapeDtypeStruct((3, rows, half), BF16),
        compiler_params=params(),
        cost_estimate=cost(),
        name="qkv_keep",
    )(pos, normed, weight, bias)


def lane_masks():
    lane = lax.broadcasted_iota(jnp.int32, (1, PAIR), 1)
    first = (lane < HEAD_DIM).astype(F32).astype(BF16)
    return first, (1 - first).astype(BF16)


def row_split(values):
    row = lax.broadcasted_iota(jnp.int32, values.shape, 0)
    keep = row < HEAD_DIM
    wide = values.astype(F32)
    return jnp.concatenate(
        [jnp.where(keep, wide, 0.0).astype(BF16), jnp.where(keep, 0.0, wide).astype(BF16)], axis=1
    )


def gather_rows(mine, other, target, sems, core, rows):
    own = pl.ds(pl.multiple_of(core * rows, 128), rows)
    far = pl.ds(pl.multiple_of((1 - core) * rows, 128), rows)
    if len(mine.shape) == 3:
        return (
            pltpu.make_async_copy(mine, target.at[:, own, :], sems.at[0]),
            pltpu.make_async_copy(other, target.at[:, far, :], sems.at[1]),
        )
    return (
        pltpu.make_async_copy(mine, target.at[own, :], sems.at[0]),
        pltpu.make_async_copy(other, target.at[far, :], sems.at[1]),
    )


def segment_firsts(seg_ref, x):
    row = seg_ref[pl.ds(x, 1), :]
    return [jnp.sum((row < number).astype(F32)).astype(jnp.int32) for number in (1, 2, 3)]


def fill_starts(firsts, start):
    at = lax.broadcasted_iota(jnp.int32, start.shape, 1)
    own = jnp.zeros(start.shape, jnp.int32)
    for first in firsts:
        own = jnp.where(at >= first, first, own)
    start[...] = own


def first_block(firsts, q0):
    own = jnp.int32(0)
    for first in firsts:
        own = jnp.where(first <= q0, first, own)
    return own // BK


def valid_keys(start, q0, kb):
    key_at = lax.broadcasted_iota(jnp.int32, (BK, BQ), 0) + kb * BK
    query_at = lax.broadcasted_iota(jnp.int32, (BK, BQ), 1) + q0
    inside = (key_at >= start) & (key_at <= query_at)
    return jnp.concatenate([inside, inside], axis=1)


def attend_kernel(pos, seg, keep, recv, *rest, ties):
    own_out, far_out, lse_out, qkv, qq, vm, sc, acc, joined, start_ref, sems = rest[ties:]
    core = pos[0]
    rows = own_out.shape[0]
    pairs = own_out.shape[1] // PAIR
    copies = gather_rows(keep, recv, qkv, sems, core, rows)
    for item in copies:
        item.start()
    firsts = segment_firsts(seg, pos[4])
    fill_starts(firsts, start_ref)
    for item in copies:
        item.wait()
    first, second = lane_masks()

    def prepare(kb, _):
        at = pl.ds(pl.multiple_of(kb * BK, BK), BK)
        for p in range(pairs):
            vm[kb, p] = row_split(qkv[2, at, p * PAIR : (p + 1) * PAIR].T)
        return 0

    lax.fori_loop(0, SEQ_LEN // BK, prepare, 0)

    def one_block(qi, _):
        q0 = pl.multiple_of(qi * BQ, BQ)
        at = pl.ds(q0, BQ)
        start = start_ref[:, at]
        low = first_block(firsts, q0)
        high = (qi + 1) * (BQ // BK)
        for p in range(pairs):
            q = qkv[0, at, p * PAIR : (p + 1) * PAIR] * jnp.asarray(0.125, BF16)
            qq[p, :BQ] = q * first
            qq[p, BQ:] = q * second
            acc[p] = jnp.zeros((PAIR, BQ), F32)

        def scores(kb, tops):
            inside = valid_keys(start, q0, kb)
            rows_at = pl.ds(pl.multiple_of(kb * BK, BK), BK)
            grown = []
            for p in range(pairs):
                s = dot_nt(qkv[1, rows_at, p * PAIR : (p + 1) * PAIR], qq[p])
                s = jnp.where(inside, s, NEG)
                sc[kb - low, p] = s
                grown.append(jnp.maximum(tops[p], jnp.max(s, axis=0, keepdims=True)))
            return tuple(grown)

        tops = lax.fori_loop(
            low, high, scores, tuple(jnp.full((1, 2 * BQ), NEG, F32) for _ in range(pairs))
        )

        def weigh(kb, sums):
            grown = []
            for p in range(pairs):
                raw = jnp.exp(sc[kb - low, p] - tops[p])
                grown.append(sums[p] + jnp.sum(raw, axis=0, keepdims=True))
                raw = raw.astype(BF16)
                acc[p] += dot(vm[kb, p], jnp.concatenate([raw[:, :BQ], raw[:, BQ:]], axis=0))
            return tuple(grown)

        sums = lax.fori_loop(
            low, high, weigh, tuple(jnp.zeros((1, 2 * BQ), F32) for _ in range(pairs))
        )
        for p in range(pairs):
            inv = 1.0 / sums[p]
            out = jnp.concatenate(
                [acc[p, :HEAD_DIM] * inv[:, :BQ], acc[p, HEAD_DIM:] * inv[:, BQ:]], axis=0
            )
            joined[at, p * PAIR : (p + 1) * PAIR] = out.T.astype(BF16)
            lse_out[qi, p] = tops[p] + jnp.log(sums[p])
        return 0

    lax.fori_loop(0, SEQ_LEN // BQ, one_block, 0)
    own_out[...] = joined[pl.ds(pl.multiple_of(core * rows, 128), rows), :]
    far_out[...] = joined[pl.ds(pl.multiple_of((1 - core) * rows, 128), rows), :]


def attend(pos, ties, seg, keep, recv):
    _, rows, half = keep.shape
    pairs = half // PAIR
    window = SEQ_LEN // BK

    def kernel(*refs):
        attend_kernel(*refs, ties=len(ties))

    return pl.pallas_call(
        kernel,
        grid_spec=pltpu.PrefetchScalarGridSpec(
            num_scalar_prefetch=1,
            grid=(1,),
            in_specs=[whole(seg.shape)] + [ANY] * (2 + len(ties)),
            out_specs=[
                whole((rows, half)),
                whole((rows, half)),
                whole((SEQ_LEN // BQ, pairs, 1, 2 * BQ)),
            ],
            scratch_shapes=[
                pltpu.VMEM((3, SEQ_LEN, half), BF16),
                pltpu.VMEM((pairs, 2 * BQ, PAIR), BF16),
                pltpu.VMEM((SEQ_LEN // BK, pairs, PAIR, 2 * BK), BF16),
                pltpu.VMEM((window, pairs, BK, 2 * BQ), F32),
                pltpu.VMEM((pairs, PAIR, BQ), F32),
                pltpu.VMEM((SEQ_LEN, half), BF16),
                pltpu.VMEM((1, SEQ_LEN), jnp.int32),
                pltpu.SemaphoreType.DMA((2,)),
            ],
        ),
        out_shape=[
            jax.ShapeDtypeStruct((rows, half), BF16),
            jax.ShapeDtypeStruct((rows, half), BF16),
            jax.ShapeDtypeStruct((SEQ_LEN // BQ, pairs, 1, 2 * BQ), F32),
        ],
        compiler_params=params(),
        cost_estimate=cost(),
        name="attend",
    )(pos, seg, keep, recv, *ties)


def attend_back_kernel(
    pos, seg, lse_ref, keep, recv, own, far, grad_own, grad_far, *rest, ties
):
    keep_out, send_out, qkv, att, dout, qq, dd, km, delta, dq_t, dq, dk, dv, start_ref, sems = rest[ties:]
    core = pos[0]
    rows, half = own.shape
    pairs = half // PAIR
    copies = (
        gather_rows(keep, recv, qkv, sems.at[0], core, rows)
        + gather_rows(own, far, att, sems.at[1], core, rows)
        + gather_rows(grad_own, grad_far, dout, sems.at[2], core, rows)
    )
    for item in copies:
        item.start()
    firsts = segment_firsts(seg, pos[4])
    fill_starts(firsts, start_ref)
    dk[...] = jnp.zeros_like(dk)
    dv[...] = jnp.zeros_like(dv)
    for item in copies:
        item.wait()
    first, second = lane_masks()

    def prepare(kb, _):
        at = pl.ds(pl.multiple_of(kb * BK, BK), BK)
        for p in range(pairs):
            km[kb, p] = row_split(qkv[1, at, p * PAIR : (p + 1) * PAIR].T)
        return 0

    lax.fori_loop(0, SEQ_LEN // BK, prepare, 0)

    def one_block(qi, _):
        q0 = pl.multiple_of(qi * BQ, BQ)
        at = pl.ds(q0, BQ)
        start = start_ref[:, at]
        low = first_block(firsts, q0)
        high = (qi + 1) * (BQ // BK)
        for p in range(pairs):
            lanes = slice(p * PAIR, (p + 1) * PAIR)
            q = qkv[0, at, lanes] * jnp.asarray(0.125, BF16)
            qq[p, :BQ] = q * first
            qq[p, BQ:] = q * second
            g = dout[at, lanes]
            dd[p, :BQ] = g * first
            dd[p, BQ:] = g * second
            both = (g.astype(F32) * att[at, lanes].astype(F32)).T
            delta[p] = jnp.concatenate(
                [
                    jnp.sum(both[:HEAD_DIM], axis=0, keepdims=True),
                    jnp.sum(both[HEAD_DIM:], axis=0, keepdims=True),
                ],
                axis=1,
            )
            dq_t[p] = jnp.zeros((PAIR, BQ), F32)

        def step(kb, _):
            inside = valid_keys(start, q0, kb)
            rows_at = pl.ds(pl.multiple_of(kb * BK, BK), BK)
            for p in range(pairs):
                lanes = slice(p * PAIR, (p + 1) * PAIR)
                s = dot_nt(qkv[1, rows_at, lanes], qq[p])
                prob = jnp.where(inside, jnp.exp(s - lse_ref[qi, p]), 0.0)
                grad_prob = dot_nt(qkv[2, rows_at, lanes], dd[p])
                grad_s = (prob * (grad_prob - delta[p])).astype(BF16)
                dv[rows_at, lanes] += dot(prob.astype(BF16), dd[p])
                dk[rows_at, lanes] += dot(grad_s, qq[p])
                dq_t[p] += dot(km[kb, p], jnp.concatenate([grad_s[:, :BQ], grad_s[:, BQ:]], axis=0))
            return 0

        lax.fori_loop(low, high, step, 0)
        for p in range(pairs):
            dq[p * PAIR : (p + 1) * PAIR, at] = (dq_t[p] * 0.125).astype(BF16)
        return 0

    lax.fori_loop(0, SEQ_LEN // BQ, one_block, 0)
    for target, at in ((keep_out, core), (send_out, 1 - core)):
        tokens = pl.ds(pl.multiple_of(at * rows, 128), rows)
        target[0] = dq[:, tokens]
        target[1] = dk[tokens, :].astype(BF16).T
        target[2] = dv[tokens, :].astype(BF16).T


def attend_back(ties, pos, seg, lse, keep, recv, own, far, grad_own, grad_far):
    _, rows, half = keep.shape
    pairs = half // PAIR
    out = (3, half, rows)

    def kernel(*refs):
        attend_back_kernel(*refs, ties=len(ties))

    return pl.pallas_call(
        kernel,
        grid_spec=pltpu.PrefetchScalarGridSpec(
            num_scalar_prefetch=1,
            grid=(1,),
            in_specs=[whole(seg.shape), whole(lse.shape)] + [ANY] * (6 + len(ties)),
            out_specs=[whole(out), whole(out)],
            scratch_shapes=[
                pltpu.VMEM((3, SEQ_LEN, half), BF16),
                pltpu.VMEM((SEQ_LEN, half), BF16),
                pltpu.VMEM((SEQ_LEN, half), BF16),
                pltpu.VMEM((pairs, 2 * BQ, PAIR), BF16),
                pltpu.VMEM((pairs, 2 * BQ, PAIR), BF16),
                pltpu.VMEM((SEQ_LEN // BK, pairs, PAIR, 2 * BK), BF16),
                pltpu.VMEM((pairs, 1, 2 * BQ), F32),
                pltpu.VMEM((pairs, PAIR, BQ), F32),
                pltpu.VMEM((half, SEQ_LEN), BF16),
                pltpu.VMEM((SEQ_LEN, half), F32),
                pltpu.VMEM((SEQ_LEN, half), F32),
                pltpu.VMEM((1, SEQ_LEN), jnp.int32),
                pltpu.SemaphoreType.DMA((3, 2)),
            ],
        ),
        out_shape=[jax.ShapeDtypeStruct(out, BF16)] * 2,
        compiler_params=params(),
        cost_estimate=cost(),
        name="attend_back",
    )(pos, seg, lse, keep, recv, own, far, grad_own, grad_far, *ties)


def gather_lanes(core, own, far, target):
    half = own.shape[1]
    target[:, half_lanes(core, half)] = own[...]
    target[:, half_lanes(1 - core, half)] = far[...]


def hidden_block(i, core):
    late = i >> 1
    return 2 * (late * core + (1 - late) * (1 - core)) + (i & 1)


def early(i):
    return jnp.minimum(i, 1)


def late(i):
    return jnp.maximum(i - 2, 0)


def ff_first_kernel(
    pos, tok, ids, emb, own, far, weight, bias, gain, shift, cot, up, up_bias, down,
    after_out, normed_out, act_own, act_send, grad_out, bias_grad, attended, act,
):
    step = pl.program_id(0)

    @pl.when(step == 0)
    def _():
        gather_lanes(pos[0], own, far, attended)
        after = embed_tokens(tok, ids, emb) + dot(attended[...], weight[...]) + wide(bias)
        after_out[...] = after
        scaled, _ = center_and_scale(after)
        normed_out[...] = (scaled * wide(gain) + wide(shift)).astype(BF16)

    for part in range(up.shape[1] // SUB):
        cols = slice(part * SUB, (part + 1) * SUB)
        u = dot(normed_out[...], up[:, cols]) + up_bias[:, cols].astype(F32)
        grad_act = dot_nt(cot[...], down[cols, :])
        square = u * u
        t = jnp.tanh(0.7978845608028654 * u * (1.0 + 0.044715 * square))
        half = 0.5 * (1.0 + t)
        act[:, cols] = (u * half).astype(BF16)
        slope = half + 0.5 * u * (1.0 - t * t) * (0.7978845608028654 * (1.0 + 0.134145 * square))
        grad = (grad_act * slope).astype(BF16)
        grad_out[:, cols] = grad
        bias_grad[:, cols] = jnp.sum(grad.astype(F32), axis=0, keepdims=True)

    @pl.when(step < 2)
    def _():
        act_send[...] = act[...]

    @pl.when(step >= 2)
    def _():
        act_own[...] = act[...]


def ff_first(pos, tok, ids, emb, own, far, weight, bias, gain, shift, cot, up, up_bias, down):
    rows, width = tok.shape
    hidden = up.shape[1]
    first = (tok, ids, emb, own, far, weight, bias, gain, shift, cot)
    shape = jax.ShapeDtypeStruct
    return pl.pallas_call(
        ff_first_kernel,
        grid_spec=pltpu.PrefetchScalarGridSpec(
            num_scalar_prefetch=1,
            grid=(4,),
            in_specs=[whole(item.shape) for item in first]
            + [
                pl.BlockSpec((width, width), lambda i, s: (0, hidden_block(i, s[0]))),
                pl.BlockSpec((1, width), lambda i, s: (0, hidden_block(i, s[0]))),
                pl.BlockSpec((width, width), lambda i, s: (hidden_block(i, s[0]), 0)),
            ],
            out_specs=[
                whole((rows, width)),
                whole((rows, width)),
                pl.BlockSpec((rows, width), lambda i, s: (0, late(i))),
                pl.BlockSpec((rows, width), lambda i, s: (0, early(i))),
                pl.BlockSpec((rows, width), lambda i, s: (0, hidden_block(i, s[0]))),
                pl.BlockSpec((1, width), lambda i, s: (0, hidden_block(i, s[0]))),
            ],
            scratch_shapes=[pltpu.VMEM((rows, width), BF16), pltpu.VMEM((rows, width), BF16)],
        ),
        out_shape=[
            shape((rows, width), F32),
            shape((rows, width), BF16),
            shape((rows, hidden // 2), BF16),
            shape((rows, hidden // 2), BF16),
            shape((rows, hidden), BF16),
            shape((1, hidden), F32),
        ],
        compiler_params=params(),
        cost_estimate=cost(),
        name="ff_first",
    )(pos, *first, up, up_bias, down)


def ff_back_kernel(
    pos, grad_pre, up, after, cot, gain, weight,
    grad_after, branch_out, own_out, far_out, sums, total,
):
    step = pl.program_id(0)
    part = dot_nt(grad_pre[...], up[...])

    @pl.when(step == 0)
    def _():
        total[...] = part

    @pl.when(step > 0)
    def _():
        total[...] += part

    @pl.when(step == pl.num_programs(0) - 1)
    def _():
        core = pos[0]
        half = own_out.shape[1]
        scaled, scale = center_and_scale(after[...])
        grad = total[...]
        inner = grad * wide(gain)
        shift = jnp.mean(inner, -1, keepdims=True)
        slope = jnp.mean(inner * scaled, -1, keepdims=True)
        cot_f32 = wide(cot)
        result = cot_f32 + scale * (inner - shift - scaled * slope)
        grad_after[...] = result
        branch_out[...] = result.astype(BF16)
        branch = branch_out[...]
        for target, at in ((far_out, 1 - core), (own_out, core)):
            rows = pl.ds(pl.multiple_of(at * half, 128), half)
            target[...] = dot_nt(branch, weight[rows, :]).astype(BF16)
        sums[0:1] = jnp.sum(grad * scaled, axis=0, keepdims=True)
        sums[1:2] = jnp.sum(grad, axis=0, keepdims=True)
        sums[2:3] = jnp.sum(branch.astype(F32), axis=0, keepdims=True)
        sums[3:4] = jnp.sum(cot_f32, axis=0, keepdims=True)


def ff_back(pos, grad_pre, up, after, cot, gain, weight):
    rows, width = after.shape
    half = width // 2
    last = (after, cot, gain, weight)
    outs = [
        jax.ShapeDtypeStruct((rows, width), F32),
        jax.ShapeDtypeStruct((rows, width), BF16),
        jax.ShapeDtypeStruct((rows, half), BF16),
        jax.ShapeDtypeStruct((rows, half), BF16),
        jax.ShapeDtypeStruct((4, width), F32),
    ]
    return pl.pallas_call(
        ff_back_kernel,
        grid_spec=pltpu.PrefetchScalarGridSpec(
            num_scalar_prefetch=1,
            grid=(grad_pre.shape[1] // width,),
            in_specs=[
                pl.BlockSpec((rows, width), lambda i, s: (0, i)),
                pl.BlockSpec((width, width), lambda i, s: (0, i)),
            ]
            + [whole(item.shape) for item in last],
            out_specs=[whole(item.shape) for item in outs],
            scratch_shapes=[pltpu.VMEM((rows, width), F32)],
        ),
        out_shape=outs,
        compiler_params=params(),
        cost_estimate=cost(),
        name="ff_back",
    )(pos, grad_pre, up, *last)


def z_place(z):
    return (z & 1) * 2 + (z >> 1)


def chips():
    return [(x, y, z) for x in range(2) for y in range(2) for z in range(4)]


def chip_row(pos, x, y, z):
    return ((2 * z_place(z) + y) ^ pos[3]) * 2 + (x ^ pos[2])


def rows_of(values, chip, per, at=0, count=None):
    count = per if count is None else count
    return values[pl.ds(pl.multiple_of(chip * per + at, 8), count), :].astype(BF16)


def down_weight_kernel(pos, act, act_far, cot, cot_far, *rest, ties):
    keep, send, rows_f32 = rest[ties:]
    per = rows_f32.shape[0] // 16
    half = rows_f32.shape[1] // 2
    rows_f32[...] = dot_tn(cot[...], act[...]) + dot_tn(cot_far[...], act_far[...])
    for x, y, z in chips():
        rows = rows_of(rows_f32, chip_row(pos, x, y, z), per)
        (keep, send)[x][y, z, :per, :] = rows[:, :half]
        (keep, send)[x][y, z, per:, :] = rows[:, half:]


def down_weight_call(pos, ties, act, act_far, cot, cot_far):
    rows, width = cot.shape
    half = width // 2
    per = width // 16
    out = jax.ShapeDtypeStruct((2, 4, 4 * per, half), BF16)

    def kernel(*refs):
        down_weight_kernel(*refs, ties=len(ties))

    return pl.pallas_call(
        kernel,
        grid_spec=pltpu.PrefetchScalarGridSpec(
            num_scalar_prefetch=1,
            grid=(2,),
            in_specs=[pl.BlockSpec((rows, width), lambda i, s: (0, i))] * 2
            + [whole(cot.shape)] * 2
            + [ANY] * len(ties),
            out_specs=[pl.BlockSpec((2, 4, 2 * per, half), lambda i, s: (0, 0, i, 0))] * 2,
            scratch_shapes=[pltpu.VMEM((width, width), F32)],
        ),
        out_shape=[out, out],
        compiler_params=params(),
        cost_estimate=cost(),
        name="down_weight",
    )(pos, act, act_far, cot, cot_far, *ties)


def up_weight_kernel(pos, grad, grad_far, normed, normed_far, keep, send, rows_f32):
    per = rows_f32.shape[0] // 4
    own = normed[:, half_lanes(pos[0], rows_f32.shape[1])]
    far = normed_far[:, half_lanes(pos[0], rows_f32.shape[1])]
    rows_f32[...] = dot_tn(grad[...], own) + dot_tn(grad_far[...], far)
    for x in range(2):
        for y in range(2):
            chip = (y ^ (pos[3] & 1)) * 2 + (x ^ pos[2])
            (keep, send)[y][x, 0, :per, :] = rows_of(rows_f32, chip, per)


def up_weight_call(pos, grad, grad_far, normed, normed_far):
    rows, width = normed.shape
    half = width // 2
    per = width // 16
    out = jax.ShapeDtypeStruct((2, 4, 5 * per, half), BF16)

    def at(i, s):
        return 0, z_place(i ^ (s[3] >> 1)), 0, 0

    return pl.pallas_call(
        up_weight_kernel,
        grid_spec=pltpu.PrefetchScalarGridSpec(
            num_scalar_prefetch=1,
            grid=(4,),
            in_specs=[pl.BlockSpec((rows, width), lambda i, s: (0, i))] * 2
            + [whole(normed.shape), whole(normed_far.shape)],
            out_specs=[pl.BlockSpec((2, 1, 4 * per, half), at)] * 2,
            scratch_shapes=[pltpu.VMEM((width, half), F32)],
        ),
        out_shape=[out, out],
        compiler_params=params(),
        cost_estimate=cost(),
        name="up_weight",
    )(pos, grad, grad_far, normed, normed_far)


def out_weight_kernel(pos, branch, branch_far, own, far, keep_in, send_in, tie, keep_out, send_out, rows_f32):
    per = rows_f32.shape[0] // 16
    rows_f32[...] = dot_tn(branch[...], own[...]) + dot_tn(branch_far[...], far[...])
    for x, y, z in chips():
        (keep_out, send_out)[y][x, z] = rows_of(rows_f32, chip_row(pos, x, y, z), per)


def out_weight_call(pos, tie, branch, branch_far, own, far, keep, send):
    rows, width = branch.shape
    half = width // 2
    block = pl.BlockSpec((2, 4, width // 16, half), lambda i, s: (0, 0, 4, 0))
    return pl.pallas_call(
        out_weight_kernel,
        grid_spec=pltpu.PrefetchScalarGridSpec(
            num_scalar_prefetch=1,
            grid=(1,),
            in_specs=[whole(branch.shape)] * 2 + [whole(own.shape)] * 2 + [ANY] * 3,
            out_specs=[block, block],
            scratch_shapes=[pltpu.VMEM((width, half), F32)],
        ),
        out_shape=[jax.ShapeDtypeStruct(keep.shape, BF16)] * 2,
        input_output_aliases={5: 0, 6: 1},
        compiler_params=params(),
        cost_estimate=cost(),
        name="out_weight",
    )(pos, branch, branch_far, own, far, keep, send, tie)


def pack_sums(tables, long, packed):
    count, _, share = packed.shape
    for device in range(count):
        low = 0
        for table in tables:
            rows = table.shape[0]
            packed[device, low : low + rows, :] = table[:, device * share : (device + 1) * share]
            low += rows
        for part in range(4):
            at = (4 * device + part) * share
            packed[device, low + part : low + part + 1, :] = long[:, at : at + share]


def mixed_kernel(pos, act_send, act_own, down, after, bias, one, two, three, four, *rest, ties, carried):
    out, packed = rest[ties + carried : ties + carried + 2]
    total = rest[-1]
    step = pl.program_id(0)

    @pl.when(step == 0)
    def _():
        total[...] = after[...] + wide(bias)

    @pl.when(step < 2)
    def _():
        total[...] += dot(act_send[...], down[...])

    @pl.when(step >= 2)
    def _():
        total[...] += dot(act_own[...], down[...])

    @pl.when(step == pl.num_programs(0) - 1)
    def _():
        out[...] = total[...].astype(BF16)
        pack_sums((one, two, three), four, packed)


def mixed_call(pos, ties, carried, act_send, act_own, down, after, bias, *sums):
    rows, width = after.shape
    devices = lax.axis_size("batch") * lax.axis_size("head")
    packed = (devices, sum(item.shape[0] for item in sums[:3]) + 4, width // devices)

    def kernel(*refs):
        mixed_kernel(*refs, ties=len(ties), carried=len(carried))

    return pl.pallas_call(
        kernel,
        grid_spec=pltpu.PrefetchScalarGridSpec(
            num_scalar_prefetch=1,
            grid=(4,),
            in_specs=[
                pl.BlockSpec((rows, width), lambda i, s: (0, early(i))),
                pl.BlockSpec((rows, width), lambda i, s: (0, late(i))),
                pl.BlockSpec((width, width), lambda i, s: (hidden_block(i, s[0]), 0)),
                whole(after.shape),
                whole(bias.shape),
            ]
            + [whole(item.shape) for item in sums]
            + [ANY] * (len(ties) + len(carried)),
            out_specs=[whole((rows, width)), whole(packed)] + [ANY] * len(carried),
            scratch_shapes=[pltpu.VMEM((rows, width), F32)],
        ),
        out_shape=[jax.ShapeDtypeStruct((rows, width), BF16), jax.ShapeDtypeStruct(packed, F32)]
        + shapes(carried),
        input_output_aliases=carry(5 + len(sums) + len(ties), 2, carried),
        compiler_params=params(),
        cost_estimate=cost(),
        name="mixed",
    )(pos, act_send, act_own, down, after, bias, *sums, *ties, *carried)


def qkv_weight_kernel(
    pos, mine, mine_far, other, other_far, normed, normed_far, *rest, ties
):
    left_keep, left_send, right_keep, right_send, sums, rows_f32 = rest[ties:]
    core = pos[0]
    half = normed_far.shape[1]
    third = pl.program_id(0)
    own = normed[:, half_lanes(core, half)]
    ones = jnp.ones((8, own.shape[0]), BF16)

    @pl.when(third == 0)
    def _():
        sums[...] = jnp.zeros_like(sums)

    for near, far, at in ((mine, mine_far, core), (other, other_far, 1 - core)):
        rows = pl.ds(pl.multiple_of((2 * third + at) * half, 128), half)
        rows_f32[rows, :] = dot(near[0], own) + dot(far[0], normed_far[...])
    row = (dot_nt(ones, mine[0]) + dot_nt(ones, mine_far[0]))[:1]
    lanes = half_lanes(core, half)
    for t in range(3):
        sums[t : t + 1, lanes] += jnp.where(third == t, row, 0.0)

    @pl.when(third == pl.num_programs(0) - 1)
    def _():
        per = rows_f32.shape[0] // 32
        for x, y, z in chips():
            chip = chip_row(pos, x, y, z)
            (left_keep, left_send)[x][y, z] = rows_of(rows_f32, chip, 2 * per, 0, per)
            (right_keep, right_send)[y][x, z] = rows_of(rows_f32, chip, 2 * per, per, per)


def qkv_weight_call(pos, ties, mine, mine_far, other, other_far, normed, normed_far):
    rows, width = normed.shape
    half = width // 2
    third = pl.BlockSpec((1, half, rows), lambda t, s: (t, 0, 0))
    out = jax.ShapeDtypeStruct((2, 4, 3 * width // 32, half), BF16)

    def kernel(*refs):
        qkv_weight_kernel(*refs, ties=len(ties))

    return pl.pallas_call(
        kernel,
        grid_spec=pltpu.PrefetchScalarGridSpec(
            num_scalar_prefetch=1,
            grid=(3,),
            in_specs=[third] * 4 + [whole(normed.shape), whole(normed_far.shape)] + [ANY] * len(ties),
            out_specs=[whole(out.shape)] * 4 + [whole((3, width))],
            scratch_shapes=[pltpu.VMEM((3 * width, half), F32)],
        ),
        out_shape=[out] * 4 + [jax.ShapeDtypeStruct((3, width), F32)],
        compiler_params=params(),
        cost_estimate=cost(),
        name="qkv_weight",
    )(pos, mine, mine_far, other, other_far, normed, normed_far, *ties)


def input_back_kernel(pos, mine, other, weight, tok, ids, emb, gain, grad_after, *rest, ties, carried):
    out, sums = rest[ties + carried : ties + carried + 2]
    joined, total = rest[-2:]
    core = pos[0]
    step = pl.program_id(0)
    half = mine.shape[1]
    joined[half_lanes(core, half), :] = mine[0]
    joined[half_lanes(1 - core, half), :] = other[0]
    part = lax.dot_general(
        joined[...], weight[...], (((0,), (1,)), ((), ())), preferred_element_type=F32
    )

    @pl.when(step == 0)
    def _():
        total[...] = part

    @pl.when(step > 0)
    def _():
        total[...] += part

    @pl.when(step == pl.num_programs(0) - 1)
    def _():
        grad = total[...]
        scaled, scale = center_and_scale(embed_tokens(tok, ids, emb))
        inner = grad * wide(gain)
        shift = jnp.mean(inner, -1, keepdims=True)
        slope = jnp.mean(inner * scaled, -1, keepdims=True)
        result = grad_after[...] + scale * (inner - shift - scaled * slope)
        out[...] = result
        passes = emb.shape[0]
        chosen = pass_rows(ids, passes)
        high = result.astype(BF16)
        less = result - high.astype(F32)
        middle = less.astype(BF16)
        least = (less - middle.astype(F32)).astype(BF16)
        sums[0:passes] = dot(chosen, high) + (dot(chosen, middle) + dot(chosen, least))
        sums[passes : passes + 1] = jnp.sum(grad * scaled, axis=0, keepdims=True)
        sums[passes + 1 : passes + 2] = jnp.sum(grad, axis=0, keepdims=True)


def input_back(pos, ties, carried, mine, other, weight, tok, ids, emb, gain, grad_after):
    rows, width = tok.shape
    third = pl.BlockSpec((1, width // 2, rows), lambda t, s: (t, 0, 0))
    fixed = (tok, ids, emb, gain, grad_after)
    outs = [
        jax.ShapeDtypeStruct((rows, width), F32),
        jax.ShapeDtypeStruct((emb.shape[0] + 2, width), F32),
    ]

    def kernel(*refs):
        input_back_kernel(*refs, ties=len(ties), carried=len(carried))

    return pl.pallas_call(
        kernel,
        grid_spec=pltpu.PrefetchScalarGridSpec(
            num_scalar_prefetch=1,
            grid=(3,),
            in_specs=[third, third, pl.BlockSpec((width, width), lambda t, s: (0, t))]
            + [whole(item.shape) for item in fixed]
            + [ANY] * (len(ties) + len(carried)),
            out_specs=[whole(item.shape) for item in outs] + [ANY] * len(carried),
            scratch_shapes=[pltpu.VMEM((width, rows), BF16), pltpu.VMEM((rows, width), F32)],
        ),
        out_shape=outs + shapes(carried),
        input_output_aliases=carry(3 + len(fixed) + len(ties), len(outs), carried),
        compiler_params=params(),
        cost_estimate=cost(),
        name="input_back",
    )(pos, mine, other, weight, *fixed, *ties, *carried)


def swap_head(values, bit):
    size = lax.axis_size("head")
    return lax.ppermute(values, "head", [(i, i ^ bit) for i in range(size)])


def swap_batch(values, bit):
    size = lax.axis_size("batch")
    return lax.ppermute(values, "batch", [(i, i ^ bit) for i in range(size)])


class Sum:
    def __init__(self, *parts):
        self.parts = parts

    def __getitem__(self, index):
        return Sum(*[part[index] for part in self.parts])

    def wide(self):
        total = self.parts[0].astype(F32)
        for part in self.parts[1:]:
            total = total + part.astype(F32)
        return total

    def sent(self):
        return self.wide().astype(BF16)


def swap_x(values):
    return swap_head(values, 2)


def swap_y(values):
    return swap_batch(values, 1)


def z_step(left, right):
    cut = left.parts[0].shape[0] // 2
    split = left.parts[0].shape[1]
    sent = jnp.concatenate([left[cut:].sent(), right[cut:].sent()], 1)

    def finish():
        got = swap_batch(sent, 2 if cut == 2 else 4)
        return Sum(*left[:cut].parts, got[:, :split]), Sum(*right[:cut].parts, got[:, split:])

    return sent, finish


def chip_sums(core, *items):
    flat = [jnp.where(core == 0, item[..., 1, :, :], item[..., 0, :, :]) for item in items]
    width = flat[0].shape[-1]
    got = swap_head(jnp.concatenate([item.reshape(-1, width) for item in flat], 0), 1)
    out, at = [], 0
    for item, sent in zip(items, flat):
        count = sent.size // width
        far = got[at : at + count].reshape(sent.shape)
        near = jnp.where(core == 0, item[..., 0, :, :], item[..., 1, :, :])
        out.append((jnp.where(core == 0, near, far), jnp.where(core == 0, far, near)))
        at += count
    return out


def scatter_any(core, values):
    half = values.shape[-1]
    rows = values.reshape(-1, half).astype(F32)
    both = lax.dynamic_update_slice(jnp.zeros((rows.shape[0], 2 * half), F32), rows, (0, core * half))
    return lax.psum_scatter(both, ("batch", "head"), scatter_dimension=0, tiled=True)


def by_chip(values):
    rest = values.shape[3:]
    split = values.reshape((2, 2, 2, 2) + rest)
    order = (3, 2, 1, 0) + tuple(range(4, split.ndim))
    return split.transpose(order).reshape((16,) + rest)


def on_device(
    tokens,
    pass_ids,
    segment_ids,
    pass_embed,
    norm1_gain,
    norm1_shift,
    qkv_weight,
    qv_bias,
    out_weight,
    out_bias,
    norm2_gain,
    norm2_shift,
    up_weight,
    up_bias,
    down_weight,
    down_bias,
    cotangent,
):
    rows, width = tokens.shape
    hidden_units = up_weight.shape[1]
    passes = pass_embed.shape[0]
    pairs = width // 2 // PAIR
    assert 2 * rows == SEQ_LEN and lax.axis_size("head") == 4 and hidden_units == 4 * width
    direct = lax.axis_size("batch") == BLOCKS

    head = lax.axis_index("head").astype(jnp.int32)
    batch = lax.axis_index("batch").astype(jnp.int32)
    core, x_bit = head % 2, head // 2
    zero = jnp.zeros((), jnp.int32)
    place = [core, x_bit, batch] if direct else [zero, zero, zero]
    pos = jnp.stack([core] + place + [x_bit])

    row = lambda item: item
    ids = row(pass_ids)
    gain_one, gain_two = row(norm1_gain), row(norm2_gain)
    cot_far = swap_head(cotangent, 1)
    normed, normed_send, send = qkv_send(
        pos, tokens, ids, pass_embed, gain_one, row(norm1_shift), qkv_weight, qv_bias
    )
    recv = swap_head(send, 1)
    normed_far = swap_head(normed_send, 1)
    keep = qkv_keep(pos, normed, qkv_weight, qv_bias)
    own, far_send, lse = attend(pos, (cot_far, normed_far), segment_ids, keep, recv)
    far = swap_head(far_send, 1)
    after, normed_two, act_own, act_send, grad_pre, up_bias_grad = ff_first(
        pos, tokens, ids, pass_embed, own, far, out_weight, row(out_bias), gain_two, row(norm2_shift),
        cotangent, up_weight, up_bias.reshape(1, -1), down_weight,
    )
    act_far = swap_head(act_send, 1)
    grad_pre_far = swap_head(grad_pre, 1)
    normed_two_far = swap_head(normed_two, 1)
    grad_after, branch, grad_own, grad_send, sums_two = ff_back(
        pos, grad_pre, up_weight, after, cotangent, gain_two, out_weight
    )
    grad_far = swap_head(grad_send, 1)
    branch_far = swap_head(branch, 1)
    up_keep, up_send = up_weight_call(pos, grad_pre, grad_pre_far, normed_two, normed_two_far)
    up_keep, up_send = out_weight_call(pos, grad_far, branch, branch_far, own, far_send, up_keep, up_send)
    down_keep, down_send = down_weight_call(pos, (up_send,), act_own, act_far, cotangent, cot_far)
    if direct:
        left = Sum(down_keep, swap_x(down_send))
        right = Sum(up_keep, swap_y(up_send))
    mine, mine_send = attend_back(
        (down_send, up_send), pos, segment_ids, lse, keep, recv, own, far_send, grad_own, grad_far
    )
    other = swap_head(mine_send, 1)
    other_far = swap_head(mine, 1)
    ties, carried = (), ()
    if direct:
        left_sent, right_sent = left[1].sent(), right[1].sent()
        ties = (left_sent, right_sent)
    left_keep, left_send, right_keep, right_send, bias_sums = qkv_weight_call(
        pos, ties, mine, mine_send, other, other_far, normed, normed_far
    )
    if direct:
        one_got, two_got = swap_x(left_send), swap_y(right_send)
        left = Sum(*left[0].parts, swap_y(left_sent))
        right = Sum(*right[0].parts, swap_x(right_sent))
        mid_sent, mid_next = z_step(left, right)
        ties, carried = (mid_sent,), (left_keep, right_keep)
    input_grad, sums_one, *carried = input_back(
        pos, ties, carried, mine, other, qkv_weight, tokens, ids, pass_embed, gain_one, grad_after
    )
    if direct:
        one, two = Sum(carried[0], one_got), Sum(carried[1], two_got)
        one_sent, two_sent = one[1].sent(), two[1].sent()
        one_last, two_last = swap_y(one_sent), swap_x(two_sent)
        mid_sent, mid_next = z_step(*mid_next())
        qkv_sent, qkv_next = z_step(Sum(*one[0].parts, one_last), Sum(*two[0].parts, two_last))
        ties = (mid_sent, qkv_sent)
    result, packed, *carried = mixed_call(
        pos, ties, carried, act_send, act_own, down_weight, after, row(down_bias),
        sums_one, bias_sums, sums_two, up_bias_grad,
    )

    per = width // 32
    if direct:
        one, two = qkv_next()
        one = Sum(carried[0][0][:2], *one.parts[1:])
        two = Sum(carried[1][0][:2], *two.parts[1:])
        _, qkv_next = z_step(one, two)
        left, right = [item.wide()[0] for item in mid_next()]
        cut = 8 * per
        down, up, out = chip_sums(
            core,
            left.reshape(4, 2, per, -1),
            right[:cut].reshape(2, 4 * per, -1),
            right[cut:].reshape(2, per, -1),
        )
        (qkv,) = chip_sums(core, jnp.stack([item.wide()[0] for item in qkv_next()]))
        down_grad = jnp.concatenate(down, 0).transpose(0, 2, 1).reshape(hidden_units, -1)
        up_grad, out_grad, qkv_grad = [jnp.concatenate(item, -1) for item in (up, out, qkv)]
    else:
        down = by_chip(jnp.stack([down_keep, down_send])).reshape(16, 4, 2 * per, -1)
        down = down.transpose(0, 2, 1, 3).reshape(16, 2 * per, -1)
        up = by_chip(jnp.stack([up_keep, up_send], 1))
        left = by_chip(jnp.stack([left_keep, left_send]))
        right = by_chip(jnp.stack([right_keep, right_send], 1))
        cut = 8 * per
        down_grad = scatter_any(core, down).T
        up_grad = scatter_any(core, up[:, :cut])
        out_grad = scatter_any(core, up[:, cut:])
        qkv_grad = scatter_any(core, jnp.concatenate([left, right], 1))
    got = lax.all_to_all(packed, ("batch", "head"), split_axis=0, concat_axis=0, tiled=True)
    small = jnp.sum(got, 0)
    bias_at, two_at, up_at = passes + 2, passes + 5, passes + 9
    return (
        result,
        input_grad,
        small[:passes],
        small[passes],
        small[passes + 1],
        qkv_grad.T,
        jnp.stack([small[bias_at], small[bias_at + 2]]),
        out_grad.T,
        small[two_at + 2],
        small[two_at],
        small[two_at + 1],
        up_grad.T,
        small[up_at:].reshape(-1),
        down_grad,
        small[two_at + 3],
    )


def solution(mesh):
    both = ("batch", "head")
    copied = P()
    in_specs = (P(both, None), P(both), P("batch", None)) + (copied,) * 13 + (P(both, None),)
    out_specs = (
        P(both, None),
        P(both, None),
        P(None, both),
        P(both),
        P(both),
        P(None, both),
        P(None, both),
        P(None, both),
        P(both),
        P(both),
        P(both),
        P(None, both),
        P(both),
        P(None, both),
        P(both),
    )
    return jax.shard_map(
        on_device, mesh=mesh, in_specs=in_specs, out_specs=out_specs, check_vma=False
    )
```
